256 devices in a mesh: ctx: 8 (over y, z_lo), exp: 16 (over z_hi, x), rep: 2 (over core).
Axes of the slice: x: 4, y: 4, z: 8 (z_hi: 4, z_lo: 2; z = z_hi * 2 + z_lo), core: 2. Of those that a mesh axis runs over, the one named last changes fastest.
Arguments:
- hidden_in: bfloat16 [8192, 4096], P(('rep', 'ctx', 'exp')), parts along dimension 0, may hold values from -6 to 6
- queries: bfloat16 [8192, 8192], P(('rep', 'ctx'), 'exp'), parts along dimension 0, may hold values from -64 to 64
- keys: bfloat16 [8192, 512], P(('rep', 'ctx')), parts along dimension 0, may hold values from -8 to 8
- values: bfloat16 [8192, 512], P(('rep', 'ctx')), parts along dimension 0, may hold values from -6 to 6
- out_proj: bfloat16 [8192, 4096], P('exp'), may hold values from -0.0625 to 0.0625
- norm_gain: float32 [4096], replicated, may hold values from 0.1 to 1.9
- expert_ids: int32 [8192, 8], P(('rep', 'ctx', 'exp')), parts along dimension 0, may hold values from 0 to 127, all different within a row; in each aligned block of 32 rows (0 to 31, 32 to 63, ...) at most 2 rows name the same one
- gate_fixed: int32 [8192, 8], P(('rep', 'ctx', 'exp')), parts along dimension 0, may hold values from 1 to 4096
- live_counts: int32 [256], P(('rep', 'ctx', 'exp')), parts along dimension 0, may hold values from 16 to 32, as said below
- gate_proj: bfloat16 [16, 4096, 1536], P('exp', None, 'ctx'), may hold values from -0.09375 to 0.09375
- up_proj: bfloat16 [16, 4096, 1536], P('exp', None, 'ctx'), may hold values from -0.09375 to 0.09375
- down_proj: bfloat16 [16, 1536, 4096], P('exp', 'ctx'), may hold values from -0.4375 to 0.4375
Outputs:
- mixed: bfloat16 [8192, 4096], P(('rep', 'ctx', 'exp')), parts along dimension 0
- expert_sum: bfloat16 [8192, 4096], P(('rep', 'ctx', 'exp')), parts along dimension 0
The draws below stay inside these ranges and needn't reach their ends.
There are 2 independent parts, one for each index of `rep`. The reference program is written for one: setup_inputs(seed, part) draws one part's arguments, and reference() takes and returns one part's arrays. A program takes and returns all parts, laid end to end along the dimension named above; an argument that names none is the same for every part. Nothing has to cross between parts.
Inputs may be any that keep to these rules, and one draw needn't show every extreme that they name: `expert_ids`: each row names 8 different experts; among the 32 rows of one device no expert is named by more than 2 rows. `live_counts`: some device has all of its rows live.
All inputs are finite; a program needn't handle non-finite values.
Results may differ from the reference program's by a relative error of at most 0.023.
Values may be sent and summed in bfloat16 or wider, within the bound.
No kernel may reach another device: no remote copies, remote signals or barrier semaphores. Data moves between devices by JAX's collectives and lax.ppermute only.
A program may use at most 64 MiB of HBM per device.

```python
import math
import jax
import jax.numpy as jnp
import numpy as np
from jax import lax

D = 4096
HEADS = 64
KV_HEADS = 4
HEAD_DIM = 128
FF = 1536
EXPERTS = 128
TOPK = 8
CAP = 2
PASS_EXPERTS = 16
GROUPS = 128
ROWS = 32
LENGTH = 4096
N_CTX = 8
N_EXP = 16


def attention_inputs(key):
    base = jax.random.fold_in(key, 7)
    first_key, second_key = jax.random.split(base, 2)
    keys_all = jnp.clip(jax.random.normal(first_key, (LENGTH, KV_HEADS, HEAD_DIM), jnp.float32), -6.0, 6.0)
    queries_all = jnp.clip(jax.random.normal(second_key, (LENGTH, HEADS, HEAD_DIM), jnp.float32), -6.0, 6.0)
    return (queries_all.reshape(LENGTH, HEADS * HEAD_DIM), keys_all.reshape(LENGTH, KV_HEADS * HEAD_DIM))


def draw_queries(key, part):
    return attention_inputs(key)[0].astype(jnp.bfloat16)


def draw_keys(key, part):
    return attention_inputs(key)[1].astype(jnp.bfloat16)


def draw_live_counts(key, part):
    counts = jax.random.randint(key, (GROUPS,), ROWS // 2, ROWS + 1, dtype=jnp.int32)
    forced = jax.random.randint(jax.random.fold_in(key, 3), (), 0, GROUPS, dtype=jnp.int32)
    return jnp.where(jnp.arange(GROUPS, dtype=jnp.int32) == forced, ROWS, counts).astype(jnp.int32)


def plant(array, own_key, least, top_value):
    spot = [jax.random.randint(jax.random.fold_in(own_key, axis), (), 0, length) for axis, length in enumerate(array.shape)]
    main_axis = array.shape.index(max(array.shape))
    neighbour = spot[:main_axis] + [(spot[main_axis] + 1) % array.shape[main_axis]] + spot[main_axis + 1:]
    return array.at[tuple(spot)].set(least).at[tuple(neighbour)].set(top_value)


def shard_levels(rng, dims, cuts, smallest, top_value):
    level = 1.0
    for dim, parts in cuts:
        draws = jax.random.uniform(jax.random.fold_in(jax.random.fold_in(rng, 6), dim), (parts,), jnp.float32, smallest / len(cuts), top_value / len(cuts))
        level = level * jnp.repeat(jnp.exp(draws), dims[dim] // parts).reshape((-1,) + (1,) * (len(dims) - 1 - dim))
    return level


def routed_block(own_key, own, number, rows, count, top, bound, slope):
    order = jax.random.permutation(own_key, count)
    heavy_load, usual = shares(count, rows * top, bound, slope, True), shares(count, rows * top, bound, slope, False)
    places = jnp.arange(count)

    def named(sizes, rotation):
        used = int((sizes > 0).sum())
        fixed = max(1, used // 4)
        moved = fixed + (places - fixed + rotation * (used - fixed)) % max(1, count - fixed)
        return jnp.zeros((count,), jnp.int32).at[order[jnp.where(places < fixed, places, moved)]].set(jnp.asarray(sizes, jnp.int32))

    sizes = jnp.where(number % 4 == 0, named(heavy_load, number // 4), named(usual, number - number // 4 - 1))
    mixed = jax.random.permutation(jax.random.fold_in(own, 3), count)
    source_of, sink = mixed[0:count // 2 * 2:2], mixed[1:count // 2 * 2:2]
    slack = jnp.minimum(sizes[source_of] - 1, bound - sizes[sink]) // 2
    slack = jnp.where((source_of == order[0]) | (sink == order[0]) | (sizes[sink] == 0), 0, jnp.maximum(slack, 0))
    moved = jax.random.randint(jax.random.fold_in(own, 4), (count // 2,), 0, 1 << 20) % (slack + 1)
    sizes = sizes.at[source_of].add(-moved).at[sink].add(moved)
    members = jnp.searchsorted(jnp.cumsum(sizes), jnp.arange(rows * top), side="right").astype(jnp.int32)
    listing = members.reshape(top, rows).T
    listing = listing[jax.random.permutation(jax.random.fold_in(own, 1), rows)]
    rotation = jax.random.randint(jax.random.fold_in(own, 2), (rows, 1), 0, top)
    return jnp.take_along_axis(listing, (jnp.arange(top)[None, :] + rotation) % top, axis=1)


def shares(number_of, total, limit, slope, full):
    portions = [(1 << 20) // math.isqrt(grade ** slope) + 1 for grade in range(1, number_of + 1)]
    largest = limit if full else min(limit, max(-(-total // number_of), total * portions[0] // sum(portions)))
    least = 1 if total - largest >= number_of - 1 else 0
    given, rest = [largest] + [least] * (number_of - 1), total - largest - least * (number_of - 1)
    while rest > 0:
        movable = [i for i in range(1, number_of) if given[i] < largest] or [i for i in range(1, number_of) if given[i] < limit]
        mass, budget = sum([portions[i] for i in movable]), rest
        for i in movable:
            addition = min(limit - given[i], max(1, budget * portions[i] // mass), rest)
            given[i] = given[i] + addition
            rest = rest - addition
    return np.array(given)


def normal_values(key, extent, deviation, bound, shards=(), kind=jnp.bfloat16):
    values = deviation * jax.random.normal(key, extent, jnp.float32)
    if shards:
        values = values * shard_levels(key, extent, shards, -0.22, 0.18)
    return jnp.clip(values, -bound, bound).astype(kind)


def setup_inputs(seed: int = 0, part: int = 0) -> dict:
    key_list = jax.random.split(jax.random.key(seed), 13)
    part_keys = jax.random.split(jax.random.fold_in(key_list[12], part), 13)
    hidden_in = normal_values(part_keys[0], (LENGTH, D), 1.0, 6.0, ((0, 128),))
    queries = draw_queries(jax.random.fold_in(jax.random.fold_in(key_list[12], part), 71), part)
    keys = draw_keys(jax.random.fold_in(jax.random.fold_in(key_list[12], part), 71), part)
    values = normal_values(part_keys[3], (LENGTH, KV_HEADS * HEAD_DIM), 1.0, 6.0, ((0, 8),))
    out_proj = normal_values(key_list[4], (HEADS * HEAD_DIM, D), (HEADS * HEAD_DIM) ** -0.5, 0.0625, ((0, 16),))
    norm_gain = jnp.clip(1.0 + 0.18 * jax.random.normal(key_list[5], (D,), jnp.float32), 0.1, 1.9)
    expert_ids_keys = jax.random.split(jax.random.fold_in(part_keys[6], 1), LENGTH // ROWS)
    expert_ids_turns = jax.random.permutation(jax.random.fold_in(part_keys[6], 3), LENGTH // ROWS)
    expert_ids = jax.vmap(lambda own, number: routed_block(jax.random.fold_in(part_keys[6], 2), own, number, ROWS, EXPERTS, TOPK, CAP, 2))(expert_ids_keys, expert_ids_turns).reshape((LENGTH, TOPK))
    gate_fixed = plant(jax.random.randint(part_keys[7], (LENGTH, TOPK), 1, 4097), jax.random.fold_in(part_keys[7], 1), 1, 4096).astype(jnp.int32)
    live_counts = draw_live_counts(jax.random.fold_in(jax.random.fold_in(key_list[12], part), 71), part)
    gate_proj = normal_values(key_list[9], (PASS_EXPERTS, D, FF), D ** -0.5, 0.09375, ((0, 16), (2, 8)))
    up_proj = normal_values(key_list[10], (PASS_EXPERTS, D, FF), D ** -0.5, 0.09375, ((0, 16), (2, 8)))
    down_proj = normal_values(key_list[11], (PASS_EXPERTS, FF, D), (FF // 8) ** -0.5, 0.4375, ((0, 16), (1, 8)))
    return {"hidden_in": hidden_in, "queries": queries, "keys": keys, "values": values, "out_proj": out_proj, "norm_gain": norm_gain, "expert_ids": expert_ids, "gate_fixed": gate_fixed, "live_counts": live_counts, "gate_proj": gate_proj, "up_proj": up_proj, "down_proj": down_proj}


def attend_head(head, queries3, keys3, values3, visible):
    group = HEADS // KV_HEADS
    query_rows = lax.dynamic_index_in_dim(queries3, head, 1, keepdims=False)
    key_rows = lax.dynamic_index_in_dim(keys3, head // group, 1, keepdims=False)
    value_rows = lax.dynamic_index_in_dim(values3, head // group, 1, keepdims=False)
    scores = jnp.dot(query_rows, key_rows.T, preferred_element_type=jnp.float32) * HEAD_DIM ** (-0.5)
    scores = jnp.where(visible, scores, -jnp.inf)
    largest = lax.optimization_barrier(jnp.max(scores, axis=1, keepdims=True))
    weights = jnp.where(visible, jnp.exp(scores - largest), 0.0)
    total = lax.optimization_barrier(jnp.sum(weights, axis=1, keepdims=True))
    summed = jnp.dot(weights.astype(jnp.bfloat16), value_rows, preferred_element_type=jnp.float32)
    return (summed / total).astype(jnp.bfloat16)

def run_expert(operands):
    rows, w_gate, w_up, w_down = operands
    width = FF // N_CTX
    total = jnp.zeros((rows.shape[0], D), jnp.float32)
    for slice_index in range(N_CTX):
        lower = slice_index * width
        gate_part = jnp.dot(rows, w_gate[:, lower:lower + width], preferred_element_type=jnp.float32)
        up_part = jnp.dot(rows, w_up[:, lower:lower + width], preferred_element_type=jnp.float32)
        hidden = (jax.nn.silu(gate_part) * up_part).astype(jnp.bfloat16)
        partial_value = jnp.dot(hidden, w_down[lower:lower + width, :], preferred_element_type=jnp.float32)
        rounded = lax.optimization_barrier(partial_value.astype(jnp.bfloat16))
        total = total + rounded.astype(jnp.float32)
    return total.astype(jnp.bfloat16)

def add_group(total, operands):
    columns, weight_rows = operands
    part = jnp.dot(columns, weight_rows, preferred_element_type=jnp.float32).astype(jnp.bfloat16)
    part = lax.optimization_barrier(part)
    return (total + part.astype(jnp.float32), None)

def reference(hidden_in, queries, keys, values, out_proj, norm_gain, expert_ids, gate_fixed, live_counts, gate_proj, up_proj, down_proj):
    queries3 = queries.reshape(LENGTH, HEADS, HEAD_DIM)
    keys3 = keys.reshape(LENGTH, KV_HEADS, HEAD_DIM)
    values3 = values.reshape(LENGTH, KV_HEADS, HEAD_DIM)
    positions = jnp.arange(LENGTH, dtype=jnp.int32)
    visible = positions[None, :] <= positions[:, None]
    heads_out = lax.map(lambda head: attend_head(head, queries3, keys3, values3, visible), jnp.arange(HEADS, dtype=jnp.int32))
    attended = heads_out.transpose(1, 0, 2).reshape(LENGTH, HEADS * HEAD_DIM)
    columns = HEADS * HEAD_DIM // N_EXP
    grouped = attended.reshape(LENGTH, N_EXP, columns).transpose(1, 0, 2)
    weight_groups = out_proj.reshape(N_EXP, columns, D)
    projected, _ = lax.scan(add_group, jnp.zeros((LENGTH, D), jnp.float32), (grouped, weight_groups))
    residual = hidden_in.astype(jnp.float32) + projected
    mixed = residual.astype(jnp.bfloat16)
    scale = lax.rsqrt(lax.optimization_barrier(jnp.mean(residual * residual, axis=1, keepdims=True)) + 1e-06)
    normed = (residual * scale * norm_gain).astype(jnp.bfloat16)
    slots = PASS_EXPERTS * CAP
    chosen = expert_ids.reshape(GROUPS, ROWS, TOPK)
    live = jnp.arange(ROWS, dtype=jnp.int32)[None, :] < live_counts[:, None]
    active = (chosen < PASS_EXPERTS) & live[:, :, None]
    onehot = ((chosen[..., None] == jnp.arange(PASS_EXPERTS, dtype=jnp.int32)) & active[..., None]).astype(jnp.int32)
    onehot = onehot.reshape(GROUPS, ROWS * TOPK, PASS_EXPERTS)
    earlier = jnp.cumsum(onehot, axis=1) - onehot
    rank = lax.optimization_barrier(jnp.sum(earlier * onehot, axis=2)).reshape(GROUPS, ROWS, TOPK)
    slot = jnp.where(active, chosen * CAP + rank, -1)
    pair_hit = slot[..., None] == jnp.arange(slots, dtype=jnp.int32)
    dispatch = jnp.any(pair_hit, axis=2).astype(jnp.float32)
    sent = jnp.einsum('brs,brd->bsd', dispatch, normed.reshape(GROUPS, ROWS, D).astype(jnp.float32)).astype(jnp.bfloat16)
    expert_in = sent.reshape(GROUPS, PASS_EXPERTS, CAP, D).transpose(1, 0, 2, 3).reshape(PASS_EXPERTS, GROUPS * CAP, D)
    expert_out = lax.map(run_expert, (expert_in, gate_proj, up_proj, down_proj))
    returned = expert_out.reshape(PASS_EXPERTS, GROUPS, CAP, D).transpose(1, 0, 2, 3).reshape(GROUPS, slots, D)
    weights = gate_fixed.reshape(GROUPS, ROWS, TOPK).astype(jnp.float32) / 4096.0
    combine = lax.optimization_barrier(jnp.sum(pair_hit.astype(jnp.float32) * weights[..., None], axis=2))
    expert_sum = jnp.einsum('brs,bsd->brd', combine, returned.astype(jnp.float32), precision=lax.Precision.HIGHEST)
    return (mixed, expert_sum.reshape(LENGTH, D).astype(jnp.bfloat16))
```

```python
import functools
import math

import jax
import jax.numpy as jnp
from jax import lax
from jax.experimental import pallas as pl
from jax.experimental.pallas import tpu as pltpu
from jax.sharding import PartitionSpec as P

D = 4096
HEADS = 64
KV_HEADS = 4
HEAD_DIM = 128
TOPK = 8
CAP = 2
N_X = 4
N_Z = 4
N_Y = 4
TOKENS = 32
BF16 = jnp.bfloat16
F32 = jnp.float32
LOWEST = -1e30
EXP2_SCALE = HEAD_DIM ** (-0.5) * math.log2(math.e)
VMEM = pltpu.VMEM
SMEM = pltpu.SMEM


def params(limit_mib=48):
    return pltpu.CompilerParams(vmem_limit_bytes=limit_mib << 20)


def whole():
    return pl.BlockSpec(memory_space=VMEM)


def shift_x(a, d):
    pairs = [(z * N_X + x, z * N_X + (x + d) % N_X) for z in range(N_Z) for x in range(N_X)]
    return lax.ppermute(a, "exp", pairs)


def shift_z(a, d):
    pairs = [(z * N_X + x, (z + d) % N_Z * N_X + x) for z in range(N_Z) for x in range(N_X)]
    return lax.ppermute(a, "exp", pairs)


def shift_y(a, d):
    pairs = [(y * 2 + k, (y + d) % N_Y * 2 + k) for y in range(N_Y) for k in range(2)]
    return lax.ppermute(a, "ctx", pairs)


def swap_l(a):
    return lax.ppermute(a, "ctx", [(i, i ^ 1) for i in range(2 * N_Y)])


def swap_core(a):
    return lax.ppermute(a, "rep", [(0, 1), (1, 0)])


def pick_head(where_am, keys, values):
    rows = keys.shape[0]

    def kernel(where_ref, key_ref, value_ref, out_ref):
        out_ref[0:rows, :] = key_ref[...]
        out_ref[rows:, :] = value_ref[...]

    column = pl.BlockSpec((rows, HEAD_DIM), lambda i, w: (0, w[0]))
    return pl.pallas_call(
        kernel,
        grid_spec=pltpu.PrefetchScalarGridSpec(
            num_scalar_prefetch=1,
            grid=(1,),
            in_specs=[column, column],
            out_specs=pl.BlockSpec((2 * rows, HEAD_DIM), lambda i, w: (0, 0)),
        ),
        out_shape=jax.ShapeDtypeStruct((2 * rows, HEAD_DIM), BF16),
        name="pick_head",
    )(where_am, keys, values)


def pick_weights(place, out_proj):
    rows, cols = out_proj.shape[0] // 2, out_proj.shape[1] // N_X

    def kernel(place_ref, *refs):
        for source, target in zip(refs[:4], refs[4:]):
            target[...] = source[...]

    def block(d):
        if d == 0:
            return pl.BlockSpec((2 * rows, cols), lambda i, w: (0, w[1]))
        return pl.BlockSpec((rows, cols), lambda i, w: (w[0], lax.rem(w[1] + d, N_X)))

    fixed = lambda i, w: (0, 0)
    return pl.pallas_call(
        kernel,
        grid_spec=pltpu.PrefetchScalarGridSpec(
            num_scalar_prefetch=1,
            grid=(1,),
            in_specs=[block(d) for d in range(4)],
            out_specs=[pl.BlockSpec((2 * rows, cols), fixed)] + [pl.BlockSpec((rows, cols), fixed)] * 3,
        ),
        out_shape=[jax.ShapeDtypeStruct((2 * rows, cols), BF16)]
        + [jax.ShapeDtypeStruct((rows, cols), BF16)] * 3,
        compiler_params=params(),
        name="pick_weights",
    )(place, out_proj, out_proj, out_proj, out_proj)


def attend(queries, blocks, flags, state, last):
    rows, heads = queries.shape[0], queries.shape[1] // HEAD_DIM
    tile = 256
    n = len(blocks)
    first = state is None

    def kernel(*refs):
        flag_ref, q_ref = refs[0], refs[1]
        kv_refs = refs[2 : 2 + n]
        rest = refs[2 + n :]
        if not first:
            acc_in, top_in = rest[0], rest[1]
            rest = rest[2:]
        if last:
            out_ref, acc_ref, top_ref = rest
        else:
            acc_ref, top_ref = rest
        acc_ref = acc_ref.at[0]
        top_ref = top_ref.at[0]

        def step(kv_ref, diagonal):
            key = kv_ref[0:rows, :]
            value = jnp.concatenate([kv_ref[rows:, :], jnp.ones((rows, HEAD_DIM), BF16)], axis=1)
            for part in range(rows // tile):
                at = pl.ds(part * tile, tile)
                scores = lax.dot_general(
                    q_ref[at, :], key, (((1,), (1,)), ((), ())), preferred_element_type=F32
                )
                if diagonal:
                    i = lax.broadcasted_iota(jnp.int32, (tile, rows), 0) + part * tile
                    j = lax.broadcasted_iota(jnp.int32, (tile, rows), 1)
                    scores = jnp.where(j <= i, scores, LOWEST)
                newest = jnp.max(scores, axis=1, keepdims=True)
                if not diagonal:
                    before = top_ref[at, :]
                    newest = jnp.maximum(before, newest)
                else:
                    newest = jnp.broadcast_to(newest, (tile, HEAD_DIM))
                weights = jnp.exp2(
                    (scores - jnp.concatenate([newest] * (rows // HEAD_DIM), axis=1)) * EXP2_SCALE
                ).astype(BF16)
                added = jnp.dot(weights, value, preferred_element_type=F32)
                if diagonal:
                    acc_ref[at, :] = added
                else:
                    factor = jnp.exp2((before - newest) * EXP2_SCALE)
                    acc_ref[at, :] = (
                        acc_ref[at, :] * jnp.concatenate([factor, factor], axis=1) + added
                    )
                top_ref[at, :] = newest

        if first:
            step(kv_refs[0], True)
        else:
            acc_ref[...] = acc_in[0]
            top_ref[...] = top_in[0]
            for b in range(n):
                pl.when(flag_ref[b] > 0)(functools.partial(step, kv_refs[b], False))
        if last:
            out_ref[...] = (acc_ref[:, 0:HEAD_DIM] / acc_ref[:, HEAD_DIM:]).astype(BF16)

    q_spec = pl.BlockSpec((rows, HEAD_DIM), lambda h, f: (0, h))
    kv_spec = pl.BlockSpec((2 * rows, HEAD_DIM), lambda h, f: (0, 0))
    acc_spec = pl.BlockSpec((1, rows, 2 * HEAD_DIM), lambda h, f: (h, 0, 0))
    top_spec = pl.BlockSpec((1, rows, HEAD_DIM), lambda h, f: (h, 0, 0))
    state_specs = [acc_spec, top_spec]
    state_shapes = [
        jax.ShapeDtypeStruct((heads, rows, 2 * HEAD_DIM), F32),
        jax.ShapeDtypeStruct((heads, rows, HEAD_DIM), F32),
    ]
    if last:
        out_specs = q_spec
        out_shape = jax.ShapeDtypeStruct(queries.shape, BF16)
        scratch = [VMEM((1, rows, 2 * HEAD_DIM), F32), VMEM((1, rows, HEAD_DIM), F32)]
    else:
        out_specs, out_shape, scratch = state_specs, state_shapes, []
    return pl.pallas_call(
        kernel,
        grid_spec=pltpu.PrefetchScalarGridSpec(
            num_scalar_prefetch=1,
            grid=(heads,),
            in_specs=[q_spec] + [kv_spec] * n + ([] if first else state_specs),
            out_specs=out_specs,
            scratch_shapes=scratch,
        ),
        out_shape=out_shape,
        compiler_params=params(),
        cost_estimate=pl.CostEstimate(
            flops=heads * n * rows * rows * HEAD_DIM * 4,
            transcendentals=heads * n * rows * rows,
            bytes_accessed=4 << 20,
        ),
        name="attend",
    )(flags, queries, *blocks, *(() if first else state))


def project(place, lefts, rights):
    cols = rights[0].shape[1]
    n = len(lefts)

    def kernel(place_ref, *refs):
        left_refs, right_refs, out_refs = refs[:n], refs[n : 2 * n], refs[2 * n :]
        z, x = place_ref[0], place_ref[1]
        for dz in range(N_Z):
            total = None
            for left_ref, right_ref in zip(left_refs, right_refs):
                pieces = []
                for dx in range(N_X):
                    row = lax.rem(z + dz, N_Z) * (N_X * TOKENS) + lax.rem(x + dx, N_X) * TOKENS
                    pieces.append(left_ref[pl.ds(pl.multiple_of(row, TOKENS), TOKENS), :])
                part = jnp.dot(
                    jnp.concatenate(pieces, axis=0), right_ref[...], preferred_element_type=F32
                )
                total = part if total is None else total + part
            out_refs[dz][...] = total.astype(BF16)

    return pl.pallas_call(
        kernel,
        in_specs=[pl.BlockSpec(memory_space=SMEM)] + [whole()] * (2 * n),
        out_specs=[whole()] * N_Z,
        out_shape=[jax.ShapeDtypeStruct((N_X * TOKENS, cols), BF16)] * N_Z,
        compiler_params=params(),
        name="project",
    )(place, *lefts, *rights)


def route(place, ids, gates, live):
    slots = N_X * N_Z * CAP

    def kernel(place_ref, live_ref, id_ref, gate_ref, pick_ref, weight_ref):
        z, x = place_ref[0], place_ref[1]
        s = lax.broadcasted_iota(jnp.int32, (slots, TOKENS), 0)
        t = lax.broadcasted_iota(jnp.int32, (slots, TOKENS), 1)
        dx, dz, cap = s // (N_Z * CAP), (s // CAP) % N_Z, s % CAP
        expert = ((z + dz) % N_Z) * N_X + (x + dx) % N_X
        present = jnp.zeros((slots, TOKENS), F32)
        weight = jnp.zeros((slots, TOKENS), F32)
        for k in range(TOPK):
            hit = ((id_ref[k : k + 1, :] == expert) & (t < live_ref[0])).astype(F32)
            present = present + hit
            weight = weight + hit * gate_ref[k : k + 1, :].astype(F32)
        earlier = (
            lax.broadcasted_iota(jnp.int32, (TOKENS, TOKENS), 0)
            < lax.broadcasted_iota(jnp.int32, (TOKENS, TOKENS), 1)
        ).astype(F32)
        rank = jnp.dot(present, earlier, preferred_element_type=F32)
        mine = jnp.abs(rank - cap.astype(F32)) < 0.5
        pick_ref[...] = jnp.where(mine, present, 0.0).astype(BF16)
        weight_ref[...] = jnp.where(mine, weight, 0.0) / 4096.0

    return pl.pallas_call(
        kernel,
        in_specs=[pl.BlockSpec(memory_space=SMEM), pl.BlockSpec(memory_space=SMEM), whole(), whole()],
        out_specs=[whole(), whole()],
        out_shape=[
            jax.ShapeDtypeStruct((slots, TOKENS), BF16),
            jax.ShapeDtypeStruct((slots, TOKENS), F32),
        ],
        name="route",
    )(place, live, ids, gates)


def normalise(place, hidden_in, own, pieces, gain, pick):
    cols = own.shape[1]

    def kernel(place_ref, hidden_ref, own_ref, p1, p2, p3, gain_ref, pick_ref, mixed_ref, *rest):
        send_refs, residual_ref = rest[:N_X], rest[N_X]
        x = place_ref[1]
        for d, piece in enumerate((own_ref, p1, p2, p3)):
            column = pl.ds(pl.multiple_of(lax.rem(x + N_X - d, N_X) * cols, cols), cols)
            residual_ref[:, column] = hidden_ref[:, column].astype(F32) + piece[...].astype(F32)
        residual = residual_ref[...]
        mixed_ref[...] = residual.astype(BF16)
        scale = lax.rsqrt(jnp.mean(residual * residual, axis=1, keepdims=True) + 1e-06)
        normed = (residual * scale * gain_ref[...]).astype(BF16)
        send = jnp.dot(pick_ref[...], normed, preferred_element_type=F32).astype(BF16)
        for dx in range(N_X):
            send_refs[dx][...] = send[dx * 8 : dx * 8 + 8, :]

    return pl.pallas_call(
        kernel,
        in_specs=[pl.BlockSpec(memory_space=SMEM)] + [whole()] * 7,
        out_specs=[whole()] * 5,
        out_shape=[jax.ShapeDtypeStruct((TOKENS, D), BF16)]
        + [jax.ShapeDtypeStruct((N_Z * CAP, D), BF16)] * N_X,
        scratch_shapes=[VMEM((TOKENS, D), F32)],
        compiler_params=params(),
        name="normalise",
    )(place, hidden_in, own, *pieces, gain, pick)


def regroup(groups):
    rows = 4 * 4 * CAP

    def kernel(*refs):
        held = jnp.concatenate([r[...] for r in refs[:4]], axis=0)
        to = lax.broadcasted_iota(jnp.int32, (rows, rows), 0)
        come = lax.broadcasted_iota(jnp.int32, (rows, rows), 1)
        b, a, cap = to // 8, (to // CAP) % 4, to % CAP
        order = (come == a * 8 + b * CAP + cap).astype(BF16)
        moved = jnp.dot(order, held, preferred_element_type=F32).astype(BF16)
        for i in range(4):
            refs[4 + i][...] = moved[i * 8 : i * 8 + 8, :]

    return pl.pallas_call(
        kernel,
        in_specs=[whole()] * 4,
        out_specs=[whole()] * 4,
        out_shape=[jax.ShapeDtypeStruct((8, D), BF16)] * 4,
        name="regroup",
    )(*groups)


def run_expert(blocks, gate, up, down):
    n = len(blocks)

    def kernel(*refs):
        in_refs, (gate_ref, up_ref, down_ref), out_refs = refs[:n], refs[n : n + 3], refs[n + 3 :]
        rows = jnp.concatenate([r[...] for r in in_refs], axis=0)
        gate_part = jnp.dot(rows, gate_ref[0], preferred_element_type=F32)
        up_part = jnp.dot(rows, up_ref[0], preferred_element_type=F32)
        hidden = (gate_part / (1.0 + jnp.exp(-gate_part)) * up_part).astype(BF16)
        result = jnp.dot(hidden, down_ref[0], preferred_element_type=F32).astype(BF16)
        at = 0
        for r in out_refs:
            r[...] = result[at : at + r.shape[0], :]
            at += r.shape[0]

    return pl.pallas_call(
        kernel,
        in_specs=[whole()] * (n + 3),
        out_specs=[whole()] * n,
        out_shape=[jax.ShapeDtypeStruct(b.shape, BF16) for b in blocks],
        compiler_params=params(56),
        name="run_expert",
    )(*blocks, gate, up, down)


def combine(weight, groups):
    def kernel(weight_ref, *refs):
        held = jnp.concatenate([r[...] for r in refs[:4]], axis=0).astype(F32)
        refs[4][...] = lax.dot_general(
            weight_ref[...],
            held,
            (((0,), (0,)), ((), ())),
            precision=lax.Precision.HIGHEST,
            preferred_element_type=F32,
        ).astype(BF16)

    return pl.pallas_call(
        kernel,
        in_specs=[whole()] * 5,
        out_specs=whole(),
        out_shape=jax.ShapeDtypeStruct((TOKENS, D), BF16),
        compiler_params=params(),
        name="combine",
    )(weight, *groups)


def gather_ctx(own, half):
    swapped = swap_l(own)
    below = shift_y(own, 1)
    above = shift_y(own, -1)
    below_swapped = swap_l(below)
    below_two = shift_y(below, 1)
    above_swapped = shift_y(swapped, -1)
    far_a = shift_y(below_swapped[:half], 1)
    far_b = shift_y(above_swapped[half:], -1)
    return own, swapped, below, above, below_swapped, below_two, above_swapped, far_a, far_b


def add(a, b):
    return (a.astype(F32) + b.astype(F32)).astype(BF16)


def scatter_ctx(parts, half):
    own, swapped, below, above, below_swapped, below_two, above_swapped, far_a, far_b = parts
    got_a = shift_y(far_a, -1)
    got_b = shift_y(far_b, 1)
    got_two = shift_y(below_two, -1)
    got_above = shift_y(above, 1)
    below_swapped = jnp.concatenate([add(below_swapped[:half], got_a), below_swapped[half:]], axis=0)
    above_swapped = jnp.concatenate([above_swapped[:half], add(above_swapped[half:], got_b)], axis=0)
    got_below_swapped = swap_l(below_swapped)
    got_above_swapped = shift_y(above_swapped, 1)
    below = (below.astype(F32) + got_two.astype(F32) + got_below_swapped.astype(F32)).astype(BF16)
    swapped = add(swapped, got_above_swapped)
    got_below = shift_y(below, -1)
    got_swapped = swap_l(swapped)
    return (
        own.astype(F32) + got_above.astype(F32) + got_below.astype(F32) + got_swapped.astype(F32)
    ).astype(BF16)


def on_device(
    hidden_in,
    queries,
    keys,
    values,
    out_proj,
    norm_gain,
    expert_ids,
    gate_fixed,
    live_counts,
    gate_proj,
    up_proj,
    down_proj,
):
    exp_index = lax.axis_index("exp")
    ctx_index = lax.axis_index("ctx")
    rep_index = lax.axis_index("rep")
    z, x = exp_index // N_X, exp_index % N_X
    y, side = ctx_index // 2, ctx_index % 2
    place = jnp.stack([z, x]).astype(jnp.int32)
    seq_rows = queries.shape[0]
    local_heads = queries.shape[1] // HEAD_DIM
    kv_index = exp_index * local_heads // (HEADS // KV_HEADS)

    kv = pick_head(kv_index.astype(jnp.int32)[None], keys, values)
    own, swapped, below, above, below_swapped, below_two, above_swapped, far_a, far_b = gather_ctx(
        kv, seq_rows
    )

    def seen(dy, flip):
        return ((((y + dy) % N_Y) * 2 + (side ^ flip)) < ctx_index).astype(jnp.int32)

    no_flag = jnp.ones((1,), jnp.int32)
    state = attend(queries, [own], no_flag, None, False)
    state = attend(
        queries,
        [swapped, below, above],
        jnp.stack([seen(0, 1), seen(-1, 0), seen(1, 0)]),
        state,
        False,
    )
    state = attend(
        queries,
        [below_swapped, below_two, above_swapped],
        jnp.stack([seen(-1, 1), seen(-2, 0), seen(1, 1)]),
        state,
        False,
    )
    far = jnp.concatenate([far_a, far_b], axis=0)
    attended = attend(queries, [far], seen(-2, 1)[None], state, True)

    own_weight, *away = pick_weights(jnp.stack([rep_index, x]).astype(jnp.int32), out_proj)
    weights = [own_weight]
    for d in range(1, N_X):
        got = shift_x(away[d - 1], d)
        other = swap_core(got)
        low = jnp.where(rep_index == 0, got, other)
        high = jnp.where(rep_index == 0, other, got)
        weights.append(jnp.concatenate([low, high], axis=0))

    half = seq_rows // 2
    from_left = shift_x(attended, 1)
    from_right = shift_x(attended, -1)
    from_far = jnp.concatenate(
        [shift_x(from_left[:half], 1), shift_x(from_right[half:], -1)], axis=0
    )
    chunks = project(place, [attended, from_left, from_far, from_right], weights)

    middle = chunks[0].shape[1] // 2
    low = shift_z(chunks[2][:, :middle], 1)
    high = shift_z(chunks[2][:, middle:], -1)
    up_chunk = jnp.concatenate([add(chunks[1][:, :middle], low), chunks[1][:, middle:]], axis=1)
    down_chunk = jnp.concatenate([chunks[3][:, :middle], add(chunks[3][:, middle:], high)], axis=1)
    got_up = shift_z(up_chunk, 1)
    got_down = shift_z(down_chunk, -1)
    summed = (chunks[0].astype(F32) + got_up.astype(F32) + got_down.astype(F32)).astype(BF16)
    pieces = [shift_x(summed[d * TOKENS : (d + 1) * TOKENS], d) for d in range(1, N_X)]

    pick, weight = route(place, expert_ids.T, gate_fixed.T, live_counts)
    mixed, *send = normalise(
        place, hidden_in, summed[:TOKENS], pieces, norm_gain.reshape(1, D), pick
    )

    by_x = [send[0]] + [shift_x(send[d], d) for d in range(1, N_X)]
    by_z = regroup(by_x)
    block = jnp.concatenate([by_z[0]] + [shift_z(by_z[d], d) for d in range(1, N_Z)], axis=0)
    rows = gather_ctx(block, TOKENS // 2)
    parts = run_expert(rows, gate_proj, up_proj, down_proj)
    result = scatter_ctx(parts, TOKENS // 2)
    back_z = [result[:8]] + [shift_z(result[8 * d : 8 * d + 8], -d) for d in range(1, N_Z)]
    back_x = regroup(back_z)
    returned = [back_x[0]] + [shift_x(back_x[d], -d) for d in range(1, N_X)]
    return (mixed, combine(weight, returned))


def solution(mesh):
    in_specs = (
        P(("rep", "ctx", "exp"), None),
        P(("rep", "ctx"), "exp"),
        P(("rep", "ctx"), None),
        P(("rep", "ctx"), None),
        P("exp", None),
        P(),
        P(("rep", "ctx", "exp"), None),
        P(("rep", "ctx", "exp"), None),
        P(("rep", "ctx", "exp")),
        P("exp", None, "ctx"),
        P("exp", None, "ctx"),
        P("exp", "ctx", None),
    )
    out_specs = (P(("rep", "ctx", "exp"), None), P(("rep", "ctx", "exp"), None))
    return jax.shard_map(
        on_device, mesh=mesh, in_specs=in_specs, out_specs=out_specs, check_vma=False
    )
```

```python
import functools
import math

import jax
import jax.numpy as jnp
from jax import lax
from jax.experimental import pallas as pl
from jax.experimental.pallas import tpu as pltpu
from jax.sharding import PartitionSpec as P

D = 4096
HEADS = 64
KV_HEADS = 4
HEAD_DIM = 128
TOPK = 8
CAP = 2
N_X = 4
N_Z = 4
N_Y = 4
TOKENS = 32
BF16 = jnp.bfloat16
F32 = jnp.float32
LOWEST = -1e30
EXP2_SCALE = HEAD_DIM ** (-0.5) * math.log2(math.e)
VMEM = pltpu.VMEM
SMEM = pltpu.SMEM


def params(limit_mib=48):
    return pltpu.CompilerParams(vmem_limit_bytes=limit_mib << 20)


def whole():
    return pl.BlockSpec(memory_space=VMEM)


def shift_x(a, d):
    pairs = [(z * N_X + x, z * N_X + (x + d) % N_X) for z in range(N_Z) for x in range(N_X)]
    return lax.ppermute(a, "exp", pairs)


def shift_z(a, d):
    pairs = [(z * N_X + x, (z + d) % N_Z * N_X + x) for z in range(N_Z) for x in range(N_X)]
    return lax.ppermute(a, "exp", pairs)


def shift_y(a, d):
    pairs = [(y * 2 + k, (y + d) % N_Y * 2 + k) for y in range(N_Y) for k in range(2)]
    return lax.ppermute(a, "ctx", pairs)


def swap_l(a):
    return lax.ppermute(a, "ctx", [(i, i ^ 1) for i in range(2 * N_Y)])


def swap_core(a):
    return lax.ppermute(a, "rep", [(0, 1), (1, 0)])


def pick_head(where_am, keys, values):
    rows = keys.shape[0]

    def kernel(where_ref, key_ref, value_ref, out_ref):
        out_ref[0:rows, :] = key_ref[...]
        out_ref[rows:, :] = value_ref[...]

    column = pl.BlockSpec((rows, HEAD_DIM), lambda i, w: (0, w[0]))
    return pl.pallas_call(
        kernel,
        grid_spec=pltpu.PrefetchScalarGridSpec(
            num_scalar_prefetch=1,
            grid=(1,),
            in_specs=[column, column],
            out_specs=pl.BlockSpec((2 * rows, HEAD_DIM), lambda i, w: (0, 0)),
        ),
        out_shape=jax.ShapeDtypeStruct((2 * rows, HEAD_DIM), BF16),
        name="pick_head",
    )(where_am, keys, values)


def pick_weights(place, out_proj):
    rows, cols = out_proj.shape[0] // 2, out_proj.shape[1] // N_X

    def kernel(place_ref, *refs):
        for source, target in zip(refs[:3], refs[3:]):
            target[...] = source[...]

    def block(d):
        return pl.BlockSpec((rows, cols), lambda i, w: (w[0], lax.rem(w[1] + d, N_X)))

    return pl.pallas_call(
        kernel,
        grid_spec=pltpu.PrefetchScalarGridSpec(
            num_scalar_prefetch=1,
            grid=(1,),
            in_specs=[block(d) for d in range(1, N_X)],
            out_specs=[pl.BlockSpec((rows, cols), lambda i, w: (0, 0))] * 3,
        ),
        out_shape=[jax.ShapeDtypeStruct((rows, cols), BF16)] * 3,
        compiler_params=params(),
        name="pick_weights",
    )(place, out_proj, out_proj, out_proj)


def attend(queries, blocks, bias, state, last):
    rows, heads = queries.shape[0], queries.shape[1] // HEAD_DIM
    tile = 128
    n = len(blocks)
    first = state is None

    def kernel(*refs):
        bias_ref, q_ref = refs[0], refs[1]
        kv_refs = refs[2 : 2 + n]
        rest = refs[2 + n :]
        if not first:
            acc_in, top_in = rest[0], rest[1]
            rest = rest[2:]
        key = jnp.concatenate([r[0:rows, :] for r in kv_refs], axis=0)
        ones = jnp.ones((rows, HEAD_DIM), BF16)
        value = jnp.concatenate(
            [jnp.concatenate([r[rows:, :], ones], axis=1) for r in kv_refs], axis=0
        )
        for part in range(rows // tile):
            at = pl.ds(part * tile, tile)
            seen = (part + 1) * tile if first else n * rows
            scores = lax.dot_general(
                q_ref[at, :], key[:seen], (((1,), (1,)), ((), ())), preferred_element_type=F32
            )
            if first:
                i = lax.broadcasted_iota(jnp.int32, scores.shape, 0) + part * tile
                j = lax.broadcasted_iota(jnp.int32, scores.shape, 1)
                scores = jnp.where(j <= i, scores, LOWEST)
                newest = jnp.broadcast_to(jnp.max(scores, axis=1, keepdims=True), (tile, HEAD_DIM))
                offsets = [newest * EXP2_SCALE]
            else:
                before = top_in[0, at, :]
                newest = before
                for b in range(n):
                    highest = jnp.max(scores[:, b * rows : (b + 1) * rows], axis=1, keepdims=True)
                    newest = jnp.maximum(newest, highest + bias_ref[b])
                offsets = [(newest - bias_ref[b]) * EXP2_SCALE for b in range(n)]
            pieces = []
            for lane in range(0, seen, HEAD_DIM):
                pieces.append(
                    jnp.exp2(
                        scores[:, lane : lane + HEAD_DIM] * EXP2_SCALE - offsets[lane // rows]
                    ).astype(BF16)
                )
            total = jnp.dot(
                jnp.concatenate(pieces, axis=1), value[:seen], preferred_element_type=F32
            )
            if not first:
                factor = jnp.exp2((before - newest) * EXP2_SCALE)
                total = acc_in[0, at, :] * jnp.concatenate([factor, factor], axis=1) + total
            if last:
                rest[0][at, :] = (total[:, :HEAD_DIM] / total[:, HEAD_DIM:]).astype(BF16)
            else:
                rest[0][0, at, :] = total
                rest[1][0, at, :] = newest

    q_spec = pl.BlockSpec((rows, HEAD_DIM), lambda h, f: (0, h))
    kv_spec = pl.BlockSpec((2 * rows, HEAD_DIM), lambda h, f: (0, 0))
    state_specs = [
        pl.BlockSpec((1, rows, 2 * HEAD_DIM), lambda h, f: (h, 0, 0)),
        pl.BlockSpec((1, rows, HEAD_DIM), lambda h, f: (h, 0, 0)),
    ]
    state_shapes = [
        jax.ShapeDtypeStruct((heads, rows, 2 * HEAD_DIM), F32),
        jax.ShapeDtypeStruct((heads, rows, HEAD_DIM), F32),
    ]
    return pl.pallas_call(
        kernel,
        grid_spec=pltpu.PrefetchScalarGridSpec(
            num_scalar_prefetch=1,
            grid=(heads,),
            in_specs=[q_spec] + [kv_spec] * n + ([] if first else state_specs),
            out_specs=q_spec if last else state_specs,
        ),
        out_shape=jax.ShapeDtypeStruct(queries.shape, BF16) if last else state_shapes,
        compiler_params=params(),
        cost_estimate=pl.CostEstimate(
            flops=heads * n * rows * rows * HEAD_DIM * 4,
            transcendentals=heads * n * rows * rows,
            bytes_accessed=4 << 20,
        ),
        name="attend",
    )(bias, queries, *blocks, *(() if first else state))


def gathered_rows(place_ref, left_ref, dz, columns):
    z, x = place_ref[0], place_ref[1]
    pieces = []
    for dx in range(N_X):
        row = lax.rem(z + dz, N_Z) * (N_X * TOKENS) + lax.rem(x + dx, N_X) * TOKENS
        pieces.append(left_ref[pl.ds(pl.multiple_of(row, TOKENS), TOKENS), columns])
    return jnp.concatenate(pieces, axis=0)


def project_near(place, own, out_proj, lefts, rights):
    n = len(lefts)
    rows = own.shape[1]
    cols = out_proj.shape[1] // N_X

    def kernel(place_ref, own_ref, weight_ref, *refs):
        left_refs, right_refs, out_refs = refs[:n], refs[n : 3 * n], refs[3 * n :]
        for dz in range(N_Z):
            out_refs[dz][...] = added(
                jnp.dot(
                    gathered_rows(place_ref, own_ref, dz, slice(None)),
                    weight_ref[...],
                    preferred_element_type=F32,
                ),
                place_ref,
                left_refs,
                right_refs,
                dz,
                rows,
            )

    fixed = lambda i, w: (0, 0)
    square = pl.BlockSpec(own.shape, fixed)
    return pl.pallas_call(
        kernel,
        grid_spec=pltpu.PrefetchScalarGridSpec(
            num_scalar_prefetch=1,
            grid=(1,),
            in_specs=[square, pl.BlockSpec((rows, cols), lambda i, w: (0, w[1]))]
            + [square] * n
            + [pl.BlockSpec((rows // 2, cols), fixed)] * (2 * n),
            out_specs=[pl.BlockSpec((N_X * TOKENS, cols), fixed)] * N_Z,
        ),
        out_shape=[jax.ShapeDtypeStruct((N_X * TOKENS, cols), F32)] * N_Z,
        compiler_params=params(),
        name="project_near",
    )(place, own, out_proj, *lefts, *rights)


def added(total, place_ref, left_refs, right_refs, dz, rows):
    half = rows // 2
    for k, left_ref in enumerate(left_refs):
        for side in range(2):
            core = place_ref[2] if side == 0 else 1 - place_ref[2]
            columns = pl.ds(pl.multiple_of(core * half, half), half)
            total = total + jnp.dot(
                gathered_rows(place_ref, left_ref, dz, columns),
                right_refs[2 * k + side][...],
                preferred_element_type=F32,
            )
    return total


def project_far(place, near, left, rights):
    rows = left.shape[1]
    shape = near[0].shape
    middle = shape[1] // 2

    def kernel(place_ref, left_ref, *refs):
        right_refs, near_refs, out_refs = refs[:2], refs[2:6], refs[6:]
        for dz in (2, 1, 3, 0):
            total = added(near_refs[dz][...], place_ref, [left_ref], right_refs, dz, rows).astype(BF16)
            if dz == 2:
                out_refs[3][...] = total[:, :middle]
                out_refs[4][...] = total[:, middle:]
            else:
                out_refs[{0: 0, 1: 1, 3: 2}[dz]][...] = total

    return pl.pallas_call(
        kernel,
        in_specs=[pl.BlockSpec(memory_space=SMEM)] + [whole()] * 7,
        out_specs=[whole()] * 5,
        out_shape=[jax.ShapeDtypeStruct(shape, BF16)] * 3
        + [jax.ShapeDtypeStruct((shape[0], middle), BF16)] * 2,
        compiler_params=params(),
        name="project_far",
    )(place, left, *rights, *near)


def pick_hidden(place, live, hidden_in, ids):
    cols = D // N_X

    def kernel(place_ref, live_ref, hidden_ref, id_ref, *out_refs):
        x = place_ref[1]
        t = lax.broadcasted_iota(jnp.int32, (TOPK, TOKENS), 1)
        alive = jnp.where(t < live_ref[0], id_ref[...] + 1, 0).astype(F32)
        for d in range(N_X):
            column = pl.ds(pl.multiple_of(lax.rem(x + N_X - d, N_X) * cols, cols), cols)
            out_refs[d][0:TOKENS, :] = hidden_ref[:, column]
            place_at = (
                lax.broadcasted_iota(jnp.int32, (TOKENS, cols), 1)
                == lax.broadcasted_iota(jnp.int32, (TOKENS, cols), 0) + d * TOKENS
            ).astype(F32)
            out_refs[d][TOKENS:, :] = jnp.dot(
                alive, place_at, preferred_element_type=F32
            ).astype(BF16)

    return pl.pallas_call(
        kernel,
        in_specs=[pl.BlockSpec(memory_space=SMEM)] * 2 + [whole()] * 2,
        out_specs=[whole()] * N_X,
        out_shape=[jax.ShapeDtypeStruct((TOKENS + TOPK, cols), BF16)] * N_X,
        name="pick_hidden",
    )(place, live, hidden_in, ids)


def route(place, hidden):
    slots = N_Z * N_X * N_X * CAP
    tokens = N_X * TOKENS

    def kernel(place_ref, *refs):
        z, x = place_ref[0], place_ref[1]
        s = lax.broadcasted_iota(jnp.int32, (slots, tokens), 0)
        t = lax.broadcasted_iota(jnp.int32, (slots, tokens), 1)
        dz, dx, o, cap = s // 32, (s // 8) % 4, (s // 2) % 4, s % 2
        expert = ((z + dz) % N_Z) * N_X + (x + dx) % N_X
        mine = ((dx + N_X - o) % N_X) == t // TOKENS
        wanted = jnp.where(mine, expert + 1, -1).astype(F32)
        ids = sum(r[TOKENS:, 0:tokens].astype(F32) for r in refs[:4])
        present = jnp.zeros((slots, tokens), F32)
        for k in range(TOPK):
            present = present + (ids[k : k + 1, :] == wanted).astype(F32)
        earlier = (
            lax.broadcasted_iota(jnp.int32, (tokens, tokens), 0)
            < lax.broadcasted_iota(jnp.int32, (tokens, tokens), 1)
        ).astype(F32)
        rank = jnp.dot(present, earlier, preferred_element_type=F32)
        fits = jnp.abs(rank - cap.astype(F32)) < 0.5
        refs[4][...] = jnp.where(fits, present, 0.0).astype(BF16)

    return pl.pallas_call(
        kernel,
        in_specs=[pl.BlockSpec(memory_space=SMEM)] + [whole()] * 4,
        out_specs=whole(),
        out_shape=jax.ShapeDtypeStruct((slots, tokens), BF16),
        name="route",
    )(place, *hidden)


def route_weights(place, ids, gates, live):
    slots = N_X * N_Z * CAP

    def kernel(place_ref, live_ref, id_ref, gate_ref, weight_ref):
        z, x = place_ref[0], place_ref[1]
        s = lax.broadcasted_iota(jnp.int32, (slots, TOKENS), 0)
        t = lax.broadcasted_iota(jnp.int32, (slots, TOKENS), 1)
        dx, dz, cap = s // (N_Z * CAP), (s // CAP) % N_Z, s % CAP
        expert = ((z + dz) % N_Z) * N_X + (x + dx) % N_X
        present = jnp.zeros((slots, TOKENS), F32)
        weight = jnp.zeros((slots, TOKENS), F32)
        for k in range(TOPK):
            hit = ((id_ref[k : k + 1, :] == expert) & (t < live_ref[0])).astype(F32)
            present = present + hit
            weight = weight + hit * gate_ref[k : k + 1, :].astype(F32)
        earlier = (
            lax.broadcasted_iota(jnp.int32, (TOKENS, TOKENS), 0)
            < lax.broadcasted_iota(jnp.int32, (TOKENS, TOKENS), 1)
        ).astype(F32)
        rank = jnp.dot(present, earlier, preferred_element_type=F32)
        weight_ref[...] = jnp.where(jnp.abs(rank - cap.astype(F32)) < 0.5, weight, 0.0) / 4096.0

    return pl.pallas_call(
        kernel,
        in_specs=[pl.BlockSpec(memory_space=SMEM)] * 2 + [whole()] * 2,
        out_specs=whole(),
        out_shape=jax.ShapeDtypeStruct((slots, TOKENS), F32),
        name="route_weights",
    )(place, live, ids, gates)


def finish_rows(hidden, sums, pick):
    cols = sums[0].shape[1]

    def kernel(h0, h1, h2, h3, s0, s1, s2, pick_ref, *out_refs):
        hidden_rows = jnp.concatenate([h[0:TOKENS, :].astype(F32) for h in (h0, h1, h2, h3)], axis=0)
        residual = hidden_rows + (
            s0[...].astype(F32) + s1[...].astype(F32) + s2[...].astype(F32)
        )
        mixed = residual.astype(BF16)
        for b in range(N_X):
            out_refs[b][...] = mixed[b * TOKENS : (b + 1) * TOKENS, :]
        send = jnp.dot(pick_ref[...], mixed, preferred_element_type=F32).astype(BF16)
        for dz in range(N_Z):
            out_refs[N_X + dz][...] = send[dz * 32 : dz * 32 + 32, :]

    return pl.pallas_call(
        kernel,
        in_specs=[whole()] * 8,
        out_specs=[whole()] * 8,
        out_shape=[jax.ShapeDtypeStruct((32, cols), BF16)] * 8,
        compiler_params=params(),
        name="finish_rows",
    )(*hidden, *sums, pick)


def by_columns(groups):
    shape = groups[0].shape

    def kernel(*refs):
        held = [r[...] for r in refs[:4]]
        for dx in range(N_X):
            refs[4 + dx][...] = jnp.concatenate([h[dx * 8 : dx * 8 + 8, :] for h in held], axis=0)

    return pl.pallas_call(
        kernel,
        in_specs=[whole()] * 4,
        out_specs=[whole()] * 4,
        out_shape=[jax.ShapeDtypeStruct(shape, BF16)] * 4,
        name="by_columns",
    )(*groups)


def join_columns(place, pieces, gain=None):
    rows, cols = pieces[0].shape
    half = rows // 2

    def kernel(place_ref, *refs):
        x = place_ref[1]
        piece_refs, rest = refs[:N_X], refs[N_X:]
        if gain is None:
            for d, piece in enumerate(piece_refs):
                column = pl.ds(pl.multiple_of(lax.rem(x + N_X - d, N_X) * cols, cols), cols)
                rest[0][:, column] = piece[...]
            return
        values = [p[...].astype(F32) for p in piece_refs]
        square = sum(jnp.sum(v * v, axis=1, keepdims=True) for v in values)
        scale = lax.rsqrt(square / D + 1e-06)
        for d, value in enumerate(values):
            column = pl.ds(pl.multiple_of(lax.rem(x + N_X - d, N_X) * cols, cols), cols)
            rest[1][:, column] = (value * scale * rest[0][:, column]).astype(BF16)

    return pl.pallas_call(
        kernel,
        in_specs=[pl.BlockSpec(memory_space=SMEM)] + [whole()] * (N_X + (gain is not None)),
        out_specs=whole(),
        out_shape=jax.ShapeDtypeStruct((rows, D), BF16),
        name="join_columns",
    )(place, *pieces, *(() if gain is None else (gain,)))


def regroup(groups):
    rows = 4 * 4 * CAP

    def kernel(*refs):
        held = jnp.concatenate([r[...] for r in refs[:4]], axis=0)
        to = lax.broadcasted_iota(jnp.int32, (rows, rows), 0)
        come = lax.broadcasted_iota(jnp.int32, (rows, rows), 1)
        b, a, cap = to // 8, (to // CAP) % 4, to % CAP
        order = (come == a * 8 + b * CAP + cap).astype(BF16)
        moved = jnp.dot(order, held, preferred_element_type=F32).astype(BF16)
        for i in range(4):
            refs[4 + i][...] = moved[i * 8 : i * 8 + 8, :]

    return pl.pallas_call(
        kernel,
        in_specs=[whole()] * 4,
        out_specs=[whole()] * 4,
        out_shape=[jax.ShapeDtypeStruct((8, D), BF16)] * 4,
        name="regroup",
    )(*groups)


def run_expert(blocks, gate, up, down):
    n = len(blocks)

    def kernel(*refs):
        in_refs, (gate_ref, up_ref, down_ref), out_refs = refs[:n], refs[n : n + 3], refs[n + 3 :]
        rows = jnp.concatenate([r[...] for r in in_refs], axis=0)
        last = (((1,), (1,)), ((), ()))
        gate_part = lax.dot_general(rows, gate_ref[...], last, preferred_element_type=F32)
        up_part = lax.dot_general(rows, up_ref[...], last, preferred_element_type=F32)
        hidden = (gate_part / (1.0 + jnp.exp(-gate_part)) * up_part).astype(BF16)
        result = jnp.dot(hidden, down_ref[...], preferred_element_type=F32).astype(BF16)
        at = 0
        for r in out_refs:
            r[...] = result[at : at + r.shape[0], :]
            at += r.shape[0]

    return pl.pallas_call(
        kernel,
        in_specs=[whole()] * (n + 3),
        out_specs=[whole()] * n,
        out_shape=[jax.ShapeDtypeStruct(b.shape, BF16) for b in blocks],
        compiler_params=params(),
        name="run_expert",
    )(*blocks, gate, up, down)


def combine(weight, groups):
    def kernel(weight_ref, *refs):
        held = jnp.concatenate([r[...] for r in refs[:4]], axis=0).astype(F32)
        refs[4][...] = lax.dot_general(
            weight_ref[...],
            held,
            (((0,), (0,)), ((), ())),
            precision=lax.Precision.HIGHEST,
            preferred_element_type=F32,
        ).astype(BF16)

    return pl.pallas_call(
        kernel,
        in_specs=[whole()] * 5,
        out_specs=whole(),
        out_shape=jax.ShapeDtypeStruct((TOKENS, D), BF16),
        compiler_params=params(),
        name="combine",
    )(weight, *groups)


def add_part(whole_rows, part, first):
    half = part.shape[0]

    def kernel(a_ref, b_ref, out_ref):
        lo = slice(0, half) if first else slice(half, 2 * half)
        keep = slice(half, 2 * half) if first else slice(0, half)
        out_ref[lo, :] = (a_ref[lo, :].astype(F32) + b_ref[...].astype(F32)).astype(BF16)
        out_ref[keep, :] = a_ref[keep, :]

    return pl.pallas_call(
        kernel,
        in_specs=[whole()] * 2,
        out_specs=whole(),
        out_shape=jax.ShapeDtypeStruct(whole_rows.shape, BF16),
        name="add_part",
    )(whole_rows, part)


def add_rows(arrays, pieces):
    shape = arrays[0].shape
    n = len(arrays)

    def kernel(*refs):
        total = sum(r[...].astype(F32) for r in refs[:n]).astype(BF16)
        if pieces:
            for i in range(4):
                refs[n + i][...] = total[i * 8 : i * 8 + 8, :]
        else:
            refs[n][...] = total

    return pl.pallas_call(
        kernel,
        in_specs=[whole()] * n,
        out_specs=[whole()] * 4 if pieces else whole(),
        out_shape=[jax.ShapeDtypeStruct((8, shape[1]), BF16)] * 4
        if pieces
        else jax.ShapeDtypeStruct(shape, BF16),
        name="add_rows",
    )(*arrays)


def tie(values, *others):
    n = len(values)
    return lax.optimization_barrier((*values, *others))[:n]


def add(a, b):
    return (a.astype(F32) + b.astype(F32)).astype(BF16)


def scatter_ctx(parts):
    own, swapped, below, above, below_swapped, below_two, above_swapped, far_a, far_b = parts
    got_a = shift_y(far_a, -1)
    got_b = shift_y(far_b, 1)
    got_two = shift_y(below_two, -1)
    got_above = shift_y(above, 1)
    got_below_swapped = swap_l(add_part(below_swapped, got_a, True))
    got_above_swapped = shift_y(add_part(above_swapped, got_b, False), 1)
    got_below = shift_y(add_rows([below, got_two, got_below_swapped], False), -1)
    got_swapped = swap_l(add_rows([swapped, got_above_swapped], False))
    return add_rows([own, got_above, got_below, got_swapped], True)


def on_device(
    hidden_in,
    queries,
    keys,
    values,
    out_proj,
    norm_gain,
    expert_ids,
    gate_fixed,
    live_counts,
    gate_proj,
    up_proj,
    down_proj,
):
    exp_index = lax.axis_index("exp")
    ctx_index = lax.axis_index("ctx")
    rep_index = lax.axis_index("rep")
    z, x = exp_index // N_X, exp_index % N_X
    y, side = ctx_index // 2, ctx_index % 2
    place = jnp.stack([z, x, rep_index]).astype(jnp.int32)
    seq_rows = queries.shape[0]
    local_heads = queries.shape[1] // HEAD_DIM
    kv_index = exp_index * local_heads // (HEADS // KV_HEADS)

    def bias(*steps):
        owners = jnp.stack([((y + dy) % N_Y) * 2 + (side ^ flip) for dy, flip in steps])
        return jnp.where(owners < ctx_index, 0.0, LOWEST).astype(F32)

    own = pick_head(kv_index.astype(jnp.int32)[None], keys, values)
    swapped = swap_l(own)
    below = shift_y(own, 1)
    above = shift_y(own, -1)
    away = pick_weights(jnp.stack([rep_index, x]).astype(jnp.int32), out_proj)
    fetched = [shift_x(away[d - 1], d) for d in range(1, N_X)]
    state = attend(queries, [own], bias((0, 0)), None, False)
    swapped, below, above = tie((swapped, below, above), *state)
    below_swapped = swap_l(below)
    below_two = shift_y(below, 1)
    above_swapped = shift_y(swapped, -1)
    state = attend(
        queries, [swapped, below, above], bias((0, 1), (-1, 0), (1, 0)), state, False
    )
    below_swapped, below_two, above_swapped = tie(
        (below_swapped, below_two, above_swapped), *state
    )
    far_a = shift_y(below_swapped[:seq_rows], 1)
    far_b = shift_y(above_swapped[seq_rows:], -1)
    state = attend(
        queries,
        [below_swapped, below_two, above_swapped],
        bias((-1, 1), (-2, 0), (1, 1)),
        state,
        False,
    )
    far_a, far_b = tie((far_a, far_b), *state)
    far = jnp.concatenate([far_a, far_b], axis=0)
    attended = attend(queries, [far], bias((-2, 1)), state, True)

    from_left = shift_x(attended, 1)
    from_right = shift_x(attended, -1)
    from_far = shift_x(attended, 2)
    fetched = tie(fetched, attended)
    other = [swap_core(f) for f in fetched]
    ids = expert_ids.T
    hidden_in, later_place = tie((hidden_in, place), *other)
    hidden = pick_hidden(later_place, live_counts, hidden_in, ids)
    hidden = [hidden[0]] + [shift_x(hidden[d], -d) for d in range(1, N_X)]
    near = project_near(
        place,
        attended,
        out_proj,
        [from_left, from_right],
        [fetched[0], other[0], fetched[2], other[2]],
    )
    from_far, *near = tie((from_far, *near))
    mine, up_chunk, down_chunk, low, high = project_far(
        place, near, from_far, [fetched[1], other[1]]
    )

    middle = low.shape[1]
    got_low = shift_z(low, 1)
    got_high = shift_z(high, -1)
    up_chunk = jnp.concatenate([add(up_chunk[:, :middle], got_low), up_chunk[:, middle:]], axis=1)
    down_chunk = jnp.concatenate(
        [down_chunk[:, :middle], add(down_chunk[:, middle:], got_high)], axis=1
    )
    got_up = shift_z(up_chunk, 1)
    got_down = shift_z(down_chunk, -1)
    pick = route(place, hidden)
    finished = finish_rows(hidden, [mine, got_up, got_down], pick)
    mixed, send = finished[:N_X], finished[N_X:]

    by_z = [send[0]] + [shift_z(send[d], d) for d in range(1, N_Z)]
    by_x = by_columns(by_z)
    block = join_columns(
        place,
        [by_x[0]] + [shift_x(by_x[d], d) for d in range(1, N_X)],
        norm_gain.reshape(1, D),
    )
    half = TOKENS // 2
    swapped = swap_l(block)
    below = shift_y(block, 1)
    above = shift_y(block, -1)
    below_swapped = swap_l(below)
    below_two = shift_y(below, 1)
    above_swapped = shift_y(swapped, -1)
    far_a = shift_y(below_swapped[:half], 1)
    far_b = shift_y(above_swapped[half:], -1)
    mixed = tie(mixed, below_two)
    mixed = [mixed[0]] + [shift_x(mixed[d], d) for d in range(1, N_X)]
    parts = run_expert(
        [block, swapped, below, above, below_swapped, below_two, above_swapped, far_a, far_b],
        gate_proj[0].T,
        up_proj[0].T,
        down_proj[0],
    )

    result = scatter_ctx(parts)
    mixed = tie(mixed, parts[0])
    mixed = join_columns(place, mixed)
    weight = route_weights(place, ids, gate_fixed.T, live_counts)
    back_z = [result[0]] + [shift_z(result[d], -d) for d in range(1, N_Z)]
    back_x = regroup(back_z)
    returned = [back_x[0]] + [shift_x(back_x[d], -d) for d in range(1, N_X)]
    return (mixed, combine(weight, returned))


def solution(mesh):
    in_specs = (
        P(("rep", "ctx", "exp"), None),
        P(("rep", "ctx"), "exp"),
        P(("rep", "ctx"), None),
        P(("rep", "ctx"), None),
        P("exp", None),
        P(),
        P(("rep", "ctx", "exp"), None),
        P(("rep", "ctx", "exp"), None),
        P(("rep", "ctx", "exp")),
        P("exp", None, "ctx"),
        P("exp", None, "ctx"),
        P("exp", "ctx", None),
    )
    out_specs = (P(("rep", "ctx", "exp"), None), P(("rep", "ctx", "exp"), None))
    return jax.shard_map(
        on_device, mesh=mesh, in_specs=in_specs, out_specs=out_specs, check_vma=False
    )
```

```python
import functools
import math

import jax
import jax.numpy as jnp
from jax import lax
from jax.experimental import pallas as pl
from jax.experimental.pallas import tpu as pltpu
from jax.sharding import PartitionSpec as P

D = 4096
HEADS = 64
KV_HEADS = 4
HEAD_DIM = 128
TOPK = 8
CAP = 2
N_X = 4
N_Z = 4
N_Y = 4
TOKENS = 32
BF16 = jnp.bfloat16
F32 = jnp.float32
LOWEST = -1e30
EXP2_SCALE = HEAD_DIM ** (-0.5) * math.log2(math.e)
VMEM = pltpu.VMEM
SMEM = pltpu.SMEM


def params(limit_mib=8):
    return pltpu.CompilerParams(vmem_limit_bytes=limit_mib << 20)


def whole():
    return pl.BlockSpec(memory_space=VMEM)


def shift_x(a, d):
    pairs = [(z * N_X + x, z * N_X + (x + d) % N_X) for z in range(N_Z) for x in range(N_X)]
    return lax.ppermute(a, "exp", pairs)


def shift_z(a, d):
    pairs = [(z * N_X + x, (z + d) % N_Z * N_X + x) for z in range(N_Z) for x in range(N_X)]
    return lax.ppermute(a, "exp", pairs)


def shift_y(a, d):
    pairs = [(y * 2 + k, (y + d) % N_Y * 2 + k) for y in range(N_Y) for k in range(2)]
    return lax.ppermute(a, "ctx", pairs)


def swap_l(a):
    return lax.ppermute(a, "ctx", [(i, i ^ 1) for i in range(2 * N_Y)])


def swap_core(a):
    return lax.ppermute(a, "rep", [(0, 1), (1, 0)])


def pick_head(where_am, keys, values):
    rows = keys.shape[0]

    def kernel(where_ref, key_ref, value_ref, out_ref):
        out_ref[0:rows, :] = key_ref[...]
        out_ref[rows:, :] = value_ref[...]

    column = pl.BlockSpec((rows, HEAD_DIM), lambda i, w: (0, w[0]))
    return pl.pallas_call(
        kernel,
        grid_spec=pltpu.PrefetchScalarGridSpec(
            num_scalar_prefetch=1,
            grid=(1,),
            in_specs=[column, column],
            out_specs=pl.BlockSpec((2 * rows, HEAD_DIM), lambda i, w: (0, 0)),
        ),
        out_shape=jax.ShapeDtypeStruct((2 * rows, HEAD_DIM), BF16),
        compiler_params=params(),
        name="pick_head",
    )(where_am, keys, values)


def pick_weights(place, out_proj):
    rows, cols = out_proj.shape[0] // 2, out_proj.shape[1] // N_X

    def kernel(place_ref, *refs):
        for source, target in zip(refs[:3], refs[3:]):
            target[...] = source[...]

    def block(d):
        return pl.BlockSpec((rows, cols), lambda i, w: (w[0], lax.rem(w[1] + d, N_X)))

    return pl.pallas_call(
        kernel,
        grid_spec=pltpu.PrefetchScalarGridSpec(
            num_scalar_prefetch=1,
            grid=(1,),
            in_specs=[block(d) for d in range(1, N_X)],
            out_specs=[pl.BlockSpec((rows, cols), lambda i, w: (0, 0))] * 3,
        ),
        out_shape=[jax.ShapeDtypeStruct((rows, cols), BF16)] * 3,
        compiler_params=params(),
        name="pick_weights",
    )(place, out_proj, out_proj, out_proj)


def attend(queries, blocks, bias, state, last):
    rows, heads = queries.shape[0], queries.shape[1] // HEAD_DIM
    n = len(blocks)
    first = state is None
    tile = 128

    def kernel(*refs):
        bias_ref, q_ref = refs[0], refs[1]
        kv_refs = refs[2 : 2 + n]
        rest = refs[2 + n :]
        if not first:
            acc_in, top_in = rest[0], rest[1]
            rest = rest[2:]
        key = jnp.concatenate([r[0:rows, :] for r in kv_refs], axis=0)
        ones = jnp.ones((rows, HEAD_DIM), BF16)
        value = jnp.concatenate(
            [jnp.concatenate([r[rows:, :], ones], axis=1) for r in kv_refs], axis=0
        )
        for part in range(rows // tile):
            at = pl.ds(part * tile, tile)
            seen = n * rows
            scores = lax.dot_general(
                q_ref[at, :], key[:seen], (((1,), (1,)), ((), ())), preferred_element_type=F32
            )
            if first:
                i = lax.broadcasted_iota(jnp.int32, (tile, rows), 0) + part * tile
                j = lax.broadcasted_iota(jnp.int32, (tile, rows), 1)
                diagonal = jnp.where(j <= i, scores[:, :rows], LOWEST)
                scores = jnp.concatenate([diagonal, scores[:, rows:]], axis=1)
                newest = jnp.full((tile, HEAD_DIM), LOWEST, F32)
            else:
                before = top_in[0, at, :]
                newest = before
            for b in range(n):
                highest = jnp.max(scores[:, b * rows : (b + 1) * rows], axis=1, keepdims=True)
                newest = jnp.maximum(newest, highest + bias_ref[b])
            offsets = [(newest - bias_ref[b]) * EXP2_SCALE for b in range(n)]
            pieces = []
            for lane in range(0, seen, HEAD_DIM):
                pieces.append(
                    jnp.exp2(
                        scores[:, lane : lane + HEAD_DIM] * EXP2_SCALE - offsets[lane // rows]
                    ).astype(BF16)
                )
            total = jnp.dot(
                jnp.concatenate(pieces, axis=1), value[:seen], preferred_element_type=F32
            )
            if not first:
                factor = jnp.exp2((before - newest) * EXP2_SCALE)
                total = acc_in[0, at, :] * jnp.concatenate([factor, factor], axis=1) + total
            if last:
                rest[0][at, :] = (total[:, :HEAD_DIM] / total[:, HEAD_DIM:]).astype(BF16)
            else:
                rest[0][0, at, :] = total
                rest[1][0, at, :] = newest

    q_spec = pl.BlockSpec((rows, HEAD_DIM), lambda h, f: (0, h))
    kv_spec = pl.BlockSpec((2 * rows, HEAD_DIM), lambda h, f: (0, 0))
    state_specs = [
        pl.BlockSpec((1, rows, 2 * HEAD_DIM), lambda h, f: (h, 0, 0)),
        pl.BlockSpec((1, rows, HEAD_DIM), lambda h, f: (h, 0, 0)),
    ]
    state_shapes = [
        jax.ShapeDtypeStruct((heads, rows, 2 * HEAD_DIM), F32),
        jax.ShapeDtypeStruct((heads, rows, HEAD_DIM), F32),
    ]
    return pl.pallas_call(
        kernel,
        grid_spec=pltpu.PrefetchScalarGridSpec(
            num_scalar_prefetch=1,
            grid=(heads,),
            in_specs=[q_spec] + [kv_spec] * n + ([] if first else state_specs),
            out_specs=q_spec if last else state_specs,
        ),
        out_shape=jax.ShapeDtypeStruct(queries.shape, BF16) if last else state_shapes,
        compiler_params=params(20),
        cost_estimate=pl.CostEstimate(
            flops=heads * n * rows * rows * HEAD_DIM * 4,
            transcendentals=heads * n * rows * rows,
            bytes_accessed=4 << 20,
        ),
        name="attend",
    )(bias, queries, *blocks, *(() if first else state))


def rows_of(place_ref, left_ref, dz, columns):
    row = lax.rem(place_ref[0] + dz, N_Z) * (N_X * TOKENS)
    return left_ref[pl.ds(pl.multiple_of(row, N_X * TOKENS), N_X * TOKENS), columns]


def project_near(place, own, out_proj, lefts, fetched, other):
    n = len(lefts)
    rows = own.shape[1]
    cols = out_proj.shape[1] // N_X

    def kernel(place_ref, own_ref, weight_ref, *refs):
        left_refs, fetched_refs, other_ref, out_refs = refs[:n], refs[n : 2 * n], refs[2 * n], refs[2 * n + 1 :]
        for dz in range(N_Z):
            total = jnp.dot(
                rows_of(place_ref, own_ref, dz, slice(None)),
                weight_ref[...],
                preferred_element_type=F32,
            )
            for k in range(n):
                total = total + fetched_part(
                    place_ref, left_refs[k], fetched_refs[k], other_ref, (0, 2)[k], dz
                )
            out_refs[dz][...] = total

    fixed = lambda i, w: (0, 0)
    square = pl.BlockSpec(own.shape, fixed)
    return pl.pallas_call(
        kernel,
        grid_spec=pltpu.PrefetchScalarGridSpec(
            num_scalar_prefetch=1,
            grid=(1,),
            in_specs=[square, pl.BlockSpec((rows, cols), lambda i, w: (0, w[1]))]
            + [square] * n
            + [pl.BlockSpec((rows // 2, cols), fixed)] * n
            + [pl.BlockSpec(other.shape, fixed)],
            out_specs=[pl.BlockSpec((N_X * TOKENS, cols), fixed)] * N_Z,
        ),
        out_shape=[jax.ShapeDtypeStruct((N_X * TOKENS, cols), F32)] * N_Z,
        compiler_params=params(28),
        name="project_near",
    )(place, own, out_proj, *lefts, *fetched, other)


def fetched_part(place_ref, left_ref, fetched_ref, other_ref, at, dz):
    half = fetched_ref.shape[0]
    core = place_ref[2]
    mine = pl.ds(pl.multiple_of(core * half, half), half)
    theirs = pl.ds(pl.multiple_of((1 - core) * half, half), half)
    return jnp.dot(
        rows_of(place_ref, left_ref, dz, mine), fetched_ref[...], preferred_element_type=F32
    ) + jnp.dot(
        rows_of(place_ref, left_ref, dz, theirs),
        other_ref[at * half : (at + 1) * half, :],
        preferred_element_type=F32,
    )


def project_far(place, near, left, fetched, other):
    shape = near[0].shape
    middle = shape[1] // 2

    def kernel(place_ref, left_ref, fetched_ref, other_ref, *refs):
        near_refs, out_refs = refs[:4], refs[4:]
        for dz in (2, 1, 3, 0):
            total = near_refs[dz][...] + fetched_part(
                place_ref, left_ref, fetched_ref, other_ref, 1, dz
            )
            total = total.astype(BF16)
            if dz == 2:
                out_refs[3][...] = total[:, :middle]
                out_refs[4][...] = total[:, middle:]
            else:
                out_refs[{0: 0, 1: 1, 3: 2}[dz]][...] = total

    return pl.pallas_call(
        kernel,
        in_specs=[pl.BlockSpec(memory_space=SMEM)] + [whole()] * 7,
        out_specs=[whole()] * 5,
        out_shape=[jax.ShapeDtypeStruct(shape, BF16)] * 3
        + [jax.ShapeDtypeStruct((shape[0], middle), BF16)] * 2,
        compiler_params=params(),
        name="project_far",
    )(place, left, fetched, other, *near)


def pick_hidden(place, live, hidden_in, ids):
    cols = D // N_X

    def kernel(place_ref, live_ref, hidden_ref, id_ref, *out_refs):
        x = place_ref[1]
        t = lax.broadcasted_iota(jnp.int32, (TOPK, TOKENS), 1)
        alive = jnp.where(t < live_ref[0], id_ref[...] + 1, 0).astype(F32)
        for d in range(N_X):
            column = pl.ds(pl.multiple_of(lax.rem(x + N_X - d, N_X) * cols, cols), cols)
            out_refs[d][0:TOKENS, :] = hidden_ref[:, column]
            place_at = (
                lax.broadcasted_iota(jnp.int32, (TOKENS, cols), 1)
                == lax.broadcasted_iota(jnp.int32, (TOKENS, cols), 0) + x * TOKENS
            ).astype(F32)
            out_refs[d][TOKENS:, :] = jnp.dot(
                alive, place_at, preferred_element_type=F32
            ).astype(BF16)

    return pl.pallas_call(
        kernel,
        in_specs=[pl.BlockSpec(memory_space=SMEM)] * 2 + [whole()] * 2,
        out_specs=[whole()] * N_X,
        out_shape=[jax.ShapeDtypeStruct((TOKENS + TOPK, cols), BF16)] * N_X,
        compiler_params=params(),
        name="pick_hidden",
    )(place, live, hidden_in, ids)


def route(place, hidden):
    slots = N_Z * N_X * N_X * CAP
    tokens = N_X * TOKENS

    def kernel(place_ref, *refs):
        z = place_ref[0]
        s = lax.broadcasted_iota(jnp.int32, (slots, tokens), 0)
        t = lax.broadcasted_iota(jnp.int32, (slots, tokens), 1)
        dz, expert_x, owner, cap = s // 32, (s // 8) % 4, (s // 2) % 4, s % 2
        expert = ((z + dz) % N_Z) * N_X + expert_x
        wanted = jnp.where(owner == t // TOKENS, expert + 1, -1).astype(F32)
        ids = sum(r[TOKENS:, 0:tokens].astype(F32) for r in refs[:4])
        present = jnp.zeros((slots, tokens), F32)
        for k in range(TOPK):
            present = present + (ids[k : k + 1, :] == wanted).astype(F32)
        earlier = (
            lax.broadcasted_iota(jnp.int32, (tokens, tokens), 0)
            < lax.broadcasted_iota(jnp.int32, (tokens, tokens), 1)
        ).astype(F32)
        rank = jnp.dot(present, earlier, preferred_element_type=F32)
        fits = jnp.abs(rank - cap.astype(F32)) < 0.5
        refs[4][...] = jnp.where(fits, present, 0.0).astype(BF16)

    return pl.pallas_call(
        kernel,
        in_specs=[pl.BlockSpec(memory_space=SMEM)] + [whole()] * 4,
        out_specs=whole(),
        out_shape=jax.ShapeDtypeStruct((slots, tokens), BF16),
        compiler_params=params(),
        name="route",
    )(place, *hidden)


def route_weights(place, ids, gates, live):
    slots = N_X * N_Z * CAP

    def kernel(place_ref, live_ref, id_ref, gate_ref, weight_ref):
        z = place_ref[0]
        s = lax.broadcasted_iota(jnp.int32, (slots, TOKENS), 0)
        t = lax.broadcasted_iota(jnp.int32, (slots, TOKENS), 1)
        expert_x, dz, cap = s // (N_Z * CAP), (s // CAP) % N_Z, s % CAP
        expert = ((z + dz) % N_Z) * N_X + expert_x
        present = jnp.zeros((slots, TOKENS), F32)
        weight = jnp.zeros((slots, TOKENS), F32)
        for k in range(TOPK):
            hit = ((id_ref[k : k + 1, :] == expert) & (t < live_ref[0])).astype(F32)
            present = present + hit
            weight = weight + hit * gate_ref[k : k + 1, :].astype(F32)
        earlier = (
            lax.broadcasted_iota(jnp.int32, (TOKENS, TOKENS), 0)
            < lax.broadcasted_iota(jnp.int32, (TOKENS, TOKENS), 1)
        ).astype(F32)
        rank = jnp.dot(present, earlier, preferred_element_type=F32)
        weight_ref[...] = jnp.where(jnp.abs(rank - cap.astype(F32)) < 0.5, weight, 0.0) / 4096.0

    return pl.pallas_call(
        kernel,
        in_specs=[pl.BlockSpec(memory_space=SMEM)] * 2 + [whole()] * 2,
        out_specs=whole(),
        out_shape=jax.ShapeDtypeStruct((slots, TOKENS), F32),
        compiler_params=params(),
        name="route_weights",
    )(place, live, ids, gates)


def finish_rows(place, hidden, sums, pick):
    cols = sums[0].shape[1]

    def kernel(place_ref, h0, h1, h2, h3, s0, s1, s2, pick_ref, *refs):
        mixed_ref, send_refs = refs[0], refs[1:5]
        for d, h in enumerate((h0, h1, h2, h3)):
            at = pl.ds(pl.multiple_of(lax.rem(place_ref[1] + d, N_X) * TOKENS, TOKENS), TOKENS)
            mixed_ref[at, :] = (
                h[0:TOKENS, :].astype(F32)
                + (s0[at, :].astype(F32) + s1[at, :].astype(F32) + s2[at, :].astype(F32))
            ).astype(BF16)
        send = jnp.dot(pick_ref[...], mixed_ref[...], preferred_element_type=F32).astype(BF16)
        for dz in range(N_Z):
            send_refs[dz][...] = send[dz * 32 : dz * 32 + 32, :]

    return pl.pallas_call(
        kernel,
        in_specs=[pl.BlockSpec(memory_space=SMEM)] + [whole()] * 8,
        out_specs=[whole()] * 5,
        out_shape=[jax.ShapeDtypeStruct((N_X * TOKENS, cols), BF16)]
        + [jax.ShapeDtypeStruct((32, cols), BF16)] * 4,
        compiler_params=params(),
        name="finish_rows",
    )(place, *hidden, *sums, pick)


def by_columns(groups, mixed):
    cols = mixed.shape[1]

    def kernel(*refs):
        held = [r[...] for r in refs[:4]]
        for x in range(N_X):
            refs[5][x, 0:32, :] = jnp.concatenate([h[x * 8 : x * 8 + 8, :] for h in held], axis=0)
            refs[5][x, 32:64, :] = refs[4][x * TOKENS : (x + 1) * TOKENS, :]

    return pl.pallas_call(
        kernel,
        in_specs=[whole()] * 5,
        out_specs=whole(),
        out_shape=jax.ShapeDtypeStruct((N_X, 64, cols), BF16),
        compiler_params=params(),
        name="by_columns",
    )(*groups, mixed)


def join_columns(pieces, gain):
    cols = pieces.shape[2]

    def kernel(piece_ref, gain_ref, block_ref, mixed_ref):
        values = [piece_ref[x, 0:32, :].astype(F32) for x in range(N_X)]
        square = sum(jnp.sum(v * v, axis=1, keepdims=True) for v in values)
        scale = lax.rsqrt(square / D + 1e-06)
        for x, value in enumerate(values):
            column = slice(x * cols, (x + 1) * cols)
            block_ref[:, column] = (value * scale * gain_ref[:, column]).astype(BF16)
            mixed_ref[:, column] = piece_ref[x, 32:64, :]

    return pl.pallas_call(
        kernel,
        in_specs=[whole()] * 2,
        out_specs=[whole()] * 2,
        out_shape=[jax.ShapeDtypeStruct((32, D), BF16)] * 2,
        compiler_params=params(),
        name="join_columns",
    )(pieces, gain)


def regroup(groups):
    rows = 4 * 4 * CAP

    def kernel(*refs):
        held = jnp.concatenate([r[...] for r in refs[:4]], axis=0)
        to = lax.broadcasted_iota(jnp.int32, (rows, rows), 0)
        come = lax.broadcasted_iota(jnp.int32, (rows, rows), 1)
        b, a, cap = to // 8, (to // CAP) % 4, to % CAP
        order = (come == a * 8 + b * CAP + cap).astype(BF16)
        moved = jnp.dot(order, held, preferred_element_type=F32).astype(BF16)
        for i in range(4):
            refs[4][i] = moved[i * 8 : i * 8 + 8, :]

    return pl.pallas_call(
        kernel,
        in_specs=[whole()] * 4,
        out_specs=whole(),
        out_shape=jax.ShapeDtypeStruct((4, 8, D), BF16),
        compiler_params=params(),
        name="regroup",
    )(*groups)


def run_expert(blocks, gate, up, down):
    n = len(blocks)

    def kernel(*refs):
        in_refs, (gate_ref, up_ref, down_ref), out_refs = refs[:n], refs[n : n + 3], refs[n + 3 :]
        rows = jnp.concatenate([r[...] for r in in_refs], axis=0)
        last = (((1,), (1,)), ((), ()))
        gate_part = lax.dot_general(rows, gate_ref[...], last, preferred_element_type=F32)
        up_part = lax.dot_general(rows, up_ref[...], last, preferred_element_type=F32)
        hidden = (gate_part / (1.0 + jnp.exp(-gate_part)) * up_part).astype(BF16)
        result = jnp.dot(hidden, down_ref[...], preferred_element_type=F32).astype(BF16)
        at = 0
        for r in out_refs:
            r[...] = result[at : at + r.shape[0], :]
            at += r.shape[0]

    return pl.pallas_call(
        kernel,
        in_specs=[whole()] * (n + 3),
        out_specs=[whole()] * n,
        out_shape=[jax.ShapeDtypeStruct(b.shape, BF16) for b in blocks],
        compiler_params=params(24),
        name="run_expert",
    )(*blocks, gate, up, down)


def combine(weight, groups):
    def kernel(weight_ref, *refs):
        held = jnp.concatenate([refs[0][i] for i in range(4)], axis=0).astype(F32)
        refs[1][...] = lax.dot_general(
            weight_ref[...],
            held,
            (((0,), (0,)), ((), ())),
            precision=lax.Precision.HIGHEST,
            preferred_element_type=F32,
        ).astype(BF16)

    return pl.pallas_call(
        kernel,
        in_specs=[whole()] * 2,
        out_specs=whole(),
        out_shape=jax.ShapeDtypeStruct((TOKENS, D), BF16),
        compiler_params=params(),
        name="combine",
    )(weight, groups)


def tie(values, *others):
    n = len(values)
    return lax.optimization_barrier((*values, *others))[:n]


def add(*arrays):
    return sum(a.astype(F32) for a in arrays).astype(BF16)


def exchange_x(a):
    groups = [[z * N_X + x for x in range(N_X)] for z in range(N_Z)]
    return lax.all_to_all(a, "exp", 0, 0, tiled=True, axis_index_groups=groups)


def scatter_ctx(parts):
    own, swapped, below, above, below_swapped, below_two, above_swapped, far = parts
    got_far = swap_l(far)
    got_below_swapped = swap_l(below_swapped)
    got_above_swapped = shift_y(above_swapped, 1)
    got_two = shift_y(add(below_two, got_far), -1)
    got_above = shift_y(above, 1)
    got_swapped = swap_l(add(swapped, got_above_swapped))
    got_below = shift_y(add(below, got_two, got_below_swapped), -1)
    return add(own, got_above, got_below, got_swapped)


def on_device(
    hidden_in,
    queries,
    keys,
    values,
    out_proj,
    norm_gain,
    expert_ids,
    gate_fixed,
    live_counts,
    gate_proj,
    up_proj,
    down_proj,
):
    exp_index = lax.axis_index("exp")
    ctx_index = lax.axis_index("ctx")
    rep_index = lax.axis_index("rep")
    z, x = exp_index // N_X, exp_index % N_X
    y, side = ctx_index // 2, ctx_index % 2
    place = jnp.stack([z, x, rep_index]).astype(jnp.int32)
    seq_rows = queries.shape[0]
    local_heads = queries.shape[1] // HEAD_DIM
    kv_index = exp_index * local_heads // (HEADS // KV_HEADS)

    def bias(*steps):
        owners = jnp.stack([((y + dy) % N_Y) * 2 + (side ^ flip) for dy, flip in steps])
        return jnp.where(owners < ctx_index, 0.0, LOWEST).astype(F32)

    own = pick_head(kv_index.astype(jnp.int32)[None], keys, values)
    swapped = swap_l(own)
    below = shift_y(own, 1)
    above = shift_y(own, -1)
    out_proj = pltpu.with_memory_space_constraint(out_proj, pltpu.HBM)
    away = pick_weights(jnp.stack([rep_index, x]).astype(jnp.int32), out_proj)
    fetched = [shift_x(away[0], 1), None, shift_x(away[2], 3)]
    swapped, below, above = tie((swapped, below, above), *away)
    below_two = shift_y(below, 1)
    below_swapped = swap_l(below)
    above_swapped = shift_y(swapped, -1)
    state = attend(
        queries,
        [own, swapped, below, above],
        jnp.concatenate([jnp.zeros((1,), F32), bias((0, 1), (-1, 0), (1, 0))]),
        None,
        False,
    )
    below_two, below_swapped, above_swapped = tie(
        (below_two, below_swapped, above_swapped), *state
    )
    far = swap_l(below_two)
    (away_far,) = tie((away[1],), *state)
    fetched[1] = shift_x(away_far, 2)
    below_swapped, above_swapped, *state = tie(
        (below_swapped, above_swapped, *state), fetched[0], fetched[2]
    )
    state = attend(
        queries,
        [below_swapped, below_two, above_swapped],
        bias((-1, 1), (-2, 0), (1, 1)),
        state,
        False,
    )
    (far,) = tie((far,), *state)
    attended = attend(queries, [far], bias((-2, 1)), state, True)

    half = seq_rows // 2
    from_left = shift_x(attended, 1)
    from_right = shift_x(attended, -1)
    ids = expert_ids.T
    hidden_in, later_place = tie((hidden_in, place), attended)
    hidden = pick_hidden(later_place, live_counts, hidden_in, ids)
    from_left, from_right = tie((from_left, from_right), *hidden)
    far_a = shift_x(from_left[:half], 1)
    far_b = shift_x(from_right[half:], -1)
    fetched = tie(fetched, from_left)
    other = swap_core(jnp.concatenate(fetched, axis=0))
    hidden = [hidden[0]] + [shift_x(hidden[d], -d) for d in range(1, N_X)]
    pick = route(place, hidden)
    weight = route_weights(later_place, ids, gate_fixed.T, live_counts)
    from_left, from_right = tie((from_left, from_right), pick, weight)
    near = project_near(
        place, attended, out_proj, [from_left, from_right], [fetched[0], fetched[2]], other
    )
    far_a, far_b = tie((far_a, far_b), *near)
    from_far = jnp.concatenate([far_a, far_b], axis=0)
    mine, up_chunk, down_chunk, low, high = project_far(place, near, from_far, fetched[1], other)

    middle = low.shape[1]
    got_low = shift_z(low, 1)
    got_high = shift_z(high, -1)
    up_chunk = jnp.concatenate([add(up_chunk[:, :middle], got_low), up_chunk[:, middle:]], axis=1)
    down_chunk = jnp.concatenate(
        [down_chunk[:, :middle], add(down_chunk[:, middle:], got_high)], axis=1
    )
    got_up = shift_z(up_chunk, 1)
    got_down = shift_z(down_chunk, -1)
    mixed, *send = finish_rows(place, hidden, [mine, got_up, got_down], pick)

    by_z = [send[0]] + [shift_z(send[d], d) for d in range(1, N_Z)]
    block, mixed = join_columns(exchange_x(by_columns(by_z, mixed)), norm_gain.reshape(1, D))
    swapped = swap_l(block)
    below = shift_y(block, 1)
    above = shift_y(block, -1)
    below_two = shift_y(below, 1)
    below_swapped = swap_l(below)
    above_swapped = shift_y(swapped, -1)
    far = swap_l(below_two)
    parts = run_expert(
        [block, swapped, below, above, below_swapped, below_two, above_swapped, far],
        gate_proj[0].T,
        up_proj[0].T,
        down_proj[0],
    )

    result = scatter_ctx(parts)
    back_z = [result[:8]] + [shift_z(result[8 * d : 8 * d + 8], -d) for d in range(1, N_Z)]
    return (mixed, combine(weight, exchange_x(regroup(back_z))))


def solution(mesh):
    in_specs = (
        P(("rep", "ctx", "exp"), None),
        P(("rep", "ctx"), "exp"),
        P(("rep", "ctx"), None),
        P(("rep", "ctx"), None),
        P("exp", None),
        P(),
        P(("rep", "ctx", "exp"), None),
        P(("rep", "ctx", "exp"), None),
        P(("rep", "ctx", "exp")),
        P("exp", None, "ctx"),
        P("exp", None, "ctx"),
        P("exp", "ctx", None),
    )
    out_specs = (P(("rep", "ctx", "exp"), None), P(("rep", "ctx", "exp"), None))
    return jax.shard_map(
        on_device, mesh=mesh, in_specs=in_specs, out_specs=out_specs, check_vma=False
    )
```

```python
import functools
import math

import jax
import jax.numpy as jnp
from jax import lax
from jax.experimental import pallas as pl
from jax.experimental.pallas import tpu as pltpu
from jax.sharding import PartitionSpec as P

D = 4096
HEADS = 64
KV_HEADS = 4
HEAD_DIM = 128
TOPK = 8
CAP = 2
N_X = 4
N_Z = 4
N_Y = 4
TOKENS = 32
RIDER = 2 * (TOKENS + TOPK)
BF16 = jnp.bfloat16
F32 = jnp.float32
LOWEST = -1e30
EXP2_SCALE = HEAD_DIM ** (-0.5) * math.log2(math.e)
VMEM = pltpu.VMEM
SMEM = pltpu.SMEM


def params(limit_mib=8):
    return pltpu.CompilerParams(vmem_limit_bytes=limit_mib << 20)


def whole():
    return pl.BlockSpec(memory_space=VMEM)


def shift_x(a, d):
    pairs = [(z * N_X + x, z * N_X + (x + d) % N_X) for z in range(N_Z) for x in range(N_X)]
    return lax.ppermute(a, "exp", pairs)


def shift_z(a, d):
    pairs = [(z * N_X + x, (z + d) % N_Z * N_X + x) for z in range(N_Z) for x in range(N_X)]
    return lax.ppermute(a, "exp", pairs)


def shift_y(a, d):
    pairs = [(y * 2 + k, (y + d) % N_Y * 2 + k) for y in range(N_Y) for k in range(2)]
    return lax.ppermute(a, "ctx", pairs)


def swap_l(a):
    return lax.ppermute(a, "ctx", [(i, i ^ 1) for i in range(2 * N_Y)])


def swap_core(a):
    return lax.ppermute(a, "rep", [(0, 1), (1, 0)])


def pick_head(where_am, keys, values):
    rows = keys.shape[0]

    def kernel(where_ref, key_ref, value_ref, out_ref):
        out_ref[0:rows, :] = key_ref[...]
        out_ref[rows:, :] = value_ref[...]

    column = pl.BlockSpec((rows, HEAD_DIM), lambda i, w: (0, w[0]))
    return pl.pallas_call(
        kernel,
        grid_spec=pltpu.PrefetchScalarGridSpec(
            num_scalar_prefetch=1,
            grid=(1,),
            in_specs=[column, column],
            out_specs=pl.BlockSpec((2 * rows, HEAD_DIM), lambda i, w: (0, 0)),
        ),
        out_shape=jax.ShapeDtypeStruct((2 * rows, HEAD_DIM), BF16),
        compiler_params=params(),
        name="pick_head",
    )(where_am, keys, values)


def pick_weights(place, out_proj):
    rows, cols = out_proj.shape[0] // 2, out_proj.shape[1] // N_X

    def kernel(place_ref, *refs):
        for source, target in zip(refs[:3], refs[3:]):
            target[...] = source[...]

    def block(d):
        return pl.BlockSpec((rows, cols), lambda i, w: (w[0], lax.rem(w[1] + d, N_X)))

    return pl.pallas_call(
        kernel,
        grid_spec=pltpu.PrefetchScalarGridSpec(
            num_scalar_prefetch=1,
            grid=(1,),
            in_specs=[block(d) for d in range(1, N_X)],
            out_specs=[pl.BlockSpec((rows, cols), lambda i, w: (0, 0))] * 3,
        ),
        out_shape=[jax.ShapeDtypeStruct((rows, cols), BF16)] * 3,
        compiler_params=params(),
        name="pick_weights",
    )(place, out_proj, out_proj, out_proj)


def attend(queries, blocks, bias, state, riders=None):
    rows, heads = queries.shape[0], queries.shape[1] // HEAD_DIM
    calls = len(blocks)
    n = sum(b.shape[0] for b in blocks) // (2 * rows)
    first = state is None
    last = riders is not None
    tile = 128

    def kernel(*refs):
        bias_ref, q_ref = refs[0], refs[1]
        kv_refs = [
            r.at[first_row : first_row + 2 * rows]
            for r in refs[2 : 2 + calls]
            for first_row in range(0, r.shape[0], 2 * rows)
        ]
        rest = refs[2 + calls :]
        if not first:
            acc_in, top_in = rest[0], rest[1]
            rest = rest[2:]
        if last:
            rider_refs, rest = rest[:3], rest[3:]
            for rider, target in zip(rider_refs, rest):
                target[rows:, :] = rider[...]
        key = jnp.concatenate([r[0:rows, :] for r in kv_refs], axis=0)
        ones = jnp.ones((rows, HEAD_DIM), BF16)
        value = jnp.concatenate(
            [jnp.concatenate([r[rows:, :], ones], axis=1) for r in kv_refs], axis=0
        )
        for part in range(rows // tile):
            at = pl.ds(part * tile, tile)
            seen = n * rows
            scores = lax.dot_general(
                q_ref[at, :], key[:seen], (((1,), (1,)), ((), ())), preferred_element_type=F32
            )
            if first:
                i = lax.broadcasted_iota(jnp.int32, (tile, rows), 0) + part * tile
                j = lax.broadcasted_iota(jnp.int32, (tile, rows), 1)
                diagonal = jnp.where(j <= i, scores[:, :rows], LOWEST)
                scores = jnp.concatenate([diagonal, scores[:, rows:]], axis=1)
                newest = jnp.full((tile, HEAD_DIM), LOWEST, F32)
            else:
                before = top_in[0, at, :]
                newest = before
            for b in range(n):
                highest = jnp.max(scores[:, b * rows : (b + 1) * rows], axis=1, keepdims=True)
                newest = jnp.maximum(newest, highest + bias_ref[b])
            offsets = [(newest - bias_ref[b]) * EXP2_SCALE for b in range(n)]
            pieces = []
            for lane in range(0, seen, HEAD_DIM):
                pieces.append(
                    jnp.exp2(
                        scores[:, lane : lane + HEAD_DIM] * EXP2_SCALE - offsets[lane // rows]
                    ).astype(BF16)
                )
            total = jnp.dot(
                jnp.concatenate(pieces, axis=1), value[:seen], preferred_element_type=F32
            )
            if not first:
                factor = jnp.exp2((before - newest) * EXP2_SCALE)
                total = acc_in[0, at, :] * jnp.concatenate([factor, factor], axis=1) + total
            if last:
                done = (total[:, :HEAD_DIM] / total[:, HEAD_DIM:]).astype(BF16)
                for target in rest:
                    target[at, :] = done
            else:
                rest[0][0, at, :] = total
                rest[1][0, at, :] = newest

    q_spec = pl.BlockSpec((rows, HEAD_DIM), lambda h, f: (0, h))
    kv_specs = [pl.BlockSpec(b.shape, lambda h, f: (0, 0)) for b in blocks]
    rider_spec = pl.BlockSpec((RIDER, HEAD_DIM), lambda h, f: (0, h))
    message_spec = pl.BlockSpec((rows + RIDER, HEAD_DIM), lambda h, f: (0, h))
    state_specs = [
        pl.BlockSpec((1, rows, 2 * HEAD_DIM), lambda h, f: (h, 0, 0)),
        pl.BlockSpec((1, rows, HEAD_DIM), lambda h, f: (h, 0, 0)),
    ]
    state_shapes = [
        jax.ShapeDtypeStruct((heads, rows, 2 * HEAD_DIM), F32),
        jax.ShapeDtypeStruct((heads, rows, HEAD_DIM), F32),
    ]
    return pl.pallas_call(
        kernel,
        grid_spec=pltpu.PrefetchScalarGridSpec(
            num_scalar_prefetch=1,
            grid=(heads,),
            in_specs=[q_spec]
            + kv_specs
            + ([] if first else state_specs)
            + ([rider_spec] * 3 if last else []),
            out_specs=[message_spec] * 3 if last else state_specs,
        ),
        out_shape=[jax.ShapeDtypeStruct((rows + RIDER, queries.shape[1]), BF16)] * 3
        if last
        else state_shapes,
        compiler_params=params(20),
        cost_estimate=pl.CostEstimate(
            flops=heads * n * rows * rows * HEAD_DIM * 4,
            transcendentals=heads * n * rows * rows,
            bytes_accessed=4 << 20,
        ),
        name="attend",
    )(bias, queries, *blocks, *(() if first else state), *(riders if last else ()))


def rows_of(place_ref, left_ref, dz, columns):
    row = lax.rem(place_ref[0] + dz, N_Z) * (N_X * TOKENS)
    return left_ref[pl.ds(pl.multiple_of(row, N_X * TOKENS), N_X * TOKENS), columns]


def project_near(place, own, out_proj, lefts, fetched, other):
    n = len(lefts)
    cols = out_proj.shape[1] // N_X

    def kernel(place_ref, own_ref, weight_ref, *refs):
        left_refs, fetched_refs, other_ref, out_refs = refs[:n], refs[n : 2 * n], refs[2 * n], refs[2 * n + 1 :]
        for dz in range(N_Z):
            total = jnp.dot(
                rows_of(place_ref, own_ref, dz, slice(None)),
                weight_ref[...],
                preferred_element_type=F32,
            )
            for k in range(n):
                total = total + fetched_part(
                    place_ref, left_refs[k], fetched_refs[k], other_ref, (0, 2)[k], dz
                )
            out_refs[dz][...] = total

    fixed = lambda i, w: (0, 0)
    square = pl.BlockSpec(own.shape, fixed)
    return pl.pallas_call(
        kernel,
        grid_spec=pltpu.PrefetchScalarGridSpec(
            num_scalar_prefetch=1,
            grid=(1,),
            in_specs=[square, pl.BlockSpec((out_proj.shape[0], cols), lambda i, w: (0, w[1]))]
            + [square] * n
            + [pl.BlockSpec(fetched[0].shape, fixed)] * n
            + [pl.BlockSpec(other.shape, fixed)],
            out_specs=[pl.BlockSpec((N_X * TOKENS, cols), fixed)] * N_Z,
        ),
        out_shape=[jax.ShapeDtypeStruct((N_X * TOKENS, cols), F32)] * N_Z,
        compiler_params=params(28),
        name="project_near",
    )(place, own, out_proj, *lefts, *fetched, other)


def fetched_part(place_ref, left_ref, fetched_ref, other_ref, at, dz):
    half = fetched_ref.shape[0]
    core = place_ref[2]
    mine = pl.ds(pl.multiple_of(core * half, half), half)
    theirs = pl.ds(pl.multiple_of((1 - core) * half, half), half)
    return jnp.dot(
        rows_of(place_ref, left_ref, dz, mine), fetched_ref[...], preferred_element_type=F32
    ) + jnp.dot(
        rows_of(place_ref, left_ref, dz, theirs),
        other_ref[at * half : (at + 1) * half, :],
        preferred_element_type=F32,
    )


def project_far(place, near, left, fetched, other):
    shape = near[0].shape
    middle = shape[1] // 2

    def kernel(place_ref, left_ref, fetched_ref, other_ref, *refs):
        near_refs, out_refs = refs[:4], refs[4:]
        for dz in (2, 1, 3, 0):
            total = near_refs[dz][...] + fetched_part(
                place_ref, left_ref, fetched_ref, other_ref, 1, dz
            )
            total = total.astype(BF16)
            if dz == 2:
                out_refs[3][...] = total[:, :middle]
                out_refs[4][...] = total[:, middle:]
            else:
                out_refs[{0: 0, 1: 1, 3: 2}[dz]][...] = total

    return pl.pallas_call(
        kernel,
        in_specs=[pl.BlockSpec(memory_space=SMEM)] + [whole()] * 7,
        out_specs=[whole()] * 5,
        out_shape=[jax.ShapeDtypeStruct(shape, BF16)] * 3
        + [jax.ShapeDtypeStruct((shape[0], middle), BF16)] * 2,
        compiler_params=params(),
        name="project_far",
    )(place, left, fetched, other, *near)


def pick_hidden(place, live, hidden_in, ids):
    cols = D // N_X // 2

    def kernel(place_ref, live_ref, hidden_ref, id_ref, *out_refs):
        x = place_ref[1]
        t = lax.broadcasted_iota(jnp.int32, (TOPK, TOKENS), 1)
        alive = jnp.where(t < live_ref[0], id_ref[...] + 1, 0).astype(F32)
        lanes = (
            lax.broadcasted_iota(jnp.int32, (TOKENS, cols), 1)
            == lax.broadcasted_iota(jnp.int32, (TOKENS, cols), 0) + x * TOKENS
        ).astype(F32)
        alive = jnp.dot(alive, lanes, preferred_element_type=F32)
        for d in range(N_X):
            for side in range(2):
                column = pl.multiple_of(lax.rem(x + d, N_X) * (2 * cols) + side * cols, cols)
                top = side * (TOKENS + TOPK)
                out_refs[d][top : top + TOKENS, :] = hidden_ref[:, pl.ds(column, cols)]
                out_refs[d][top + TOKENS : top + TOKENS + TOPK, :] = (
                    alive if side == 0 else jnp.zeros_like(alive)
                ).astype(BF16)

    return pl.pallas_call(
        kernel,
        in_specs=[pl.BlockSpec(memory_space=SMEM)] * 2 + [whole()] * 2,
        out_specs=[whole()] * N_X,
        out_shape=[jax.ShapeDtypeStruct((RIDER, cols), BF16)] * N_X,
        compiler_params=params(),
        name="pick_hidden",
    )(place, live, hidden_in, ids)


def route(place, hidden):
    slots = N_Z * N_X * N_X * CAP
    tokens = N_X * TOKENS

    def kernel(place_ref, *refs):
        z = place_ref[0]
        s = lax.broadcasted_iota(jnp.int32, (slots, tokens), 0)
        t = lax.broadcasted_iota(jnp.int32, (slots, tokens), 1)
        dz, expert_x, owner, cap = s // 32, (s // 8) % 4, (s // 2) % 4, s % 2
        expert = ((z + dz) % N_Z) * N_X + expert_x
        wanted = jnp.where(owner == t // TOKENS, expert + 1, -1).astype(F32)
        ids = sum(
            r[r.shape[0] - RIDER + TOKENS : r.shape[0] - RIDER + TOKENS + TOPK, 0:tokens].astype(F32)
            for r in refs[:4]
        )
        present = jnp.zeros((slots, tokens), F32)
        for k in range(TOPK):
            present = present + (ids[k : k + 1, :] == wanted).astype(F32)
        earlier = (
            lax.broadcasted_iota(jnp.int32, (tokens, tokens), 0)
            < lax.broadcasted_iota(jnp.int32, (tokens, tokens), 1)
        ).astype(F32)
        rank = jnp.dot(present, earlier, preferred_element_type=F32)
        fits = jnp.abs(rank - cap.astype(F32)) < 0.5
        refs[4][...] = jnp.where(fits, present, 0.0).astype(BF16)

    return pl.pallas_call(
        kernel,
        in_specs=[pl.BlockSpec(memory_space=SMEM)] + [whole()] * 4,
        out_specs=whole(),
        out_shape=jax.ShapeDtypeStruct((slots, tokens), BF16),
        compiler_params=params(),
        name="route",
    )(place, *hidden)


def route_weights(place, ids, gates, live):
    slots = N_X * N_Z * CAP

    def kernel(place_ref, live_ref, id_ref, gate_ref, weight_ref):
        z = place_ref[0]
        s = lax.broadcasted_iota(jnp.int32, (slots, TOKENS), 0)
        t = lax.broadcasted_iota(jnp.int32, (slots, TOKENS), 1)
        expert_x, dz, cap = s // (N_Z * CAP), (s // CAP) % N_Z, s % CAP
        expert = ((z + dz) % N_Z) * N_X + expert_x
        present = jnp.zeros((slots, TOKENS), F32)
        weight = jnp.zeros((slots, TOKENS), F32)
        for k in range(TOPK):
            hit = ((id_ref[k : k + 1, :] == expert) & (t < live_ref[0])).astype(F32)
            present = present + hit
            weight = weight + hit * gate_ref[k : k + 1, :].astype(F32)
        earlier = (
            lax.broadcasted_iota(jnp.int32, (TOKENS, TOKENS), 0)
            < lax.broadcasted_iota(jnp.int32, (TOKENS, TOKENS), 1)
        ).astype(F32)
        rank = jnp.dot(present, earlier, preferred_element_type=F32)
        weight_ref[...] = jnp.where(jnp.abs(rank - cap.astype(F32)) < 0.5, weight, 0.0) / 4096.0

    return pl.pallas_call(
        kernel,
        in_specs=[pl.BlockSpec(memory_space=SMEM)] * 2 + [whole()] * 2,
        out_specs=whole(),
        out_shape=jax.ShapeDtypeStruct((slots, TOKENS), F32),
        compiler_params=params(),
        name="route_weights",
    )(place, live, ids, gates)


def finish_rows(place, hidden, sums, pick):
    cols = sums[0].shape[1]

    def kernel(place_ref, h0, h1, h2, h3, s0, s1, s2, pick_ref, *refs):
        mixed_ref, send_refs = refs[0], refs[1:5]
        for d, h in enumerate((h0, h1, h2, h3)):
            row = lax.rem(place_ref[1] + N_X - d, N_X) * TOKENS
            at = pl.ds(pl.multiple_of(row, TOKENS), TOKENS)
            top = h.shape[0] - RIDER
            rows = jnp.concatenate(
                [h[top : top + TOKENS, :], h[top + TOKENS + TOPK : top + 2 * TOKENS + TOPK, :]], axis=1
            )
            mixed_ref[at, :] = (
                rows.astype(F32)
                + (s0[at, :].astype(F32) + s1[at, :].astype(F32) + s2[at, :].astype(F32))
            ).astype(BF16)
        send = jnp.dot(pick_ref[...], mixed_ref[...], preferred_element_type=F32).astype(BF16)
        for dz in range(N_Z):
            send_refs[dz][...] = send[dz * 32 : dz * 32 + 32, :]

    return pl.pallas_call(
        kernel,
        in_specs=[pl.BlockSpec(memory_space=SMEM)] + [whole()] * 8,
        out_specs=[whole()] * 5,
        out_shape=[jax.ShapeDtypeStruct((N_X * TOKENS, cols), BF16)]
        + [jax.ShapeDtypeStruct((32, cols), BF16)] * 4,
        compiler_params=params(),
        name="finish_rows",
    )(place, *hidden, *sums, pick)


def by_columns(groups, mixed):
    cols = mixed.shape[1]

    def kernel(*refs):
        held = [r[...] for r in refs[:4]]
        for x in range(N_X):
            refs[5][x, 0:32, :] = jnp.concatenate([h[x * 8 : x * 8 + 8, :] for h in held], axis=0)
            refs[5][x, 32:64, :] = refs[4][x * TOKENS : (x + 1) * TOKENS, :]

    return pl.pallas_call(
        kernel,
        in_specs=[whole()] * 5,
        out_specs=whole(),
        out_shape=jax.ShapeDtypeStruct((N_X, 64, cols), BF16),
        compiler_params=params(),
        name="by_columns",
    )(*groups, mixed)


def join_columns(pieces, gain):
    cols = pieces.shape[2]

    def kernel(piece_ref, gain_ref, block_ref, mixed_ref):
        values = [piece_ref[x, 0:32, :].astype(F32) for x in range(N_X)]
        square = sum(jnp.sum(v * v, axis=1, keepdims=True) for v in values)
        scale = lax.rsqrt(square / D + 1e-06)
        for x, value in enumerate(values):
            column = slice(x * cols, (x + 1) * cols)
            block_ref[:, column] = (value * scale * gain_ref[:, column]).astype(BF16)
            mixed_ref[:, column] = piece_ref[x, 32:64, :]

    return pl.pallas_call(
        kernel,
        in_specs=[whole()] * 2,
        out_specs=[whole()] * 2,
        out_shape=[jax.ShapeDtypeStruct((32, D), BF16)] * 2,
        compiler_params=params(),
        name="join_columns",
    )(pieces, gain)


def regroup(groups):
    rows = 4 * 4 * CAP

    def kernel(*refs):
        held = jnp.concatenate([r[...] for r in refs[:4]], axis=0)
        to = lax.broadcasted_iota(jnp.int32, (rows, rows), 0)
        come = lax.broadcasted_iota(jnp.int32, (rows, rows), 1)
        b, a, cap = to // 8, (to // CAP) % 4, to % CAP
        order = (come == a * 8 + b * CAP + cap).astype(BF16)
        moved = jnp.dot(order, held, preferred_element_type=F32).astype(BF16)
        for i in range(4):
            refs[4][i] = moved[i * 8 : i * 8 + 8, :]

    return pl.pallas_call(
        kernel,
        in_specs=[whole()] * 4,
        out_specs=whole(),
        out_shape=jax.ShapeDtypeStruct((4, 8, D), BF16),
        compiler_params=params(),
        name="regroup",
    )(*groups)


def run_expert(blocks, gate, up, down):
    n = len(blocks)

    def kernel(*refs):
        in_refs, (gate_ref, up_ref, down_ref), out_refs = refs[:n], refs[n : n + 3], refs[n + 3 :]
        rows = jnp.concatenate([r[...] for r in in_refs], axis=0)
        last = (((1,), (1,)), ((), ()))
        gate_part = lax.dot_general(rows, gate_ref[...], last, preferred_element_type=F32)
        up_part = lax.dot_general(rows, up_ref[...], last, preferred_element_type=F32)
        hidden = (gate_part / (1.0 + jnp.exp(-gate_part)) * up_part).astype(BF16)
        result = jnp.dot(hidden, down_ref[...], preferred_element_type=F32).astype(BF16)
        at = 0
        for r in out_refs:
            r[...] = result[at : at + r.shape[0], :]
            at += r.shape[0]

    return pl.pallas_call(
        kernel,
        in_specs=[whole()] * (n + 3),
        out_specs=[whole()] * n,
        out_shape=[jax.ShapeDtypeStruct(b.shape, BF16) for b in blocks],
        compiler_params=params(24),
        name="run_expert",
    )(*blocks, gate, up, down)


def combine(weight, groups):
    def kernel(weight_ref, *refs):
        held = jnp.concatenate([refs[0][i] for i in range(4)], axis=0).astype(F32)
        refs[1][...] = lax.dot_general(
            weight_ref[...],
            held,
            (((0,), (0,)), ((), ())),
            precision=lax.Precision.HIGHEST,
            preferred_element_type=F32,
        ).astype(BF16)

    return pl.pallas_call(
        kernel,
        in_specs=[whole()] * 2,
        out_specs=whole(),
        out_shape=jax.ShapeDtypeStruct((TOKENS, D), BF16),
        compiler_params=params(),
        name="combine",
    )(weight, groups)


def tie(values, *others):
    n = len(values)
    return lax.optimization_barrier((*values, *others))[:n]


def add(*arrays):
    return sum(a.astype(F32) for a in arrays).astype(BF16)


def exchange_x(a):
    groups = [[z * N_X + x for x in range(N_X)] for z in range(N_Z)]
    return lax.all_to_all(a, "exp", 0, 0, tiled=True, axis_index_groups=groups)


def scatter_ctx(parts):
    own, swapped, below, above, below_swapped, below_two, above_swapped, far = parts
    got_far = swap_l(far)
    got_below_swapped = swap_l(below_swapped)
    got_above_swapped = shift_y(above_swapped, 1)
    got_two = shift_y(add(below_two, got_far), -1)
    got_above = shift_y(above, 1)
    got_swapped = swap_l(add(swapped, got_above_swapped))
    got_below = shift_y(add(below, got_two, got_below_swapped), -1)
    return add(own, got_above, got_below, got_swapped)


def on_device(
    hidden_in,
    queries,
    keys,
    values,
    out_proj,
    norm_gain,
    expert_ids,
    gate_fixed,
    live_counts,
    gate_proj,
    up_proj,
    down_proj,
):
    exp_index = lax.axis_index("exp")
    ctx_index = lax.axis_index("ctx")
    rep_index = lax.axis_index("rep")
    z, x = exp_index // N_X, exp_index % N_X
    y, side = ctx_index // 2, ctx_index % 2
    place = jnp.stack([z, x, rep_index]).astype(jnp.int32)
    seq_rows = queries.shape[0]
    local_heads = queries.shape[1] // HEAD_DIM
    kv_index = exp_index * local_heads // (HEADS // KV_HEADS)

    def bias(*steps):
        owners = jnp.stack([((y + dy) % N_Y) * 2 + (side ^ flip) for dy, flip in steps])
        return jnp.where(owners < ctx_index, 0.0, LOWEST).astype(F32)

    keys, values, out_proj = [
        pltpu.with_memory_space_constraint(a, pltpu.HBM) for a in (keys, values, out_proj)
    ]
    own = pick_head(kv_index.astype(jnp.int32)[None], keys, values)
    swapped = swap_l(own)
    away = pick_weights(jnp.stack([rep_index, x]).astype(jnp.int32), out_proj)
    fetched = [shift_x(away[d - 1], d) for d in range(1, N_X)]
    (swapped,) = tie((swapped,), *away)
    pair = jnp.concatenate([own, swapped], axis=0)
    below = shift_y(pair, 1)
    above = shift_y(pair, -1)
    state = attend(
        queries,
        [pair],
        jnp.concatenate([jnp.zeros((1,), F32), bias((0, 1))]),
        None,
    )
    riders = pick_hidden(place, live_counts, hidden_in, expert_ids.T)
    below, above = tie((below, above), *state, *riders)
    block = own.shape[0]
    far_a = shift_y(below[:block], 1)
    far_b = shift_y(above[block:], -1)
    state = attend(
        queries, [below, above], bias((-1, 0), (-1, 1), (1, 0), (1, 1)), state
    )
    far_a, far_b = tie((far_a, far_b), *state, *fetched)
    messages = attend(
        queries, [far_a, far_b], bias((-2, 0), (-2, 1)), state, riders[1:]
    )

    from_left = shift_x(messages[0], 1)
    from_right = shift_x(messages[2], 3)
    from_far = shift_x(messages[1], 2)
    weight = route_weights(
        tie((place,), from_left)[0], live=live_counts, ids=expert_ids.T, gates=gate_fixed.T
    )
    fetched = tie(fetched, from_left, from_right)
    other = swap_core(jnp.concatenate(fetched, axis=0))
    near = project_near(
        place, messages[0], out_proj, [from_left, from_right], [fetched[0], fetched[2]], other
    )
    from_far, *near = tie((from_far, *near))
    hidden = [riders[0], from_left, from_far, from_right]
    mine, up_chunk, down_chunk, low, high = project_far(place, near, from_far, fetched[1], other)

    middle = low.shape[1]
    got_low = shift_z(low, 1)
    got_high = shift_z(high, -1)
    pick = route(place, hidden)
    got_low, got_high = tie((got_low, got_high), pick)
    up_chunk = jnp.concatenate([add(up_chunk[:, :middle], got_low), up_chunk[:, middle:]], axis=1)
    down_chunk = jnp.concatenate(
        [down_chunk[:, :middle], add(down_chunk[:, middle:], got_high)], axis=1
    )
    got_up = shift_z(up_chunk, 1)
    got_down = shift_z(down_chunk, -1)
    mixed, *send = finish_rows(place, hidden, [mine, got_up, got_down], pick)

    by_z = [send[0]] + [shift_z(send[d], d) for d in range(1, N_Z)]
    block, mixed = join_columns(exchange_x(by_columns(by_z, mixed)), norm_gain.reshape(1, D))
    swapped = swap_l(block)
    below = shift_y(block, 1)
    above = shift_y(block, -1)
    below_two = shift_y(below, 1)
    below_swapped = swap_l(below)
    above_swapped = shift_y(swapped, -1)
    far = swap_l(below_two)
    parts = run_expert(
        [block, swapped, below, above, below_swapped, below_two, above_swapped, far],
        gate_proj[0].T,
        up_proj[0].T,
        down_proj[0],
    )

    result = scatter_ctx(parts)
    back_z = [result[:8]] + [shift_z(result[8 * d : 8 * d + 8], -d) for d in range(1, N_Z)]
    return (mixed, combine(weight, exchange_x(regroup(back_z))))


def solution(mesh):
    in_specs = (
        P(("rep", "ctx", "exp"), None),
        P(("rep", "ctx"), "exp"),
        P(("rep", "ctx"), None),
        P(("rep", "ctx"), None),
        P("exp", None),
        P(),
        P(("rep", "ctx", "exp"), None),
        P(("rep", "ctx", "exp"), None),
        P(("rep", "ctx", "exp")),
        P("exp", None, "ctx"),
        P("exp", None, "ctx"),
        P("exp", "ctx", None),
    )
    out_specs = (P(("rep", "ctx", "exp"), None), P(("rep", "ctx", "exp"), None))
    return jax.shard_map(
        on_device, mesh=mesh, in_specs=in_specs, out_specs=out_specs, check_vma=False
    )
```

```python
import functools
import math

import jax
import jax.numpy as jnp
from jax import lax
from jax.experimental import pallas as pl
from jax.experimental.pallas import tpu as pltpu
from jax.sharding import PartitionSpec as P

D = 4096
HEADS = 64
KV_HEADS = 4
HEAD_DIM = 128
TOPK = 8
CAP = 2
N_X = 4
N_Z = 4
N_Y = 4
TOKENS = 32
RIDER = 2 * (TOKENS + TOPK)
BF16 = jnp.bfloat16
F32 = jnp.float32
LOWEST = -1e30
EXP2_SCALE = HEAD_DIM ** (-0.5) * math.log2(math.e)
VMEM = pltpu.VMEM
SMEM = pltpu.SMEM


def params(limit_mib=8):
    return pltpu.CompilerParams(vmem_limit_bytes=limit_mib << 20)


def whole():
    return pl.BlockSpec(memory_space=VMEM)


def shift_x(a, d):
    pairs = [(z * N_X + x, z * N_X + (x + d) % N_X) for z in range(N_Z) for x in range(N_X)]
    return lax.ppermute(a, "exp", pairs)


def shift_z(a, d):
    pairs = [(z * N_X + x, (z + d) % N_Z * N_X + x) for z in range(N_Z) for x in range(N_X)]
    return lax.ppermute(a, "exp", pairs)


def shift_y(a, d):
    pairs = [(y * 2 + k, (y + d) % N_Y * 2 + k) for y in range(N_Y) for k in range(2)]
    return lax.ppermute(a, "ctx", pairs)


def swap_l(a):
    return lax.ppermute(a, "ctx", [(i, i ^ 1) for i in range(2 * N_Y)])


def swap_core(a):
    return lax.ppermute(a, "rep", [(0, 1), (1, 0)])


def pick_head(where_am, keys, values):
    rows = keys.shape[0]

    def kernel(where_ref, key_ref, value_ref, out_ref):
        out_ref[0:rows, :] = key_ref[...]
        out_ref[rows:, :] = value_ref[...]

    column = pl.BlockSpec((rows, HEAD_DIM), lambda i, w: (0, w[0]))
    return pl.pallas_call(
        kernel,
        grid_spec=pltpu.PrefetchScalarGridSpec(
            num_scalar_prefetch=1,
            grid=(1,),
            in_specs=[column, column],
            out_specs=pl.BlockSpec((2 * rows, HEAD_DIM), lambda i, w: (0, 0)),
        ),
        out_shape=jax.ShapeDtypeStruct((2 * rows, HEAD_DIM), BF16),
        compiler_params=params(),
        name="pick_head",
    )(where_am, keys, values)


def pick_weights(place, out_proj):
    rows, cols = out_proj.shape[0] // 2, out_proj.shape[1] // N_X

    def kernel(place_ref, *refs):
        for source, target in zip(refs[:3], refs[3:]):
            target[...] = source[...]

    def block(d):
        return pl.BlockSpec((rows, cols), lambda i, w: (w[0], lax.rem(w[1] + d, N_X)))

    return pl.pallas_call(
        kernel,
        grid_spec=pltpu.PrefetchScalarGridSpec(
            num_scalar_prefetch=1,
            grid=(1,),
            in_specs=[block(d) for d in range(1, N_X)],
            out_specs=[pl.BlockSpec((rows, cols), lambda i, w: (0, 0))] * 3,
        ),
        out_shape=[jax.ShapeDtypeStruct((rows, cols), BF16)] * 3,
        compiler_params=params(),
        name="pick_weights",
    )(place, out_proj, out_proj, out_proj)


def attend(queries, blocks, spot, steps, state, riders=None):
    rows, heads = queries.shape[0], queries.shape[1] // HEAD_DIM
    calls = len(blocks)
    n = sum(b.shape[0] for b in blocks) // (2 * rows)
    first = state is None
    last = riders is not None
    tile = 128

    def kernel(*refs):
        spot_ref, q_ref = refs[0], refs[1]
        bias = []
        for dy, flip in steps:
            side = 1 - spot_ref[1] if flip else spot_ref[1]
            owner = lax.rem(spot_ref[0] + N_Y + dy, N_Y) * 2 + side
            bias.append(jnp.where(owner <= spot_ref[2], 0.0, LOWEST).astype(F32))
        kv_refs = [
            r.at[first_row : first_row + 2 * rows]
            for r in refs[2 : 2 + calls]
            for first_row in range(0, r.shape[0], 2 * rows)
        ]
        rest, (key_ref, value_ref) = refs[2 + calls : -2], refs[-2:]
        if not first:
            acc_in, top_in = rest[0], rest[1]
            rest = rest[2:]
        if last:
            rider_refs, rest = rest[:3], rest[3:]
            for rider, target in zip(rider_refs, rest):
                target[rows:, :] = rider[...]
        for b, r in enumerate(kv_refs):
            at = slice(b * rows, (b + 1) * rows)
            key_ref[at, :] = r[0:rows, :]
            value_ref[at, 0:HEAD_DIM] = r[rows:, :]
        value_ref[:, HEAD_DIM:] = jnp.ones((n * rows, HEAD_DIM), BF16)

        def head(h, carry):
            lanes = pl.ds(pl.multiple_of(h * HEAD_DIM, HEAD_DIM), HEAD_DIM)

            def score(part):
                return lax.dot_general(
                    q_ref[pl.ds(part * tile, tile), lanes],
                    key_ref[...],
                    (((1,), (1,)), ((), ())),
                    preferred_element_type=F32,
                )

            upcoming = score(0)
            for part in range(rows // tile):
                at = pl.ds(part * tile, tile)
                scores = upcoming
                if (part + 1) * tile < rows:
                    upcoming = score(part + 1)
                if first:
                    i = lax.broadcasted_iota(jnp.int32, (tile, rows), 0) + part * tile
                    j = lax.broadcasted_iota(jnp.int32, (tile, rows), 1)
                    diagonal = jnp.where(j <= i, scores[:, :rows], LOWEST)
                    scores = jnp.concatenate([diagonal, scores[:, rows:]], axis=1)
                    newest = jnp.full((tile, HEAD_DIM), LOWEST, F32)
                else:
                    before = top_in[h, at, :]
                    newest = before
                for b in range(n):
                    highest = jnp.max(scores[:, b * rows : (b + 1) * rows], axis=1, keepdims=True)
                    newest = jnp.maximum(newest, highest + bias[b])
                offsets = [(newest - bias[b]) * EXP2_SCALE for b in range(n)]
                pieces = []
                for lane in range(0, n * rows, HEAD_DIM):
                    pieces.append(
                        jnp.exp2(
                            scores[:, lane : lane + HEAD_DIM] * EXP2_SCALE - offsets[lane // rows]
                        ).astype(BF16)
                    )
                total = jnp.dot(
                    jnp.concatenate(pieces, axis=1), value_ref[...], preferred_element_type=F32
                )
                if not first:
                    factor = jnp.exp2((before - newest) * EXP2_SCALE)
                    total = acc_in[h, at, :] * jnp.concatenate([factor, factor], axis=1) + total
                if last:
                    done = (total[:, :HEAD_DIM] / total[:, HEAD_DIM:]).astype(BF16)
                    for target in rest:
                        target[at, lanes] = done
                else:
                    rest[0][h, at, :] = total
                    rest[1][h, at, :] = newest
            return carry

        lax.fori_loop(0, heads, head, 0)

    state_shapes = [
        jax.ShapeDtypeStruct((heads, rows, 2 * HEAD_DIM), F32),
        jax.ShapeDtypeStruct((heads, rows, HEAD_DIM), F32),
    ]
    return pl.pallas_call(
        kernel,
        in_specs=[pl.BlockSpec(memory_space=SMEM)]
        + [whole()] * (1 + calls + (0 if first else 2) + (3 if last else 0)),
        out_specs=[whole()] * (3 if last else 2),
        out_shape=[jax.ShapeDtypeStruct((rows + RIDER, queries.shape[1]), BF16)] * 3
        if last
        else state_shapes,
        scratch_shapes=[VMEM((n * rows, HEAD_DIM), BF16), VMEM((n * rows, 2 * HEAD_DIM), BF16)],
        compiler_params=params(16),
        cost_estimate=pl.CostEstimate(
            flops=heads * n * rows * rows * HEAD_DIM * 4,
            transcendentals=heads * n * rows * rows,
            bytes_accessed=4 << 20,
        ),
        name="attend",
    )(spot, queries, *blocks, *(() if first else state), *(riders if last else ()))


def rows_of(place_ref, left_ref, dz, columns):
    row = lax.rem(place_ref[0] + dz, N_Z) * (N_X * TOKENS)
    return left_ref[pl.ds(pl.multiple_of(row, N_X * TOKENS), N_X * TOKENS), columns]


def project_near(place, own, out_proj, lefts, fetched, other):
    n = len(lefts)
    cols = out_proj.shape[1] // N_X

    def kernel(place_ref, own_ref, weight_ref, *refs):
        left_refs, fetched_refs, other_ref, out_refs = refs[:n], refs[n : 2 * n], refs[2 * n], refs[2 * n + 1 :]
        for dz in range(N_Z):
            total = jnp.dot(
                rows_of(place_ref, own_ref, dz, slice(None)),
                weight_ref[...],
                preferred_element_type=F32,
            )
            for k in range(n):
                total = total + fetched_part(
                    place_ref, left_refs[k], fetched_refs[k], other_ref, (0, 2)[k], dz
                )
            out_refs[dz][...] = total

    fixed = lambda i, w: (0, 0)
    square = pl.BlockSpec(own.shape, fixed)
    return pl.pallas_call(
        kernel,
        grid_spec=pltpu.PrefetchScalarGridSpec(
            num_scalar_prefetch=1,
            grid=(1,),
            in_specs=[square, pl.BlockSpec((out_proj.shape[0], cols), lambda i, w: (0, w[1]))]
            + [square] * n
            + [pl.BlockSpec(fetched[0].shape, fixed)] * n
            + [pl.BlockSpec(other.shape, fixed)],
            out_specs=[pl.BlockSpec((N_X * TOKENS, cols), fixed)] * N_Z,
        ),
        out_shape=[jax.ShapeDtypeStruct((N_X * TOKENS, cols), F32)] * N_Z,
        compiler_params=params(28),
        cost_estimate=pl.CostEstimate(flops=1, transcendentals=0, bytes_accessed=1),
        name="project_near",
    )(place, own, out_proj, *lefts, *fetched, other)


def fetched_part(place_ref, left_ref, fetched_ref, other_ref, at, dz):
    half = fetched_ref.shape[0]
    core = place_ref[2]
    mine = pl.ds(pl.multiple_of(core * half, half), half)
    theirs = pl.ds(pl.multiple_of((1 - core) * half, half), half)
    return jnp.dot(
        rows_of(place_ref, left_ref, dz, mine), fetched_ref[...], preferred_element_type=F32
    ) + jnp.dot(
        rows_of(place_ref, left_ref, dz, theirs),
        other_ref[at * half : (at + 1) * half, :],
        preferred_element_type=F32,
    )


def project_far(place, near, left, fetched, other):
    shape = near[0].shape
    middle = shape[1] // 2

    def kernel(place_ref, left_ref, fetched_ref, other_ref, *refs):
        near_refs, out_refs = refs[:4], refs[4:]
        for dz in (2, 1, 3, 0):
            total = near_refs[dz][...] + fetched_part(
                place_ref, left_ref, fetched_ref, other_ref, 1, dz
            )
            total = total.astype(BF16)
            if dz == 2:
                out_refs[3][...] = total[:, :middle]
                out_refs[4][...] = total[:, middle:]
            else:
                out_refs[{0: 0, 1: 1, 3: 2}[dz]][...] = total

    return pl.pallas_call(
        kernel,
        in_specs=[pl.BlockSpec(memory_space=SMEM)] + [whole()] * 7,
        out_specs=[whole()] * 5,
        out_shape=[jax.ShapeDtypeStruct(shape, BF16)] * 3
        + [jax.ShapeDtypeStruct((shape[0], middle), BF16)] * 2,
        compiler_params=params(),
        name="project_far",
    )(place, left, fetched, other, *near)


def pick_hidden(place, live, hidden_in, ids):
    cols = D // N_X // 2

    def kernel(place_ref, live_ref, hidden_ref, id_ref, *out_refs):
        x = place_ref[1]
        t = lax.broadcasted_iota(jnp.int32, (TOPK, TOKENS), 1)
        alive = jnp.where(t < live_ref[0], id_ref[...] + 1, 0).astype(F32)
        lanes = (
            lax.broadcasted_iota(jnp.int32, (TOKENS, cols), 1)
            == lax.broadcasted_iota(jnp.int32, (TOKENS, cols), 0) + x * TOKENS
        ).astype(F32)
        alive = jnp.dot(alive, lanes, preferred_element_type=F32)
        for d in range(N_X):
            for side in range(2):
                column = pl.multiple_of(lax.rem(x + d, N_X) * (2 * cols) + side * cols, cols)
                top = side * (TOKENS + TOPK)
                out_refs[d][top : top + TOKENS, :] = hidden_ref[:, pl.ds(column, cols)]
                out_refs[d][top + TOKENS : top + TOKENS + TOPK, :] = (
                    alive if side == 0 else jnp.zeros_like(alive)
                ).astype(BF16)

    return pl.pallas_call(
        kernel,
        in_specs=[pl.BlockSpec(memory_space=SMEM)] * 2 + [whole()] * 2,
        out_specs=[whole()] * N_X,
        out_shape=[jax.ShapeDtypeStruct((RIDER, cols), BF16)] * N_X,
        compiler_params=params(),
        name="pick_hidden",
    )(place, live, hidden_in, ids)


def route(place, hidden):
    slots = N_Z * N_X * N_X * CAP
    tokens = N_X * TOKENS

    def kernel(place_ref, *refs):
        z = place_ref[0]
        s = lax.broadcasted_iota(jnp.int32, (slots, tokens), 0)
        t = lax.broadcasted_iota(jnp.int32, (slots, tokens), 1)
        dz, expert_x, owner, cap = s // 32, (s // 8) % 4, (s // 2) % 4, s % 2
        expert = ((z + dz) % N_Z) * N_X + expert_x
        wanted = jnp.where(owner == t // TOKENS, expert + 1, -1).astype(F32)
        ids = sum(
            r[r.shape[0] - RIDER + TOKENS : r.shape[0] - RIDER + TOKENS + TOPK, 0:tokens].astype(F32)
            for r in refs[:4]
        )
        present = jnp.zeros((slots, tokens), F32)
        for k in range(TOPK):
            present = present + (ids[k : k + 1, :] == wanted).astype(F32)
        earlier = (
            lax.broadcasted_iota(jnp.int32, (tokens, tokens), 0)
            < lax.broadcasted_iota(jnp.int32, (tokens, tokens), 1)
        ).astype(F32)
        rank = jnp.dot(present, earlier, preferred_element_type=F32)
        fits = jnp.abs(rank - cap.astype(F32)) < 0.5
        refs[4][...] = jnp.where(fits, present, 0.0).astype(BF16)

    return pl.pallas_call(
        kernel,
        in_specs=[pl.BlockSpec(memory_space=SMEM)] + [whole()] * 4,
        out_specs=whole(),
        out_shape=jax.ShapeDtypeStruct((slots, tokens), BF16),
        compiler_params=params(),
        name="route",
    )(place, *hidden)


def route_weights(place, ids, gates, live):
    slots = N_X * N_Z * CAP

    def kernel(place_ref, live_ref, id_ref, gate_ref, weight_ref):
        z = place_ref[0]
        s = lax.broadcasted_iota(jnp.int32, (slots, TOKENS), 0)
        t = lax.broadcasted_iota(jnp.int32, (slots, TOKENS), 1)
        expert_x, dz, cap = s // (N_Z * CAP), (s // CAP) % N_Z, s % CAP
        expert = ((z + dz) % N_Z) * N_X + expert_x
        present = jnp.zeros((slots, TOKENS), F32)
        weight = jnp.zeros((slots, TOKENS), F32)
        for k in range(TOPK):
            hit = ((id_ref[k : k + 1, :] == expert) & (t < live_ref[0])).astype(F32)
            present = present + hit
            weight = weight + hit * gate_ref[k : k + 1, :].astype(F32)
        earlier = (
            lax.broadcasted_iota(jnp.int32, (TOKENS, TOKENS), 0)
            < lax.broadcasted_iota(jnp.int32, (TOKENS, TOKENS), 1)
        ).astype(F32)
        rank = jnp.dot(present, earlier, preferred_element_type=F32)
        weight_ref[...] = jnp.where(jnp.abs(rank - cap.astype(F32)) < 0.5, weight, 0.0) / 4096.0

    return pl.pallas_call(
        kernel,
        in_specs=[pl.BlockSpec(memory_space=SMEM)] * 2 + [whole()] * 2,
        out_specs=whole(),
        out_shape=jax.ShapeDtypeStruct((slots, TOKENS), F32),
        compiler_params=params(),
        name="route_weights",
    )(place, live, ids, gates)


def finish_rows(place, hidden, sums, pick):
    cols = sums[0].shape[1]

    def kernel(place_ref, h0, h1, h2, h3, s0, s1, s2, pick_ref, *refs):
        mixed_ref, send_refs = refs[0], refs[1:5]
        for d, h in enumerate((h0, h1, h2, h3)):
            row = lax.rem(place_ref[1] + N_X - d, N_X) * TOKENS
            at = pl.ds(pl.multiple_of(row, TOKENS), TOKENS)
            top = h.shape[0] - RIDER
            rows = jnp.concatenate(
                [h[top : top + TOKENS, :], h[top + TOKENS + TOPK : top + 2 * TOKENS + TOPK, :]], axis=1
            )
            mixed_ref[at, :] = (
                rows.astype(F32)
                + (s0[at, :].astype(F32) + s1[at, :].astype(F32) + s2[at, :].astype(F32))
            ).astype(BF16)
        send = jnp.dot(pick_ref[...], mixed_ref[...], preferred_element_type=F32).astype(BF16)
        for dz in range(N_Z):
            send_refs[dz][...] = send[dz * 32 : dz * 32 + 32, :]

    return pl.pallas_call(
        kernel,
        in_specs=[pl.BlockSpec(memory_space=SMEM)] + [whole()] * 8,
        out_specs=[whole()] * 5,
        out_shape=[jax.ShapeDtypeStruct((N_X * TOKENS, cols), BF16)]
        + [jax.ShapeDtypeStruct((32, cols), BF16)] * 4,
        compiler_params=params(),
        name="finish_rows",
    )(place, *hidden, *sums, pick)


def by_columns(groups, mixed):
    cols = mixed.shape[1]

    def kernel(*refs):
        held = [r[...] for r in refs[:4]]
        for x in range(N_X):
            refs[5][x, 0:32, :] = jnp.concatenate([h[x * 8 : x * 8 + 8, :] for h in held], axis=0)
            refs[5][x, 32:64, :] = refs[4][x * TOKENS : (x + 1) * TOKENS, :]

    return pl.pallas_call(
        kernel,
        in_specs=[whole()] * 5,
        out_specs=whole(),
        out_shape=jax.ShapeDtypeStruct((N_X, 64, cols), BF16),
        compiler_params=params(),
        name="by_columns",
    )(*groups, mixed)


def join_columns(pieces, gain):
    cols = pieces.shape[2]

    def kernel(piece_ref, gain_ref, block_ref, mixed_ref):
        values = [piece_ref[x, 0:32, :].astype(F32) for x in range(N_X)]
        square = sum(jnp.sum(v * v, axis=1, keepdims=True) for v in values)
        scale = lax.rsqrt(square / D + 1e-06)
        for x, value in enumerate(values):
            column = slice(x * cols, (x + 1) * cols)
            block_ref[:, column] = (value * scale * gain_ref[:, column]).astype(BF16)
            mixed_ref[:, column] = piece_ref[x, 32:64, :]

    return pl.pallas_call(
        kernel,
        in_specs=[whole()] * 2,
        out_specs=[whole()] * 2,
        out_shape=[jax.ShapeDtypeStruct((32, D), BF16)] * 2,
        compiler_params=params(),
        name="join_columns",
    )(pieces, gain)


def regroup(groups):
    rows = 4 * 4 * CAP

    def kernel(*refs):
        held = jnp.concatenate([r[...] for r in refs[:4]], axis=0)
        to = lax.broadcasted_iota(jnp.int32, (rows, rows), 0)
        come = lax.broadcasted_iota(jnp.int32, (rows, rows), 1)
        b, a, cap = to // 8, (to // CAP) % 4, to % CAP
        order = (come == a * 8 + b * CAP + cap).astype(BF16)
        moved = jnp.dot(order, held, preferred_element_type=F32).astype(BF16)
        for i in range(4):
            refs[4][i] = moved[i * 8 : i * 8 + 8, :]

    return pl.pallas_call(
        kernel,
        in_specs=[whole()] * 4,
        out_specs=whole(),
        out_shape=jax.ShapeDtypeStruct((4, 8, D), BF16),
        compiler_params=params(),
        name="regroup",
    )(*groups)


def run_expert(blocks, gate, up, down):
    n = len(blocks)

    def kernel(*refs):
        in_refs, (gate_ref, up_ref, down_ref), out_refs = refs[:n], refs[n : n + 3], refs[n + 3 :]
        rows = jnp.concatenate([r[...] for r in in_refs], axis=0)
        last = (((1,), (1,)), ((), ()))
        gate_part = lax.dot_general(rows, gate_ref[...], last, preferred_element_type=F32)
        up_part = lax.dot_general(rows, up_ref[...], last, preferred_element_type=F32)
        hidden = (gate_part / (1.0 + jnp.exp(-gate_part)) * up_part).astype(BF16)
        result = jnp.dot(hidden, down_ref[...], preferred_element_type=F32).astype(BF16)
        at = 0
        for r in out_refs:
            r[...] = result[at : at + r.shape[0], :]
            at += r.shape[0]

    return pl.pallas_call(
        kernel,
        in_specs=[whole()] * (n + 3),
        out_specs=[whole()] * n,
        out_shape=[jax.ShapeDtypeStruct(b.shape, BF16) for b in blocks],
        compiler_params=params(24),
        name="run_expert",
    )(*blocks, gate, up, down)


def combine(weight, groups):
    def kernel(weight_ref, *refs):
        held = jnp.concatenate([refs[0][i] for i in range(4)], axis=0).astype(F32)
        refs[1][...] = lax.dot_general(
            weight_ref[...],
            held,
            (((0,), (0,)), ((), ())),
            precision=lax.Precision.HIGHEST,
            preferred_element_type=F32,
        ).astype(BF16)

    return pl.pallas_call(
        kernel,
        in_specs=[whole()] * 2,
        out_specs=whole(),
        out_shape=jax.ShapeDtypeStruct((TOKENS, D), BF16),
        compiler_params=params(),
        name="combine",
    )(weight, groups)


def stack(arrays):
    rows = sum(a.shape[0] for a in arrays)

    def kernel(*refs):
        at = 0
        for r in refs[:-1]:
            refs[-1][at : at + r.shape[0], :] = r[...]
            at += r.shape[0]

    return pl.pallas_call(
        kernel,
        in_specs=[whole()] * len(arrays),
        out_specs=whole(),
        out_shape=jax.ShapeDtypeStruct((rows, arrays[0].shape[1]), BF16),
        compiler_params=params(4),
        name="stack",
    )(*arrays)


def tie(values, *others):
    n = len(values)
    return lax.optimization_barrier((*values, *others))[:n]


def add(*arrays):
    return sum(a.astype(F32) for a in arrays).astype(BF16)


def exchange_x(a):
    groups = [[z * N_X + x for x in range(N_X)] for z in range(N_Z)]
    return lax.all_to_all(a, "exp", 0, 0, tiled=True, axis_index_groups=groups)


def scatter_ctx(parts):
    own, swapped, below, above, below_swapped, below_two, above_swapped, far = parts
    got_far = swap_l(far)
    got_below_swapped = swap_l(below_swapped)
    got_above_swapped = shift_y(above_swapped, 1)
    got_two = shift_y(add(below_two, got_far), -1)
    got_above = shift_y(above, 1)
    got_swapped = swap_l(add(swapped, got_above_swapped))
    got_below = shift_y(add(below, got_two, got_below_swapped), -1)
    return add(own, got_above, got_below, got_swapped)


def on_device(
    hidden_in,
    queries,
    keys,
    values,
    out_proj,
    norm_gain,
    expert_ids,
    gate_fixed,
    live_counts,
    gate_proj,
    up_proj,
    down_proj,
):
    exp_index = lax.axis_index("exp")
    ctx_index = lax.axis_index("ctx")
    rep_index = lax.axis_index("rep")
    z, x = exp_index // N_X, exp_index % N_X
    y, side = ctx_index // 2, ctx_index % 2
    place = jnp.stack([z, x, rep_index]).astype(jnp.int32)
    seq_rows = queries.shape[0]
    local_heads = queries.shape[1] // HEAD_DIM
    kv_index = exp_index * local_heads // (HEADS // KV_HEADS)

    spot = jnp.stack([y, side, ctx_index]).astype(jnp.int32)

    keys, values, out_proj = [
        pltpu.with_memory_space_constraint(a, pltpu.HBM) for a in (keys, values, out_proj)
    ]
    own = pick_head(kv_index.astype(jnp.int32)[None], keys, values)
    swapped = swap_l(own)
    away = pick_weights(jnp.stack([rep_index, x]).astype(jnp.int32), out_proj)
    fetched = [shift_x(away[d - 1], d) for d in range(1, N_X)]
    (swapped,) = tie((swapped,), *away)
    pair = stack([own, swapped])
    below = shift_y(pair, 1)
    above = shift_y(pair, -1)
    state = attend(queries, [pair], spot, [(0, 0), (0, 1)], None)
    riders = pick_hidden(place, live_counts, hidden_in, expert_ids.T)
    below, above = tie((below, above), *state, *riders)
    block = own.shape[0]
    far_a = shift_y(below[:block], 1)
    far_b = shift_y(above[block:], -1)
    state = attend(
        queries, [below, above], spot, [(-1, 0), (-1, 1), (1, 0), (1, 1)], state
    )
    far_a, far_b, *fetched = tie((far_a, far_b, *fetched), *state)
    messages = attend(
        queries, [far_a, far_b], spot, [(-2, 0), (-2, 1)], state, riders[1:]
    )

    from_left = shift_x(messages[0], 1)
    from_right = shift_x(messages[2], 3)
    from_far = shift_x(messages[1], 2)
    weight = route_weights(
        tie((place,), from_left)[0], live=live_counts, ids=expert_ids.T, gates=gate_fixed.T
    )
    other = swap_core(stack(fetched))
    near = project_near(
        place, messages[0], out_proj, [from_left, from_right], [fetched[0], fetched[2]], other
    )
    from_far, *near = tie((from_far, *near))
    hidden = [riders[0], from_left, from_far, from_right]
    mine, up_chunk, down_chunk, low, high = project_far(place, near, from_far, fetched[1], other)

    middle = low.shape[1]
    got_low = shift_z(low, 1)
    got_high = shift_z(high, -1)
    pick = route(place, hidden)
    got_low, got_high = tie((got_low, got_high), pick)
    up_chunk = jnp.concatenate([add(up_chunk[:, :middle], got_low), up_chunk[:, middle:]], axis=1)
    down_chunk = jnp.concatenate(
        [down_chunk[:, :middle], add(down_chunk[:, middle:], got_high)], axis=1
    )
    got_up = shift_z(up_chunk, 1)
    got_down = shift_z(down_chunk, -1)
    mixed, *send = finish_rows(place, hidden, [mine, got_up, got_down], pick)

    by_z = [send[0]] + [shift_z(send[d], d) for d in range(1, N_Z)]
    block, mixed = join_columns(exchange_x(by_columns(by_z, mixed)), norm_gain.reshape(1, D))
    swapped = swap_l(block)
    below = shift_y(block, 1)
    above = shift_y(block, -1)
    below_two = shift_y(below, 1)
    below_swapped = swap_l(below)
    above_swapped = shift_y(swapped, -1)
    far = swap_l(below_two)
    parts = run_expert(
        [block, swapped, below, above, below_swapped, below_two, above_swapped, far],
        gate_proj[0].T,
        up_proj[0].T,
        down_proj[0],
    )

    result = scatter_ctx(parts)
    back_z = [result[:8]] + [shift_z(result[8 * d : 8 * d + 8], -d) for d in range(1, N_Z)]
    return (mixed, combine(weight, exchange_x(regroup(back_z))))


def solution(mesh):
    in_specs = (
        P(("rep", "ctx", "exp"), None),
        P(("rep", "ctx"), "exp"),
        P(("rep", "ctx"), None),
        P(("rep", "ctx"), None),
        P("exp", None),
        P(),
        P(("rep", "ctx", "exp"), None),
        P(("rep", "ctx", "exp"), None),
        P(("rep", "ctx", "exp")),
        P("exp", None, "ctx"),
        P("exp", None, "ctx"),
        P("exp", "ctx", None),
    )
    out_specs = (P(("rep", "ctx", "exp"), None), P(("rep", "ctx", "exp"), None))
    return jax.shard_map(
        on_device, mesh=mesh, in_specs=in_specs, out_specs=out_specs, check_vma=False
    )
```

```python
import functools
import math

import jax
import jax.numpy as jnp
from jax import lax
from jax.experimental import pallas as pl
from jax.experimental.pallas import tpu as pltpu
from jax.sharding import PartitionSpec as P

D = 4096
HEADS = 64
KV_HEADS = 4
HEAD_DIM = 128
TOPK = 8
CAP = 2
N_X = 4
N_Z = 4
N_Y = 4
TOKENS = 32
RIDER = 2 * (TOKENS + TOPK)
BF16 = jnp.bfloat16
F32 = jnp.float32
LOWEST = -1e30
EXP2_SCALE = HEAD_DIM ** (-0.5) * math.log2(math.e)
VMEM = pltpu.VMEM
SMEM = pltpu.SMEM


def params(limit_mib=8):
    return pltpu.CompilerParams(vmem_limit_bytes=limit_mib << 20)


def whole():
    return pl.BlockSpec(memory_space=VMEM)


def shift_x(a, d):
    pairs = [(z * N_X + x, z * N_X + (x + d) % N_X) for z in range(N_Z) for x in range(N_X)]
    return lax.ppermute(a, "exp", pairs)


def shift_z(a, d):
    pairs = [(z * N_X + x, (z + d) % N_Z * N_X + x) for z in range(N_Z) for x in range(N_X)]
    return lax.ppermute(a, "exp", pairs)


def shift_y(a, d):
    pairs = [(y * 2 + k, (y + d) % N_Y * 2 + k) for y in range(N_Y) for k in range(2)]
    return lax.ppermute(a, "ctx", pairs)


def swap_l(a):
    return lax.ppermute(a, "ctx", [(i, i ^ 1) for i in range(2 * N_Y)])


def swap_core(a):
    return lax.ppermute(a, "rep", [(0, 1), (1, 0)])


def pick_head(where_am, keys, values):
    rows = keys.shape[0]

    def kernel(where_ref, key_ref, value_ref, out_ref):
        out_ref[0:rows, :] = key_ref[...]
        out_ref[rows:, :] = value_ref[...]

    column = pl.BlockSpec((rows, HEAD_DIM), lambda i, w: (0, w[0]))
    return pl.pallas_call(
        kernel,
        grid_spec=pltpu.PrefetchScalarGridSpec(
            num_scalar_prefetch=1,
            grid=(1,),
            in_specs=[column, column],
            out_specs=pl.BlockSpec((2 * rows, HEAD_DIM), lambda i, w: (0, 0)),
        ),
        out_shape=jax.ShapeDtypeStruct((2 * rows, HEAD_DIM), BF16),
        compiler_params=params(),
        name="pick_head",
    )(where_am, keys, values)


def pick_weights(place, out_proj):
    rows, cols = out_proj.shape[0] // 2, out_proj.shape[1] // N_X

    def kernel(place_ref, *refs):
        for source, target in zip(refs[:3], refs[3:]):
            target[...] = source[...]

    def block(d):
        return pl.BlockSpec((rows, cols), lambda i, w: (w[0], lax.rem(w[1] + d, N_X)))

    return pl.pallas_call(
        kernel,
        grid_spec=pltpu.PrefetchScalarGridSpec(
            num_scalar_prefetch=1,
            grid=(1,),
            in_specs=[block(d) for d in range(1, N_X)],
            out_specs=[pl.BlockSpec((rows, cols), lambda i, w: (0, 0))] * 3,
        ),
        out_shape=[jax.ShapeDtypeStruct((rows, cols), BF16)] * 3,
        compiler_params=params(),
        name="pick_weights",
    )(place, out_proj, out_proj, out_proj)


def attend(queries, blocks, spot, steps, state, riders=None):
    rows, heads = queries.shape[0], queries.shape[1] // HEAD_DIM
    calls = len(blocks)
    n = sum(b.shape[0] for b in blocks) // (2 * rows)
    first = state is None
    last = riders is not None
    passengers = [r for group in riders for r in group] if last else []
    tile = 128

    def kernel(*refs):
        spot_ref, q_ref = refs[0], refs[1]
        bias = []
        for dy, flip in steps:
            side = 1 - spot_ref[1] if flip else spot_ref[1]
            owner = lax.rem(spot_ref[0] + N_Y + dy, N_Y) * 2 + side
            bias.append(jnp.where(owner <= spot_ref[2], 0.0, LOWEST).astype(F32))
        kv_refs = [
            r.at[first_row : first_row + 2 * rows]
            for r in refs[2 : 2 + calls]
            for first_row in range(0, r.shape[0], 2 * rows)
        ]
        rest, (key_ref, value_ref) = refs[2 + calls : -2], refs[-2:]
        if not first:
            acc_in, top_in = rest[0], rest[1]
            rest = rest[2:]
        if last:
            rider_refs, rest = list(rest[: len(passengers)]), rest[len(passengers) :]
            for group, target in zip(riders, rest):
                for at in range(rows, rows + RIDER * len(group), RIDER):
                    target[at : at + RIDER, :] = rider_refs.pop(0)[...]
        for b, r in enumerate(kv_refs):
            at = slice(b * rows, (b + 1) * rows)
            key_ref[at, :] = r[0:rows, :]
            value_ref[at, 0:HEAD_DIM] = r[rows:, :]
        value_ref[:, HEAD_DIM:] = jnp.ones((n * rows, HEAD_DIM), BF16)

        def head(h, carry):
            lanes = pl.ds(pl.multiple_of(h * HEAD_DIM, HEAD_DIM), HEAD_DIM)

            def score(part):
                return lax.dot_general(
                    q_ref[pl.ds(part * tile, tile), lanes],
                    key_ref[...],
                    (((1,), (1,)), ((), ())),
                    preferred_element_type=F32,
                )

            upcoming = score(0)
            for part in range(rows // tile):
                at = pl.ds(part * tile, tile)
                scores = upcoming
                if (part + 1) * tile < rows:
                    upcoming = score(part + 1)
                if first:
                    i = lax.broadcasted_iota(jnp.int32, (tile, rows), 0) + part * tile
                    j = lax.broadcasted_iota(jnp.int32, (tile, rows), 1)
                    diagonal = jnp.where(j <= i, scores[:, :rows], LOWEST)
                    scores = jnp.concatenate([diagonal, scores[:, rows:]], axis=1)
                    newest = jnp.full((tile, HEAD_DIM), LOWEST, F32)
                else:
                    before = top_in[h, at, :]
                    newest = before
                for b in range(n):
                    highest = jnp.max(scores[:, b * rows : (b + 1) * rows], axis=1, keepdims=True)
                    newest = jnp.maximum(newest, highest + bias[b])
                offsets = [(newest - bias[b]) * EXP2_SCALE for b in range(n)]
                pieces = []
                for lane in range(0, n * rows, HEAD_DIM):
                    pieces.append(
                        jnp.exp2(
                            scores[:, lane : lane + HEAD_DIM] * EXP2_SCALE - offsets[lane // rows]
                        ).astype(BF16)
                    )
                total = jnp.dot(
                    jnp.concatenate(pieces, axis=1), value_ref[...], preferred_element_type=F32
                )
                if not first:
                    factor = jnp.exp2((before - newest) * EXP2_SCALE)
                    total = acc_in[h, at, :] * jnp.concatenate([factor, factor], axis=1) + total
                if last:
                    done = (total[:, :HEAD_DIM] / total[:, HEAD_DIM:]).astype(BF16)
                    for target in rest:
                        target[at, lanes] = done
                else:
                    rest[0][h, at, :] = total
                    rest[1][h, at, :] = newest
            return carry

        lax.fori_loop(0, heads, head, 0)

    state_shapes = [
        jax.ShapeDtypeStruct((heads, rows, 2 * HEAD_DIM), F32),
        jax.ShapeDtypeStruct((heads, rows, HEAD_DIM), F32),
    ]
    return pl.pallas_call(
        kernel,
        in_specs=[pl.BlockSpec(memory_space=SMEM)]
        + [whole()] * (1 + calls + (0 if first else 2) + len(passengers)),
        out_specs=[whole()] * 2,
        out_shape=[
            jax.ShapeDtypeStruct((rows + RIDER * len(group), queries.shape[1]), BF16)
            for group in riders
        ]
        if last
        else state_shapes,
        scratch_shapes=[VMEM((n * rows, HEAD_DIM), BF16), VMEM((n * rows, 2 * HEAD_DIM), BF16)],
        compiler_params=params(16),
        cost_estimate=pl.CostEstimate(
            flops=heads * n * rows * rows * HEAD_DIM * 4,
            transcendentals=heads * n * rows * rows,
            bytes_accessed=4 << 20,
        ),
        name="attend",
    )(spot, queries, *blocks, *(() if first else state), *passengers)


def rows_of(place_ref, left_ref, dz, columns):
    row = lax.rem(place_ref[0] + dz, N_Z) * (N_X * TOKENS)
    return left_ref[pl.ds(pl.multiple_of(row, N_X * TOKENS), N_X * TOKENS), columns]


def project_near(place, own, out_proj, lefts, fetched, other):
    n = len(lefts)
    cols = out_proj.shape[1] // N_X

    def kernel(place_ref, own_ref, weight_ref, *refs):
        left_refs, fetched_refs, other_ref, out_ref = refs[:n], refs[n : 2 * n], refs[2 * n], refs[-1]

        def chunk(dz, carry):
            total = jnp.dot(
                rows_of(place_ref, own_ref, dz, slice(None)),
                weight_ref[...],
                preferred_element_type=F32,
            )
            for k in range(n):
                total = total + fetched_part(
                    place_ref, left_refs[k], fetched_refs[k], other_ref, (0, 2)[k], dz
                )
            out_ref[dz] = total
            return carry

        lax.fori_loop(0, N_Z, chunk, 0)

    fixed = lambda i, w: (0, 0)
    square = pl.BlockSpec(own.shape, fixed)
    return pl.pallas_call(
        kernel,
        grid_spec=pltpu.PrefetchScalarGridSpec(
            num_scalar_prefetch=1,
            grid=(1,),
            in_specs=[square, pl.BlockSpec((out_proj.shape[0], cols), lambda i, w: (0, w[1]))]
            + [pl.BlockSpec(left.shape, fixed) for left in lefts]
            + [pl.BlockSpec(fetched[0].shape, fixed)] * n
            + [pl.BlockSpec(other.shape, fixed)],
            out_specs=pl.BlockSpec((N_Z, N_X * TOKENS, cols), lambda i, w: (0, 0, 0)),
        ),
        out_shape=jax.ShapeDtypeStruct((N_Z, N_X * TOKENS, cols), F32),
        compiler_params=params(28),
        cost_estimate=pl.CostEstimate(flops=1, transcendentals=0, bytes_accessed=1),
        name="project_near",
    )(place, own, out_proj, *lefts, *fetched, other)


def fetched_part(place_ref, left_ref, fetched_ref, other_ref, at, dz):
    half = fetched_ref.shape[0]
    core = place_ref[2]
    mine = pl.ds(pl.multiple_of(core * half, half), half)
    theirs = pl.ds(pl.multiple_of((1 - core) * half, half), half)
    return jnp.dot(
        rows_of(place_ref, left_ref, dz, mine), fetched_ref[...], preferred_element_type=F32
    ) + jnp.dot(
        rows_of(place_ref, left_ref, dz, theirs),
        other_ref[at * half : (at + 1) * half, :],
        preferred_element_type=F32,
    )


def forward(message, first, rows, riders):
    attended = message.shape[0] // 512 * 512

    def kernel(message_ref, out_ref):
        out_ref[0:rows, :] = message_ref[first : first + rows, :]
        if riders:
            out_ref[rows:, :] = message_ref[attended : attended + riders, :]

    return pl.pallas_call(
        kernel,
        in_specs=[whole()],
        out_specs=whole(),
        out_shape=jax.ShapeDtypeStruct((rows + riders, message.shape[1]), BF16),
        compiler_params=params(4),
        name="forward",
    )(message)


def project_far(place, near, lefts, fetched, other):
    shape = near.shape[1:]
    middle = shape[1] // 2

    def kernel(place_ref, upper_ref, lower_ref, fetched_ref, other_ref, *refs):
        near_ref, out_refs, left_ref = refs[0], refs[1:-1], refs[-1]
        half = left_ref.shape[0] // 2
        left_ref[:half, :] = upper_ref[:half, :]
        left_ref[half:, :] = lower_ref[...]
        for dz in (2, 1, 3, 0):
            total = near_ref[dz] + fetched_part(
                place_ref, left_ref, fetched_ref, other_ref, 1, dz
            )
            total = total.astype(BF16)
            if dz == 2:
                out_refs[3][...] = total[:, :middle]
                out_refs[4][...] = total[:, middle:]
            else:
                out_refs[{0: 0, 1: 1, 3: 2}[dz]][...] = total

    return pl.pallas_call(
        kernel,
        in_specs=[pl.BlockSpec(memory_space=SMEM)] + [whole()] * 5,
        out_specs=[whole()] * 5,
        scratch_shapes=[VMEM((2 * lefts[1].shape[0], lefts[1].shape[1]), BF16)],
        out_shape=[jax.ShapeDtypeStruct(shape, BF16)] * 3
        + [jax.ShapeDtypeStruct((shape[0], middle), BF16)] * 2,
        compiler_params=params(),
        name="project_far",
    )(place, *lefts, fetched, other, near)


def pick_hidden(place, live, hidden_in, ids):
    cols = D // N_X // 2

    def kernel(place_ref, live_ref, hidden_ref, id_ref, *out_refs):
        x = place_ref[1]
        t = lax.broadcasted_iota(jnp.int32, (TOPK, TOKENS), 1)
        alive = jnp.where(t < live_ref[0], id_ref[...] + 1, 0).astype(F32)
        lanes = (
            lax.broadcasted_iota(jnp.int32, (TOKENS, cols), 1)
            == lax.broadcasted_iota(jnp.int32, (TOKENS, cols), 0) + x * TOKENS
        ).astype(F32)
        alive = jnp.dot(alive, lanes, preferred_element_type=F32)
        for d in range(N_X):
            for side in range(2):
                column = pl.multiple_of(lax.rem(x + d, N_X) * (2 * cols) + side * cols, cols)
                top = side * (TOKENS + TOPK)
                out_refs[d][top : top + TOKENS, :] = hidden_ref[:, pl.ds(column, cols)]
                out_refs[d][top + TOKENS : top + TOKENS + TOPK, :] = (
                    alive if side == 0 else jnp.zeros_like(alive)
                ).astype(BF16)

    return pl.pallas_call(
        kernel,
        in_specs=[pl.BlockSpec(memory_space=SMEM)] * 2 + [whole()] * 2,
        out_specs=[whole()] * N_X,
        out_shape=[jax.ShapeDtypeStruct((RIDER, cols), BF16)] * N_X,
        compiler_params=params(),
        name="pick_hidden",
    )(place, live, hidden_in, ids)


def route(place, hidden):
    slots = N_Z * N_X * N_X * CAP
    tokens = N_X * TOKENS

    def kernel(place_ref, *refs):
        z = place_ref[0]
        s = lax.broadcasted_iota(jnp.int32, (slots, tokens), 0)
        t = lax.broadcasted_iota(jnp.int32, (slots, tokens), 1)
        dz, expert_x, owner, cap = s // 32, (s // 8) % 4, (s // 2) % 4, s % 2
        expert = ((z + dz) % N_Z) * N_X + expert_x
        wanted = jnp.where(owner == t // TOKENS, expert + 1, -1).astype(F32)
        ids = sum(
            r[r.shape[0] - RIDER + TOKENS : r.shape[0] - RIDER + TOKENS + TOPK, 0:tokens].astype(F32)
            for r in refs[:4]
        )
        present = jnp.zeros((slots, tokens), F32)
        for k in range(TOPK):
            present = present + (ids[k : k + 1, :] == wanted).astype(F32)
        earlier = (
            lax.broadcasted_iota(jnp.int32, (tokens, tokens), 0)
            < lax.broadcasted_iota(jnp.int32, (tokens, tokens), 1)
        ).astype(F32)
        rank = jnp.dot(present, earlier, preferred_element_type=F32)
        fits = jnp.abs(rank - cap.astype(F32)) < 0.5
        refs[4][...] = jnp.where(fits, present, 0.0).astype(BF16)

    return pl.pallas_call(
        kernel,
        in_specs=[pl.BlockSpec(memory_space=SMEM)] + [whole()] * 4,
        out_specs=whole(),
        out_shape=jax.ShapeDtypeStruct((slots, tokens), BF16),
        compiler_params=params(),
        name="route",
    )(place, *hidden)


def route_weights(place, ids, gates, live):
    slots = N_X * N_Z * CAP

    def kernel(place_ref, live_ref, id_ref, gate_ref, weight_ref):
        z = place_ref[0]
        s = lax.broadcasted_iota(jnp.int32, (slots, TOKENS), 0)
        t = lax.broadcasted_iota(jnp.int32, (slots, TOKENS), 1)
        expert_x, dz, cap = s // (N_Z * CAP), (s // CAP) % N_Z, s % CAP
        expert = ((z + dz) % N_Z) * N_X + expert_x
        present = jnp.zeros((slots, TOKENS), F32)
        weight = jnp.zeros((slots, TOKENS), F32)
        for k in range(TOPK):
            hit = ((id_ref[k : k + 1, :] == expert) & (t < live_ref[0])).astype(F32)
            present = present + hit
            weight = weight + hit * gate_ref[k : k + 1, :].astype(F32)
        earlier = (
            lax.broadcasted_iota(jnp.int32, (TOKENS, TOKENS), 0)
            < lax.broadcasted_iota(jnp.int32, (TOKENS, TOKENS), 1)
        ).astype(F32)
        rank = jnp.dot(present, earlier, preferred_element_type=F32)
        weight_ref[...] = jnp.where(jnp.abs(rank - cap.astype(F32)) < 0.5, weight, 0.0) / 4096.0

    return pl.pallas_call(
        kernel,
        in_specs=[pl.BlockSpec(memory_space=SMEM)] * 2 + [whole()] * 2,
        out_specs=whole(),
        out_shape=jax.ShapeDtypeStruct((slots, TOKENS), F32),
        compiler_params=params(),
        name="route_weights",
    )(place, live, ids, gates)


def finish_rows(place, hidden, sums, pick):
    cols = sums[0].shape[1]

    def kernel(place_ref, h0, h1, h2, h3, s0, s1, s2, pick_ref, *refs):
        mixed_ref, send_refs = refs[0], refs[1:5]
        for d, h in enumerate((h0, h1, h2, h3)):
            row = lax.rem(place_ref[1] + N_X - d, N_X) * TOKENS
            at = pl.ds(pl.multiple_of(row, TOKENS), TOKENS)
            top = h.shape[0] - RIDER
            rows = jnp.concatenate(
                [h[top : top + TOKENS, :], h[top + TOKENS + TOPK : top + 2 * TOKENS + TOPK, :]], axis=1
            )
            mixed_ref[at, :] = (
                rows.astype(F32)
                + (s0[at, :].astype(F32) + s1[at, :].astype(F32) + s2[at, :].astype(F32))
            ).astype(BF16)
        send = jnp.dot(pick_ref[...], mixed_ref[...], preferred_element_type=F32).astype(BF16)
        for dz in range(N_Z):
            send_refs[dz][...] = send[dz * 32 : dz * 32 + 32, :]

    return pl.pallas_call(
        kernel,
        in_specs=[pl.BlockSpec(memory_space=SMEM)] + [whole()] * 8,
        out_specs=[whole()] * 5,
        out_shape=[jax.ShapeDtypeStruct((N_X * TOKENS, cols), BF16)]
        + [jax.ShapeDtypeStruct((32, cols), BF16)] * 4,
        compiler_params=params(),
        name="finish_rows",
    )(place, *hidden, *sums, pick)


def by_columns(groups, mixed):
    cols = mixed.shape[1]

    def kernel(*refs):
        held = [r[...] for r in refs[:4]]
        for x in range(N_X):
            refs[5][x, 0:32, :] = jnp.concatenate([h[x * 8 : x * 8 + 8, :] for h in held], axis=0)
            refs[5][x, 32:64, :] = refs[4][x * TOKENS : (x + 1) * TOKENS, :]

    return pl.pallas_call(
        kernel,
        in_specs=[whole()] * 5,
        out_specs=whole(),
        out_shape=jax.ShapeDtypeStruct((N_X, 64, cols), BF16),
        compiler_params=params(),
        name="by_columns",
    )(*groups, mixed)


def join_columns(pieces, gain):
    cols = pieces.shape[2]

    def kernel(piece_ref, gain_ref, block_ref, mixed_ref):
        values = [piece_ref[x, 0:32, :].astype(F32) for x in range(N_X)]
        square = sum(jnp.sum(v * v, axis=1, keepdims=True) for v in values)
        scale = lax.rsqrt(square / D + 1e-06)
        for x, value in enumerate(values):
            column = slice(x * cols, (x + 1) * cols)
            block_ref[:, column] = (value * scale * gain_ref[:, column]).astype(BF16)
            mixed_ref[:, column] = piece_ref[x, 32:64, :]

    return pl.pallas_call(
        kernel,
        in_specs=[whole()] * 2,
        out_specs=[whole()] * 2,
        out_shape=[jax.ShapeDtypeStruct((32, D), BF16)] * 2,
        compiler_params=params(),
        name="join_columns",
    )(pieces, gain)


def regroup(groups):
    rows = 4 * 4 * CAP

    def kernel(*refs):
        held = jnp.concatenate([r[...] for r in refs[:4]], axis=0)
        to = lax.broadcasted_iota(jnp.int32, (rows, rows), 0)
        come = lax.broadcasted_iota(jnp.int32, (rows, rows), 1)
        b, a, cap = to // 8, (to // CAP) % 4, to % CAP
        order = (come == a * 8 + b * CAP + cap).astype(BF16)
        moved = jnp.dot(order, held, preferred_element_type=F32).astype(BF16)
        for i in range(4):
            refs[4][i] = moved[i * 8 : i * 8 + 8, :]

    return pl.pallas_call(
        kernel,
        in_specs=[whole()] * 4,
        out_specs=whole(),
        out_shape=jax.ShapeDtypeStruct((4, 8, D), BF16),
        compiler_params=params(),
        name="regroup",
    )(*groups)


def run_expert(blocks, gate, up, down):
    n = len(blocks)

    def kernel(*refs):
        in_refs, (gate_ref, up_ref, down_ref), out_refs = refs[:n], refs[n : n + 3], refs[n + 3 :]
        rows = jnp.concatenate([r[...] for r in in_refs], axis=0)
        last = (((1,), (1,)), ((), ()))
        gate_part = lax.dot_general(rows, gate_ref[...], last, preferred_element_type=F32)
        up_part = lax.dot_general(rows, up_ref[...], last, preferred_element_type=F32)
        hidden = (gate_part / (1.0 + jnp.exp(-gate_part)) * up_part).astype(BF16)
        result = jnp.dot(hidden, down_ref[...], preferred_element_type=F32).astype(BF16)
        at = 0
        for r in out_refs:
            r[...] = result[at : at + r.shape[0], :]
            at += r.shape[0]

    return pl.pallas_call(
        kernel,
        in_specs=[whole()] * (n + 3),
        out_specs=[whole()] * n,
        out_shape=[jax.ShapeDtypeStruct(b.shape, BF16) for b in blocks],
        compiler_params=params(24),
        name="run_expert",
    )(*blocks, gate, up, down)


def combine(weight, groups):
    def kernel(weight_ref, *refs):
        held = jnp.concatenate([refs[0][i] for i in range(4)], axis=0).astype(F32)
        refs[1][...] = lax.dot_general(
            weight_ref[...],
            held,
            (((0,), (0,)), ((), ())),
            precision=lax.Precision.HIGHEST,
            preferred_element_type=F32,
        ).astype(BF16)

    return pl.pallas_call(
        kernel,
        in_specs=[whole()] * 2,
        out_specs=whole(),
        out_shape=jax.ShapeDtypeStruct((TOKENS, D), BF16),
        compiler_params=params(),
        name="combine",
    )(weight, groups)


def stack(arrays):
    rows = sum(a.shape[0] for a in arrays)

    def kernel(*refs):
        at = 0
        for r in refs[:-1]:
            refs[-1][at : at + r.shape[0], :] = r[...]
            at += r.shape[0]

    return pl.pallas_call(
        kernel,
        in_specs=[whole()] * len(arrays),
        out_specs=whole(),
        out_shape=jax.ShapeDtypeStruct((rows, arrays[0].shape[1]), BF16),
        compiler_params=params(4),
        name="stack",
    )(*arrays)


def tie(values, *others):
    n = len(values)
    return lax.optimization_barrier((*values, *others))[:n]


def add(*arrays):
    return sum(a.astype(F32) for a in arrays).astype(BF16)


def exchange_x(a):
    groups = [[z * N_X + x for x in range(N_X)] for z in range(N_Z)]
    return lax.all_to_all(a, "exp", 0, 0, tiled=True, axis_index_groups=groups)


def scatter_ctx(parts):
    own, swapped, below, above, below_swapped, below_two, above_swapped, far = parts
    got_far = swap_l(far)
    got_below_swapped = swap_l(below_swapped)
    got_above_swapped = shift_y(above_swapped, 1)
    got_two = shift_y(add(below_two, got_far), -1)
    got_above = shift_y(above, 1)
    got_swapped = swap_l(add(swapped, got_above_swapped))
    got_below = shift_y(add(below, got_two, got_below_swapped), -1)
    return add(own, got_above, got_below, got_swapped)


def on_device(
    hidden_in,
    queries,
    keys,
    values,
    out_proj,
    norm_gain,
    expert_ids,
    gate_fixed,
    live_counts,
    gate_proj,
    up_proj,
    down_proj,
):
    exp_index = lax.axis_index("exp")
    ctx_index = lax.axis_index("ctx")
    rep_index = lax.axis_index("rep")
    z, x = exp_index // N_X, exp_index % N_X
    y, side = ctx_index // 2, ctx_index % 2
    place = jnp.stack([z, x, rep_index]).astype(jnp.int32)
    seq_rows = queries.shape[0]
    local_heads = queries.shape[1] // HEAD_DIM
    kv_index = exp_index * local_heads // (HEADS // KV_HEADS)

    spot = jnp.stack([y, side, ctx_index]).astype(jnp.int32)

    keys, values, out_proj = [
        pltpu.with_memory_space_constraint(a, pltpu.HBM) for a in (keys, values, out_proj)
    ]
    own = pick_head(kv_index.astype(jnp.int32)[None], keys, values)
    swapped = swap_l(own)
    away = pick_weights(jnp.stack([rep_index, x]).astype(jnp.int32), out_proj)
    fetched = [shift_x(away[d - 1], d) for d in range(1, N_X)]
    (swapped,) = tie((swapped,), *away)
    pair = stack([own, swapped])
    below = shift_y(pair, 1)
    above = shift_y(pair, -1)
    state = attend(queries, [pair], spot, [(0, 0), (0, 1)], None)
    riders = pick_hidden(place, live_counts, hidden_in, expert_ids.T)
    below, above = tie((below, above), *state, *riders)
    block = own.shape[0]
    far_a = shift_y(below[:block], 1)
    far_b = shift_y(above[block:], -1)
    state = attend(
        queries, [below, above], spot, [(-1, 0), (-1, 1), (1, 0), (1, 1)], state
    )
    far_a, far_b, *fetched = tie((far_a, far_b, *fetched), *state)
    messages = attend(
        queries, [far_a, far_b], spot, [(-2, 0), (-2, 1)], state, [[riders[2], riders[1]], [riders[3]]]
    )

    from_left = shift_x(messages[0], 1)
    from_right = shift_x(messages[1], 3)
    half = seq_rows // 2
    far_a = shift_x(forward(from_left, 0, half, RIDER), 1)
    far_b = shift_x(forward(from_right, half, half, 0), 3)
    weight = route_weights(
        tie((place,), from_left)[0], live=live_counts, ids=expert_ids.T, gates=gate_fixed.T
    )
    other = swap_core(stack(fetched))
    near = project_near(
        place, messages[0], out_proj, [from_left, from_right], [fetched[0], fetched[2]], other
    )
    far_a, far_b, near = tie((far_a, far_b, near))
    hidden = [riders[0], from_left, far_a, from_right]
    mine, up_chunk, down_chunk, low, high = project_far(
        place, near, [far_a, far_b], fetched[1], other
    )

    middle = low.shape[1]
    got_low = shift_z(low, 1)
    got_high = shift_z(high, -1)
    pick = route(place, hidden)
    got_low, got_high = tie((got_low, got_high), pick)
    up_chunk = jnp.concatenate([add(up_chunk[:, :middle], got_low), up_chunk[:, middle:]], axis=1)
    down_chunk = jnp.concatenate(
        [down_chunk[:, :middle], add(down_chunk[:, middle:], got_high)], axis=1
    )
    got_up = shift_z(up_chunk, 1)
    got_down = shift_z(down_chunk, -1)
    mixed, *send = finish_rows(place, hidden, [mine, got_up, got_down], pick)

    by_z = [send[0]] + [shift_z(send[d], d) for d in range(1, N_Z)]
    block, mixed = join_columns(exchange_x(by_columns(by_z, mixed)), norm_gain.reshape(1, D))
    swapped = swap_l(block)
    below = shift_y(block, 1)
    above = shift_y(block, -1)
    below_two = shift_y(below, 1)
    below_swapped = swap_l(below)
    above_swapped = shift_y(swapped, -1)
    far = swap_l(below_two)
    parts = run_expert(
        [block, swapped, below, above, below_swapped, below_two, above_swapped, far],
        gate_proj[0].T,
        up_proj[0].T,
        down_proj[0],
    )

    result = scatter_ctx(parts)
    back_z = [result[:8]] + [shift_z(result[8 * d : 8 * d + 8], -d) for d in range(1, N_Z)]
    return (mixed, combine(weight, exchange_x(regroup(back_z))))


def solution(mesh):
    in_specs = (
        P(("rep", "ctx", "exp"), None),
        P(("rep", "ctx"), "exp"),
        P(("rep", "ctx"), None),
        P(("rep", "ctx"), None),
        P("exp", None),
        P(),
        P(("rep", "ctx", "exp"), None),
        P(("rep", "ctx", "exp"), None),
        P(("rep", "ctx", "exp")),
        P("exp", None, "ctx"),
        P("exp", None, "ctx"),
        P("exp", "ctx", None),
    )
    out_specs = (P(("rep", "ctx", "exp"), None), P(("rep", "ctx", "exp"), None))
    return jax.shard_map(
        on_device, mesh=mesh, in_specs=in_specs, out_specs=out_specs, check_vma=False
    )
```

```python
import functools
import math

import jax
import jax.numpy as jnp
from jax import lax
from jax.experimental import pallas as pl
from jax.experimental.pallas import tpu as pltpu
from jax.sharding import PartitionSpec as P

D = 4096
HEADS = 64
KV_HEADS = 4
HEAD_DIM = 128
TOPK = 8
CAP = 2
N_X = 4
N_Z = 4
N_Y = 4
TOKENS = 32
RIDER = 2 * (TOKENS + TOPK)
BF16 = jnp.bfloat16
F32 = jnp.float32
LOWEST = -1e30
EXP2_SCALE = HEAD_DIM ** (-0.5) * math.log2(math.e)
VMEM = pltpu.VMEM
SMEM = pltpu.SMEM


def params(limit_mib=8):
    return pltpu.CompilerParams(vmem_limit_bytes=limit_mib << 20)


def whole():
    return pl.BlockSpec(memory_space=VMEM)


def shift_x(a, d):
    pairs = [(z * N_X + x, z * N_X + (x + d) % N_X) for z in range(N_Z) for x in range(N_X)]
    return lax.ppermute(a, "exp", pairs)


def shift_z(a, d):
    pairs = [(z * N_X + x, (z + d) % N_Z * N_X + x) for z in range(N_Z) for x in range(N_X)]
    return lax.ppermute(a, "exp", pairs)


def shift_y(a, d):
    pairs = [(y * 2 + k, (y + d) % N_Y * 2 + k) for y in range(N_Y) for k in range(2)]
    return lax.ppermute(a, "ctx", pairs)


def swap_l(a):
    return lax.ppermute(a, "ctx", [(i, i ^ 1) for i in range(2 * N_Y)])


def swap_core(a):
    return lax.ppermute(a, "rep", [(0, 1), (1, 0)])


def pick_head(where_am, keys, values):
    rows = keys.shape[0]

    def kernel(where_ref, key_ref, value_ref, out_ref):
        out_ref[0:rows, :] = key_ref[...]
        out_ref[rows:, :] = value_ref[...]

    column = pl.BlockSpec((rows, HEAD_DIM), lambda i, w: (0, w[0]))
    return pl.pallas_call(
        kernel,
        grid_spec=pltpu.PrefetchScalarGridSpec(
            num_scalar_prefetch=1,
            grid=(1,),
            in_specs=[column, column],
            out_specs=pl.BlockSpec((2 * rows, HEAD_DIM), lambda i, w: (0, 0)),
        ),
        out_shape=jax.ShapeDtypeStruct((2 * rows, HEAD_DIM), BF16),
        compiler_params=params(),
        name="pick_head",
    )(where_am, keys, values)


def pick_weights(place, out_proj):
    rows, cols = out_proj.shape[0] // 2, out_proj.shape[1] // N_X

    def kernel(place_ref, *refs):
        for source, target in zip(refs[:3], refs[3:]):
            target[...] = source[...]

    def block(d):
        return pl.BlockSpec((rows, cols), lambda i, w: (w[0], lax.rem(w[1] + d, N_X)))

    return pl.pallas_call(
        kernel,
        grid_spec=pltpu.PrefetchScalarGridSpec(
            num_scalar_prefetch=1,
            grid=(1,),
            in_specs=[block(d) for d in range(1, N_X)],
            out_specs=[pl.BlockSpec((rows, cols), lambda i, w: (0, 0))] * 3,
        ),
        out_shape=[jax.ShapeDtypeStruct((rows, cols), BF16)] * 3,
        compiler_params=params(),
        name="pick_weights",
    )(place, out_proj, out_proj, out_proj)


def attend(queries, blocks, spot, steps, state, riders=None):
    rows, heads = queries.shape[0], queries.shape[1] // HEAD_DIM
    calls = len(blocks)
    n = sum(b.shape[0] for b in blocks) // (2 * rows)
    first = state is None
    last = riders is not None
    passengers = [r for group in riders for r in group] if last else []
    tile = 128

    def kernel(*refs):
        spot_ref, q_ref = refs[0], refs[1]
        bias = []
        for dy, flip in steps:
            side = 1 - spot_ref[1] if flip else spot_ref[1]
            owner = lax.rem(spot_ref[0] + N_Y + dy, N_Y) * 2 + side
            bias.append(jnp.where(owner <= spot_ref[2], 0.0, LOWEST).astype(F32))
        kv_refs = [
            r.at[first_row : first_row + 2 * rows]
            for r in refs[2 : 2 + calls]
            for first_row in range(0, r.shape[0], 2 * rows)
        ]
        rest, (key_ref, value_ref) = refs[2 + calls : -2], refs[-2:]
        if not first:
            acc_in, top_in = rest[0], rest[1]
            rest = rest[2:]
        if last:
            rider_refs, rest = list(rest[: len(passengers)]), rest[len(passengers) :]
            for group, target in zip(riders, rest):
                for at in range(rows, rows + RIDER * len(group), RIDER):
                    target[at : at + RIDER, :] = rider_refs.pop(0)[...]
        for b, r in enumerate(kv_refs):
            at = slice(b * rows, (b + 1) * rows)
            key_ref[at, :] = r[0:rows, :]
            value_ref[at, 0:HEAD_DIM] = r[rows:, :]
        value_ref[:, HEAD_DIM:] = jnp.ones((n * rows, HEAD_DIM), BF16)

        def head(h, carry):
            lanes = pl.ds(pl.multiple_of(h * HEAD_DIM, HEAD_DIM), HEAD_DIM)

            def score(part):
                return lax.dot_general(
                    q_ref[pl.ds(part * tile, tile), lanes],
                    key_ref[...],
                    (((1,), (1,)), ((), ())),
                    preferred_element_type=F32,
                )

            upcoming = score(0)
            for part in range(rows // tile):
                at = pl.ds(part * tile, tile)
                scores = upcoming
                if (part + 1) * tile < rows:
                    upcoming = score(part + 1)
                if first:
                    i = lax.broadcasted_iota(jnp.int32, (tile, rows), 0) + part * tile
                    j = lax.broadcasted_iota(jnp.int32, (tile, rows), 1)
                    diagonal = jnp.where(j <= i, scores[:, :rows], LOWEST)
                    scores = jnp.concatenate([diagonal, scores[:, rows:]], axis=1)
                    newest = jnp.full((tile, HEAD_DIM), LOWEST, F32)
                else:
                    before = top_in[h, at, :]
                    newest = before
                for b in range(n):
                    highest = jnp.max(scores[:, b * rows : (b + 1) * rows], axis=1, keepdims=True)
                    newest = jnp.maximum(newest, highest + bias[b])
                offsets = [(newest - bias[b]) * EXP2_SCALE for b in range(n)]
                pieces = []
                for lane in range(0, n * rows, HEAD_DIM):
                    pieces.append(
                        jnp.exp2(
                            scores[:, lane : lane + HEAD_DIM] * EXP2_SCALE - offsets[lane // rows]
                        ).astype(BF16)
                    )
                total = jnp.dot(
                    jnp.concatenate(pieces, axis=1), value_ref[...], preferred_element_type=F32
                )
                if not first:
                    factor = jnp.exp2((before - newest) * EXP2_SCALE)
                    total = acc_in[h, at, :] * jnp.concatenate([factor, factor], axis=1) + total
                if last:
                    done = (total[:, :HEAD_DIM] / total[:, HEAD_DIM:]).astype(BF16)
                    for target in rest:
                        target[at, lanes] = done
                else:
                    rest[0][h, at, :] = total
                    rest[1][h, at, :] = newest
            return carry

        lax.fori_loop(0, heads, head, 0)

    state_shapes = [
        jax.ShapeDtypeStruct((heads, rows, 2 * HEAD_DIM), F32),
        jax.ShapeDtypeStruct((heads, rows, HEAD_DIM), F32),
    ]
    return pl.pallas_call(
        kernel,
        in_specs=[pl.BlockSpec(memory_space=SMEM)]
        + [whole()] * (1 + calls + (0 if first else 2) + len(passengers)),
        out_specs=[whole()] * 2,
        out_shape=[
            jax.ShapeDtypeStruct((rows + RIDER * len(group), queries.shape[1]), BF16)
            for group in riders
        ]
        if last
        else state_shapes,
        scratch_shapes=[VMEM((n * rows, HEAD_DIM), BF16), VMEM((n * rows, 2 * HEAD_DIM), BF16)],
        compiler_params=params(16),
        cost_estimate=pl.CostEstimate(
            flops=heads * n * rows * rows * HEAD_DIM * 4,
            transcendentals=heads * n * rows * rows,
            bytes_accessed=4 << 20,
        ),
        name="attend",
    )(spot, queries, *blocks, *(() if first else state), *passengers)


def rows_of(place_ref, left_ref, dz, columns):
    row = lax.rem(place_ref[0] + dz, N_Z) * (N_X * TOKENS)
    return left_ref[pl.ds(pl.multiple_of(row, N_X * TOKENS), N_X * TOKENS), columns]


def project_near(place, own, out_proj, lefts, fetched, other):
    n = len(lefts)
    cols = out_proj.shape[1] // N_X

    def kernel(place_ref, own_ref, weight_ref, *refs):
        left_refs, fetched_refs, other_ref, out_ref = refs[:n], refs[n : 2 * n], refs[2 * n], refs[-1]

        def chunk(dz, carry):
            total = jnp.dot(
                rows_of(place_ref, own_ref, dz, slice(None)),
                weight_ref[...],
                preferred_element_type=F32,
            )
            for k in range(n):
                total = total + fetched_part(
                    place_ref, left_refs[k], fetched_refs[k], other_ref, (0, 2)[k], dz
                )
            out_ref[dz] = total
            return carry

        lax.fori_loop(0, N_Z, chunk, 0)

    fixed = lambda i, w: (0, 0)
    square = pl.BlockSpec(own.shape, fixed)
    return pl.pallas_call(
        kernel,
        grid_spec=pltpu.PrefetchScalarGridSpec(
            num_scalar_prefetch=1,
            grid=(1,),
            in_specs=[square, pl.BlockSpec((out_proj.shape[0], cols), lambda i, w: (0, w[1]))]
            + [pl.BlockSpec(left.shape, fixed) for left in lefts]
            + [pl.BlockSpec(fetched[0].shape, fixed)] * n
            + [pl.BlockSpec(other.shape, fixed)],
            out_specs=pl.BlockSpec((N_Z, N_X * TOKENS, cols), lambda i, w: (0, 0, 0)),
        ),
        out_shape=jax.ShapeDtypeStruct((N_Z, N_X * TOKENS, cols), F32),
        compiler_params=params(28),
        cost_estimate=pl.CostEstimate(flops=1, transcendentals=0, bytes_accessed=1),
        name="project_near",
    )(place, own, out_proj, *lefts, *fetched, other)


def fetched_part(place_ref, left_ref, fetched_ref, other_ref, at, dz):
    half = fetched_ref.shape[0]
    core = place_ref[2]
    mine = pl.ds(pl.multiple_of(core * half, half), half)
    theirs = pl.ds(pl.multiple_of((1 - core) * half, half), half)
    return jnp.dot(
        rows_of(place_ref, left_ref, dz, mine), fetched_ref[...], preferred_element_type=F32
    ) + jnp.dot(
        rows_of(place_ref, left_ref, dz, theirs),
        other_ref[at * half : (at + 1) * half, :],
        preferred_element_type=F32,
    )


def forward(message, first, rows, riders):
    attended = message.shape[0] // 512 * 512

    def kernel(message_ref, out_ref):
        out_ref[0:rows, :] = message_ref[first : first + rows, :]
        if riders:
            out_ref[rows:, :] = message_ref[attended : attended + riders, :]

    return pl.pallas_call(
        kernel,
        in_specs=[whole()],
        out_specs=whole(),
        out_shape=jax.ShapeDtypeStruct((rows + riders, message.shape[1]), BF16),
        compiler_params=params(4),
        name="forward",
    )(message)


def project_far(place, near, lefts, fetched, other):
    shape = near.shape[1:]
    middle = shape[1] // 2

    def kernel(place_ref, upper_ref, lower_ref, fetched_ref, other_ref, *refs):
        near_ref, out_refs, left_ref = refs[0], refs[1:-1], refs[-1]
        half = left_ref.shape[0] // 2
        left_ref[:half, :] = upper_ref[:half, :]
        left_ref[half:, :] = lower_ref[...]
        for dz in (2, 1, 3, 0):
            total = near_ref[dz] + fetched_part(
                place_ref, left_ref, fetched_ref, other_ref, 1, dz
            )
            total = total.astype(BF16)
            if dz == 2:
                out_refs[3][...] = total[:, :middle]
                out_refs[4][...] = total[:, middle:]
            else:
                out_refs[{0: 0, 1: 1, 3: 2}[dz]][...] = total

    return pl.pallas_call(
        kernel,
        in_specs=[pl.BlockSpec(memory_space=SMEM)] + [whole()] * 5,
        out_specs=[whole()] * 5,
        scratch_shapes=[VMEM((2 * lefts[1].shape[0], lefts[1].shape[1]), BF16)],
        out_shape=[jax.ShapeDtypeStruct(shape, BF16)] * 3
        + [jax.ShapeDtypeStruct((shape[0], middle), BF16)] * 2,
        compiler_params=params(),
        name="project_far",
    )(place, *lefts, fetched, other, near)


def pick_hidden(place, live, hidden_in, ids):
    cols = D // N_X // 2

    def kernel(place_ref, live_ref, hidden_ref, id_ref, *out_refs):
        x = place_ref[1]
        t = lax.broadcasted_iota(jnp.int32, (TOPK, TOKENS), 1)
        alive = jnp.where(t < live_ref[0], id_ref[...] + 1, 0).astype(F32)
        lanes = (
            lax.broadcasted_iota(jnp.int32, (TOKENS, cols), 1)
            == lax.broadcasted_iota(jnp.int32, (TOKENS, cols), 0) + x * TOKENS
        ).astype(F32)
        alive = jnp.dot(alive, lanes, preferred_element_type=F32)
        for d in range(N_X):
            for side in range(2):
                column = pl.multiple_of(lax.rem(x + d, N_X) * (2 * cols) + side * cols, cols)
                top = side * (TOKENS + TOPK)
                out_refs[d][top : top + TOKENS, :] = hidden_ref[:, pl.ds(column, cols)]
                out_refs[d][top + TOKENS : top + TOKENS + TOPK, :] = (
                    alive if side == 0 else jnp.zeros_like(alive)
                ).astype(BF16)

    return pl.pallas_call(
        kernel,
        in_specs=[pl.BlockSpec(memory_space=SMEM)] * 2 + [whole()] * 2,
        out_specs=[whole()] * N_X,
        out_shape=[jax.ShapeDtypeStruct((RIDER, cols), BF16)] * N_X,
        compiler_params=params(),
        name="pick_hidden",
    )(place, live, hidden_in, ids)


def route(place, hidden):
    slots = N_Z * N_X * N_X * CAP
    tokens = N_X * TOKENS

    def kernel(place_ref, *refs):
        z = place_ref[0]
        s = lax.broadcasted_iota(jnp.int32, (slots, tokens), 0)
        t = lax.broadcasted_iota(jnp.int32, (slots, tokens), 1)
        dz, expert_x, owner, cap = s // 32, (s // 8) % 4, (s // 2) % 4, s % 2
        expert = ((z + dz) % N_Z) * N_X + expert_x
        wanted = jnp.where(owner == t // TOKENS, expert + 1, -1).astype(F32)
        ids = sum(
            r[r.shape[0] - RIDER + TOKENS : r.shape[0] - RIDER + TOKENS + TOPK, 0:tokens].astype(F32)
            for r in refs[:4]
        )
        present = jnp.zeros((slots, tokens), F32)
        for k in range(TOPK):
            present = present + (ids[k : k + 1, :] == wanted).astype(F32)
        earlier = (
            lax.broadcasted_iota(jnp.int32, (tokens, tokens), 0)
            < lax.broadcasted_iota(jnp.int32, (tokens, tokens), 1)
        ).astype(F32)
        rank = jnp.dot(present, earlier, preferred_element_type=F32)
        fits = jnp.abs(rank - cap.astype(F32)) < 0.5
        refs[4][...] = jnp.where(fits, present, 0.0).astype(BF16)

    return pl.pallas_call(
        kernel,
        in_specs=[pl.BlockSpec(memory_space=SMEM)] + [whole()] * 4,
        out_specs=whole(),
        out_shape=jax.ShapeDtypeStruct((slots, tokens), BF16),
        compiler_params=params(),
        name="route",
    )(place, *hidden)


def route_weights(place, ids, gates, live):
    slots = N_X * N_Z * CAP

    def kernel(place_ref, live_ref, id_ref, gate_ref, weight_ref):
        z = place_ref[0]
        s = lax.broadcasted_iota(jnp.int32, (slots, TOKENS), 0)
        t = lax.broadcasted_iota(jnp.int32, (slots, TOKENS), 1)
        expert_x, dz, cap = s // (N_Z * CAP), (s // CAP) % N_Z, s % CAP
        expert = ((z + dz) % N_Z) * N_X + expert_x
        present = jnp.zeros((slots, TOKENS), F32)
        weight = jnp.zeros((slots, TOKENS), F32)
        for k in range(TOPK):
            hit = ((id_ref[k : k + 1, :] == expert) & (t < live_ref[0])).astype(F32)
            present = present + hit
            weight = weight + hit * gate_ref[k : k + 1, :].astype(F32)
        earlier = (
            lax.broadcasted_iota(jnp.int32, (TOKENS, TOKENS), 0)
            < lax.broadcasted_iota(jnp.int32, (TOKENS, TOKENS), 1)
        ).astype(F32)
        rank = jnp.dot(present, earlier, preferred_element_type=F32)
        weight_ref[...] = jnp.where(jnp.abs(rank - cap.astype(F32)) < 0.5, weight, 0.0) / 4096.0

    return pl.pallas_call(
        kernel,
        in_specs=[pl.BlockSpec(memory_space=SMEM)] * 2 + [whole()] * 2,
        out_specs=whole(),
        out_shape=jax.ShapeDtypeStruct((slots, TOKENS), F32),
        compiler_params=params(),
        name="route_weights",
    )(place, live, ids, gates)


def finish_rows(place, hidden, sums, pick):
    cols = sums[0].shape[1]

    def kernel(place_ref, h0, h1, h2, h3, s0, s1, s2, pick_ref, *refs):
        mixed_ref, send_refs = refs[0], refs[1:5]
        for d, h in enumerate((h0, h1, h2, h3)):
            row = lax.rem(place_ref[1] + N_X - d, N_X) * TOKENS
            at = pl.ds(pl.multiple_of(row, TOKENS), TOKENS)
            top = h.shape[0] - RIDER
            rows = jnp.concatenate(
                [h[top : top + TOKENS, :], h[top + TOKENS + TOPK : top + 2 * TOKENS + TOPK, :]], axis=1
            )
            mixed_ref[at, :] = (
                rows.astype(F32)
                + (s0[at, :].astype(F32) + s1[at, :].astype(F32) + s2[at, :].astype(F32))
            ).astype(BF16)
        send = jnp.dot(pick_ref[...], mixed_ref[...], preferred_element_type=F32).astype(BF16)
        for dz in range(N_Z):
            send_refs[dz][...] = send[dz * 32 : dz * 32 + 32, :]

    return pl.pallas_call(
        kernel,
        in_specs=[pl.BlockSpec(memory_space=SMEM)] + [whole()] * 8,
        out_specs=[whole()] * 5,
        out_shape=[jax.ShapeDtypeStruct((N_X * TOKENS, cols), BF16)]
        + [jax.ShapeDtypeStruct((32, cols), BF16)] * 4,
        compiler_params=params(),
        name="finish_rows",
    )(place, *hidden, *sums, pick)


def by_columns(groups, mixed):
    cols = mixed.shape[1]

    def kernel(*refs):
        held = [r[...] for r in refs[:4]]
        for x in range(N_X):
            refs[5][x, 0:32, :] = jnp.concatenate([h[x * 8 : x * 8 + 8, :] for h in held], axis=0)
            refs[5][x, 32:64, :] = refs[4][x * TOKENS : (x + 1) * TOKENS, :]

    return pl.pallas_call(
        kernel,
        in_specs=[whole()] * 5,
        out_specs=whole(),
        out_shape=jax.ShapeDtypeStruct((N_X, 64, cols), BF16),
        compiler_params=params(),
        name="by_columns",
    )(*groups, mixed)


def join_columns(pieces, gain):
    cols = pieces.shape[2]

    def kernel(piece_ref, gain_ref, block_ref, mixed_ref):
        values = [piece_ref[x, 0:32, :].astype(F32) for x in range(N_X)]
        square = sum(jnp.sum(v * v, axis=1, keepdims=True) for v in values)
        scale = lax.rsqrt(square / D + 1e-06)
        for x, value in enumerate(values):
            column = slice(x * cols, (x + 1) * cols)
            block_ref[:, column] = (value * scale * gain_ref[:, column]).astype(BF16)
            mixed_ref[:, column] = piece_ref[x, 32:64, :]

    return pl.pallas_call(
        kernel,
        in_specs=[whole()] * 2,
        out_specs=[whole()] * 2,
        out_shape=[jax.ShapeDtypeStruct((32, D), BF16)] * 2,
        compiler_params=params(),
        name="join_columns",
    )(pieces, gain)


def regroup(groups):
    rows = 4 * 4 * CAP

    def kernel(*refs):
        held = jnp.concatenate([r[...] for r in refs[:4]], axis=0)
        to = lax.broadcasted_iota(jnp.int32, (rows, rows), 0)
        come = lax.broadcasted_iota(jnp.int32, (rows, rows), 1)
        b, a, cap = to // 8, (to // CAP) % 4, to % CAP
        order = (come == a * 8 + b * CAP + cap).astype(BF16)
        moved = jnp.dot(order, held, preferred_element_type=F32).astype(BF16)
        for i in range(4):
            refs[4][i] = moved[i * 8 : i * 8 + 8, :]

    return pl.pallas_call(
        kernel,
        in_specs=[whole()] * 4,
        out_specs=whole(),
        out_shape=jax.ShapeDtypeStruct((4, 8, D), BF16),
        compiler_params=params(),
        name="regroup",
    )(*groups)


def run_expert(blocks, gate, up, down):
    n = len(blocks)

    def kernel(*refs):
        in_refs, (gate_ref, up_ref, down_ref), out_refs = refs[:n], refs[n : n + 3], refs[n + 3 :]
        rows = jnp.concatenate([r[...] for r in in_refs], axis=0)
        last = (((1,), (1,)), ((), ()))
        gate_part = lax.dot_general(rows, gate_ref[...], last, preferred_element_type=F32)
        up_part = lax.dot_general(rows, up_ref[...], last, preferred_element_type=F32)
        hidden = (gate_part / (1.0 + jnp.exp(-gate_part)) * up_part).astype(BF16)
        result = jnp.dot(hidden, down_ref[...], preferred_element_type=F32).astype(BF16)
        at = 0
        for r in out_refs:
            r[...] = result[at : at + r.shape[0], :]
            at += r.shape[0]

    return pl.pallas_call(
        kernel,
        in_specs=[whole()] * (n + 3),
        out_specs=[whole()] * n,
        out_shape=[jax.ShapeDtypeStruct(b.shape, BF16) for b in blocks],
        compiler_params=params(24),
        name="run_expert",
    )(*blocks, gate, up, down)


def combine(weight, groups):
    def kernel(weight_ref, *refs):
        held = jnp.concatenate([refs[0][i] for i in range(4)], axis=0).astype(F32)
        refs[1][...] = lax.dot_general(
            weight_ref[...],
            held,
            (((0,), (0,)), ((), ())),
            precision=lax.Precision.HIGHEST,
            preferred_element_type=F32,
        ).astype(BF16)

    return pl.pallas_call(
        kernel,
        in_specs=[whole()] * 2,
        out_specs=whole(),
        out_shape=jax.ShapeDtypeStruct((TOKENS, D), BF16),
        compiler_params=params(),
        name="combine",
    )(weight, groups)


def stack(arrays):
    rows = sum(a.shape[0] for a in arrays)

    def kernel(*refs):
        at = 0
        for r in refs[:-1]:
            refs[-1][at : at + r.shape[0], :] = r[...]
            at += r.shape[0]

    return pl.pallas_call(
        kernel,
        in_specs=[whole()] * len(arrays),
        out_specs=whole(),
        out_shape=jax.ShapeDtypeStruct((rows, arrays[0].shape[1]), BF16),
        compiler_params=params(4),
        name="stack",
    )(*arrays)


def tie(values, *others):
    n = len(values)
    return lax.optimization_barrier((*values, *others))[:n]


def add(*arrays):
    return sum(a.astype(F32) for a in arrays).astype(BF16)


def exchange_x(a):
    groups = [[z * N_X + x for x in range(N_X)] for z in range(N_Z)]
    return lax.all_to_all(a, "exp", 0, 0, tiled=True, axis_index_groups=groups)


def scatter_ctx(parts):
    own, swapped, below, above, below_swapped, below_two, above_swapped, far = parts
    got_far = swap_l(far)
    got_below_swapped = shift_y(below_swapped, -1)
    got_above_swapped = shift_y(above_swapped, 1)
    got_two = shift_y(add(below_two, got_far), -1)
    got_above = shift_y(above, 1)
    got_swapped = swap_l(add(swapped, got_above_swapped, got_below_swapped))
    got_below = shift_y(add(below, got_two), -1)
    return add(own, got_above, got_below, got_swapped)


def on_device(
    hidden_in,
    queries,
    keys,
    values,
    out_proj,
    norm_gain,
    expert_ids,
    gate_fixed,
    live_counts,
    gate_proj,
    up_proj,
    down_proj,
):
    exp_index = lax.axis_index("exp")
    ctx_index = lax.axis_index("ctx")
    rep_index = lax.axis_index("rep")
    z, x = exp_index // N_X, exp_index % N_X
    y, side = ctx_index // 2, ctx_index % 2
    place = jnp.stack([z, x, rep_index]).astype(jnp.int32)
    seq_rows = queries.shape[0]
    local_heads = queries.shape[1] // HEAD_DIM
    kv_index = exp_index * local_heads // (HEADS // KV_HEADS)

    spot = jnp.stack([y, side, ctx_index]).astype(jnp.int32)

    keys, values, out_proj = [
        pltpu.with_memory_space_constraint(a, pltpu.HBM) for a in (keys, values, out_proj)
    ]
    own = pick_head(kv_index.astype(jnp.int32)[None], keys, values)
    swapped = swap_l(own)
    away = pick_weights(jnp.stack([rep_index, x]).astype(jnp.int32), out_proj)
    fetched = [shift_x(away[d - 1], d) for d in range(1, N_X)]
    (swapped,) = tie((swapped,), *away)
    pair = stack([own, swapped])
    below = shift_y(pair, 1)
    above = shift_y(pair, -1)
    state = attend(queries, [pair], spot, [(0, 0), (0, 1)], None)
    riders = pick_hidden(place, live_counts, hidden_in, expert_ids.T)
    below, above = tie((below, above), *state, *riders)
    block = own.shape[0]
    far_a = shift_y(forward(below, 0, block, 0), 1)
    far_b = shift_y(forward(above, block, block, 0), -1)
    state = attend(
        queries, [below, above], spot, [(-1, 0), (-1, 1), (1, 0), (1, 1)], state
    )
    far_a, far_b, *fetched = tie((far_a, far_b, *fetched), *state)
    messages = attend(
        queries, [far_a, far_b], spot, [(-2, 0), (-2, 1)], state, [[riders[2], riders[1]], [riders[3]]]
    )

    from_left = shift_x(messages[0], 1)
    from_right = shift_x(messages[1], 3)
    half = seq_rows // 2
    far_a = shift_x(forward(from_left, 0, half, RIDER), 1)
    far_b = shift_x(forward(from_right, half, half, 0), 3)
    weight = route_weights(
        tie((place,), from_left)[0], live=live_counts, ids=expert_ids.T, gates=gate_fixed.T
    )
    other = swap_core(stack(fetched))
    near = project_near(
        place, messages[0], out_proj, [from_left, from_right], [fetched[0], fetched[2]], other
    )
    far_a, far_b, near = tie((far_a, far_b, near))
    hidden = [riders[0], from_left, far_a, from_right]
    mine, up_chunk, down_chunk, low, high = project_far(
        place, near, [far_a, far_b], fetched[1], other
    )

    middle = low.shape[1]
    got_low = shift_z(low, 1)
    got_high = shift_z(high, -1)
    pick = route(place, hidden)
    got_low, got_high = tie((got_low, got_high), pick)
    up_chunk = jnp.concatenate([add(up_chunk[:, :middle], got_low), up_chunk[:, middle:]], axis=1)
    down_chunk = jnp.concatenate(
        [down_chunk[:, :middle], add(down_chunk[:, middle:], got_high)], axis=1
    )
    got_up = shift_z(up_chunk, 1)
    got_down = shift_z(down_chunk, -1)
    mixed, *send = finish_rows(place, hidden, [mine, got_up, got_down], pick)

    by_z = [send[0]] + [shift_z(send[d], d) for d in range(1, N_Z)]
    block, mixed = join_columns(exchange_x(by_columns(by_z, mixed)), norm_gain.reshape(1, D))
    swapped = swap_l(block)
    below = shift_y(block, 1)
    above = shift_y(block, -1)
    below_two = shift_y(below, 1)
    below_swapped = shift_y(swapped, 1)
    above_swapped = shift_y(swapped, -1)
    far = swap_l(below_two)
    parts = run_expert(
        [block, swapped, below, above, below_swapped, below_two, above_swapped, far],
        gate_proj[0].T,
        up_proj[0].T,
        down_proj[0],
    )

    result = scatter_ctx(parts)
    back_z = [result[:8]] + [shift_z(result[8 * d : 8 * d + 8], -d) for d in range(1, N_Z)]
    return (mixed, combine(weight, exchange_x(regroup(back_z))))


def solution(mesh):
    in_specs = (
        P(("rep", "ctx", "exp"), None),
        P(("rep", "ctx"), "exp"),
        P(("rep", "ctx"), None),
        P(("rep", "ctx"), None),
        P("exp", None),
        P(),
        P(("rep", "ctx", "exp"), None),
        P(("rep", "ctx", "exp"), None),
        P(("rep", "ctx", "exp")),
        P("exp", None, "ctx"),
        P("exp", None, "ctx"),
        P("exp", "ctx", None),
    )
    out_specs = (P(("rep", "ctx", "exp"), None), P(("rep", "ctx", "exp"), None))
    return jax.shard_map(
        on_device, mesh=mesh, in_specs=in_specs, out_specs=out_specs, check_vma=False
    )
```

```python
import functools
import math

import jax
import jax.numpy as jnp
from jax import lax
from jax.experimental import pallas as pl
from jax.experimental.pallas import tpu as pltpu
from jax.sharding import PartitionSpec as P

D = 4096
HEADS = 64
KV_HEADS = 4
HEAD_DIM = 128
TOPK = 8
CAP = 2
N_X = 4
N_Z = 4
N_Y = 4
TOKENS = 32
RIDER = 2 * (TOKENS + TOPK)
BF16 = jnp.bfloat16
F32 = jnp.float32
LOWEST = -1e30
EXP2_SCALE = HEAD_DIM ** (-0.5) * math.log2(math.e)
VMEM = pltpu.VMEM
SMEM = pltpu.SMEM


def params(limit_mib=8):
    return pltpu.CompilerParams(vmem_limit_bytes=limit_mib << 20)


def whole():
    return pl.BlockSpec(memory_space=VMEM)


def shift_x(a, d):
    pairs = [(z * N_X + x, z * N_X + (x + d) % N_X) for z in range(N_Z) for x in range(N_X)]
    return lax.ppermute(a, "exp", pairs)


def shift_z(a, d):
    pairs = [(z * N_X + x, (z + d) % N_Z * N_X + x) for z in range(N_Z) for x in range(N_X)]
    return lax.ppermute(a, "exp", pairs)


def shift_y(a, d):
    pairs = [(y * 2 + k, (y + d) % N_Y * 2 + k) for y in range(N_Y) for k in range(2)]
    return lax.ppermute(a, "ctx", pairs)


def turn_y(a, d):
    pairs = []
    for core in range(2):
        for y in range(N_Y):
            to = (y + (d if core == 0 else -d)) % N_Y
            pairs += [((y * 2 + k) * 2 + core, (to * 2 + k) * 2 + core) for k in range(2)]
    return lax.ppermute(a, ("ctx", "rep"), pairs)


def swap_l(a):
    return lax.ppermute(a, "ctx", [(i, i ^ 1) for i in range(2 * N_Y)])


def swap_core(a):
    return lax.ppermute(a, "rep", [(0, 1), (1, 0)])


def pick_head(where_am, keys, values):
    rows = keys.shape[0]

    def kernel(where_ref, key_ref, value_ref, out_ref):
        out_ref[0:rows, :] = key_ref[...]
        out_ref[rows:, :] = value_ref[...]

    column = pl.BlockSpec((rows, HEAD_DIM), lambda i, w: (0, w[0]))
    return pl.pallas_call(
        kernel,
        grid_spec=pltpu.PrefetchScalarGridSpec(
            num_scalar_prefetch=1,
            grid=(1,),
            in_specs=[column, column],
            out_specs=pl.BlockSpec((2 * rows, HEAD_DIM), lambda i, w: (0, 0)),
        ),
        out_shape=jax.ShapeDtypeStruct((2 * rows, HEAD_DIM), BF16),
        compiler_params=params(),
        name="pick_head",
    )(where_am, keys, values)


def pick_weights(place, out_proj):
    rows, cols = out_proj.shape[0] // 2, out_proj.shape[1] // N_X

    def kernel(place_ref, *refs):
        for source, target in zip(refs[:3], refs[3:]):
            target[...] = source[...]

    def block(d):
        return pl.BlockSpec((rows, cols), lambda i, w: (w[0], lax.rem(w[1] + d, N_X)))

    return pl.pallas_call(
        kernel,
        grid_spec=pltpu.PrefetchScalarGridSpec(
            num_scalar_prefetch=1,
            grid=(1,),
            in_specs=[block(d) for d in range(1, N_X)],
            out_specs=[pl.BlockSpec((rows, cols), lambda i, w: (0, 0))] * 3,
        ),
        out_shape=[jax.ShapeDtypeStruct((rows, cols), BF16)] * 3,
        compiler_params=params(),
        name="pick_weights",
    )(place, out_proj, out_proj, out_proj)


def attend(queries, blocks, spot, steps, state, riders=None):
    rows, heads = queries.shape[0], queries.shape[1] // HEAD_DIM
    calls = len(blocks)
    n = sum(b.shape[0] for b in blocks) // (2 * rows)
    first = state is None
    last = riders is not None
    passengers = [r for group in riders for r in group] if last else []
    tile = 128

    def kernel(*refs):
        spot_ref, q_ref = refs[0], refs[1]
        bias = []
        for dy, flip in steps:
            side = 1 - spot_ref[1] if flip else spot_ref[1]
            owner = lax.rem(spot_ref[0] + N_Y + dy, N_Y) * 2 + side
            bias.append(jnp.where(owner <= spot_ref[2], 0.0, LOWEST).astype(F32))
        kv_refs = [
            r.at[first_row : first_row + 2 * rows]
            for r in refs[2 : 2 + calls]
            for first_row in range(0, r.shape[0], 2 * rows)
        ]
        rest, (key_ref, value_ref) = refs[2 + calls : -2], refs[-2:]
        if not first:
            acc_in, top_in = rest[0], rest[1]
            rest = rest[2:]
        if last:
            rider_refs, rest = list(rest[: len(passengers)]), rest[len(passengers) :]
            for group, target in zip(riders, rest):
                for at in range(rows, rows + RIDER * len(group), RIDER):
                    target[at : at + RIDER, :] = rider_refs.pop(0)[...]
        for b, r in enumerate(kv_refs):
            at = slice(b * rows, (b + 1) * rows)
            key_ref[at, :] = r[0:rows, :]
            value_ref[at, 0:HEAD_DIM] = r[rows:, :]
        value_ref[:, HEAD_DIM:] = jnp.ones((n * rows, HEAD_DIM), BF16)

        def head(h, carry):
            lanes = pl.ds(pl.multiple_of(h * HEAD_DIM, HEAD_DIM), HEAD_DIM)

            def score(part):
                return lax.dot_general(
                    q_ref[pl.ds(part * tile, tile), lanes],
                    key_ref[...],
                    (((1,), (1,)), ((), ())),
                    preferred_element_type=F32,
                )

            upcoming = score(0)
            for part in range(rows // tile):
                at = pl.ds(part * tile, tile)
                scores = upcoming
                if (part + 1) * tile < rows:
                    upcoming = score(part + 1)
                if first:
                    i = lax.broadcasted_iota(jnp.int32, (tile, rows), 0) + part * tile
                    j = lax.broadcasted_iota(jnp.int32, (tile, rows), 1)
                    diagonal = jnp.where(j <= i, scores[:, :rows], LOWEST)
                    scores = jnp.concatenate([diagonal, scores[:, rows:]], axis=1)
                    newest = jnp.full((tile, HEAD_DIM), LOWEST, F32)
                else:
                    before = top_in[h, at, :]
                    newest = before
                for b in range(n):
                    highest = jnp.max(scores[:, b * rows : (b + 1) * rows], axis=1, keepdims=True)
                    newest = jnp.maximum(newest, highest + bias[b])
                offsets = [(newest - bias[b]) * EXP2_SCALE for b in range(n)]
                pieces = []
                for lane in range(0, n * rows, HEAD_DIM):
                    pieces.append(
                        jnp.exp2(
                            scores[:, lane : lane + HEAD_DIM] * EXP2_SCALE - offsets[lane // rows]
                        ).astype(BF16)
                    )
                total = jnp.dot(
                    jnp.concatenate(pieces, axis=1), value_ref[...], preferred_element_type=F32
                )
                if not first:
                    factor = jnp.exp2((before - newest) * EXP2_SCALE)
                    total = acc_in[h, at, :] * jnp.concatenate([factor, factor], axis=1) + total
                if last:
                    done = (total[:, :HEAD_DIM] / total[:, HEAD_DIM:]).astype(BF16)
                    for target in rest:
                        target[at, lanes] = done
                else:
                    rest[0][h, at, :] = total
                    rest[1][h, at, :] = newest
            return carry

        lax.fori_loop(0, heads, head, 0)

    state_shapes = [
        jax.ShapeDtypeStruct((heads, rows, 2 * HEAD_DIM), F32),
        jax.ShapeDtypeStruct((heads, rows, HEAD_DIM), F32),
    ]
    return pl.pallas_call(
        kernel,
        in_specs=[pl.BlockSpec(memory_space=SMEM)]
        + [whole()] * (1 + calls + (0 if first else 2) + len(passengers)),
        out_specs=[whole()] * 2,
        out_shape=[
            jax.ShapeDtypeStruct((rows + RIDER * len(group), queries.shape[1]), BF16)
            for group in riders
        ]
        if last
        else state_shapes,
        scratch_shapes=[VMEM((n * rows, HEAD_DIM), BF16), VMEM((n * rows, 2 * HEAD_DIM), BF16)],
        compiler_params=params(16),
        cost_estimate=pl.CostEstimate(
            flops=heads * n * rows * rows * HEAD_DIM * 4,
            transcendentals=heads * n * rows * rows,
            bytes_accessed=4 << 20,
        ),
        name="attend",
    )(spot, queries, *blocks, *(() if first else state), *passengers)


def rows_of(place_ref, left_ref, dz, columns):
    row = lax.rem(place_ref[0] + dz, N_Z) * (N_X * TOKENS)
    return left_ref[pl.ds(pl.multiple_of(row, N_X * TOKENS), N_X * TOKENS), columns]


def project_near(place, own, out_proj, lefts, fetched, other):
    n = len(lefts)
    cols = out_proj.shape[1] // N_X

    def kernel(place_ref, own_ref, weight_ref, *refs):
        left_refs, fetched_refs, other_ref, out_ref = refs[:n], refs[n : 2 * n], refs[2 * n], refs[-1]

        def chunk(dz, carry):
            total = jnp.dot(
                rows_of(place_ref, own_ref, dz, slice(None)),
                weight_ref[...],
                preferred_element_type=F32,
            )
            for k in range(n):
                total = total + fetched_part(
                    place_ref, left_refs[k], fetched_refs[k], other_ref, (0, 2)[k], dz
                )
            out_ref[dz] = total
            return carry

        lax.fori_loop(0, N_Z, chunk, 0)

    fixed = lambda i, w: (0, 0)
    square = pl.BlockSpec(own.shape, fixed)
    return pl.pallas_call(
        kernel,
        grid_spec=pltpu.PrefetchScalarGridSpec(
            num_scalar_prefetch=1,
            grid=(1,),
            in_specs=[square, pl.BlockSpec((out_proj.shape[0], cols), lambda i, w: (0, w[1]))]
            + [pl.BlockSpec(left.shape, fixed) for left in lefts]
            + [pl.BlockSpec(fetched[0].shape, fixed)] * n
            + [pl.BlockSpec(other.shape, fixed)],
            out_specs=pl.BlockSpec((N_Z, N_X * TOKENS, cols), lambda i, w: (0, 0, 0)),
        ),
        out_shape=jax.ShapeDtypeStruct((N_Z, N_X * TOKENS, cols), F32),
        compiler_params=params(28),
        cost_estimate=pl.CostEstimate(flops=1, transcendentals=0, bytes_accessed=1),
        name="project_near",
    )(place, own, out_proj, *lefts, *fetched, other)


def fetched_part(place_ref, left_ref, fetched_ref, other_ref, at, dz):
    half = fetched_ref.shape[0]
    core = place_ref[2]
    mine = pl.ds(pl.multiple_of(core * half, half), half)
    theirs = pl.ds(pl.multiple_of((1 - core) * half, half), half)
    return jnp.dot(
        rows_of(place_ref, left_ref, dz, mine), fetched_ref[...], preferred_element_type=F32
    ) + jnp.dot(
        rows_of(place_ref, left_ref, dz, theirs),
        other_ref[at * half : (at + 1) * half, :],
        preferred_element_type=F32,
    )


def forward(message, first, rows, riders):
    attended = message.shape[0] // 512 * 512

    def kernel(message_ref, out_ref):
        out_ref[0:rows, :] = message_ref[first : first + rows, :]
        if riders:
            out_ref[rows:, :] = message_ref[attended : attended + riders, :]

    return pl.pallas_call(
        kernel,
        in_specs=[whole()],
        out_specs=whole(),
        out_shape=jax.ShapeDtypeStruct((rows + riders, message.shape[1]), BF16),
        compiler_params=params(4),
        name="forward",
    )(message)


def project_far(place, near, lefts, fetched, other):
    shape = near.shape[1:]
    middle = shape[1] // 2

    def kernel(place_ref, upper_ref, lower_ref, fetched_ref, other_ref, *refs):
        near_ref, out_refs, left_ref = refs[0], refs[1:-1], refs[-1]
        half = left_ref.shape[0] // 2
        left_ref[:half, :] = upper_ref[:half, :]
        left_ref[half:, :] = lower_ref[...]
        for dz in (2, 1, 3, 0):
            total = near_ref[dz] + fetched_part(
                place_ref, left_ref, fetched_ref, other_ref, 1, dz
            )
            total = total.astype(BF16)
            if dz == 2:
                out_refs[3][...] = total[:, :middle]
                out_refs[4][...] = total[:, middle:]
            else:
                out_refs[{0: 0, 1: 1, 3: 2}[dz]][...] = total

    return pl.pallas_call(
        kernel,
        in_specs=[pl.BlockSpec(memory_space=SMEM)] + [whole()] * 5,
        out_specs=[whole()] * 5,
        scratch_shapes=[VMEM((2 * lefts[1].shape[0], lefts[1].shape[1]), BF16)],
        out_shape=[jax.ShapeDtypeStruct(shape, BF16)] * 3
        + [jax.ShapeDtypeStruct((shape[0], middle), BF16)] * 2,
        compiler_params=params(),
        name="project_far",
    )(place, *lefts, fetched, other, near)


def pick_hidden(place, live, hidden_in, ids):
    cols = D // N_X // 2

    def kernel(place_ref, live_ref, hidden_ref, id_ref, *out_refs):
        x = place_ref[1]
        t = lax.broadcasted_iota(jnp.int32, (TOPK, TOKENS), 1)
        alive = jnp.where(t < live_ref[0], id_ref[...] + 1, 0).astype(F32)
        lanes = (
            lax.broadcasted_iota(jnp.int32, (TOKENS, cols), 1)
            == lax.broadcasted_iota(jnp.int32, (TOKENS, cols), 0) + x * TOKENS
        ).astype(F32)
        alive = jnp.dot(alive, lanes, preferred_element_type=F32)
        for d in range(N_X):
            for side in range(2):
                column = pl.multiple_of(lax.rem(x + d, N_X) * (2 * cols) + side * cols, cols)
                top = side * (TOKENS + TOPK)
                out_refs[d][top : top + TOKENS, :] = hidden_ref[:, pl.ds(column, cols)]
                out_refs[d][top + TOKENS : top + TOKENS + TOPK, :] = (
                    alive if side == 0 else jnp.zeros_like(alive)
                ).astype(BF16)

    return pl.pallas_call(
        kernel,
        in_specs=[pl.BlockSpec(memory_space=SMEM)] * 2 + [whole()] * 2,
        out_specs=[whole()] * N_X,
        out_shape=[jax.ShapeDtypeStruct((RIDER, cols), BF16)] * N_X,
        compiler_params=params(),
        name="pick_hidden",
    )(place, live, hidden_in, ids)


def route(place, hidden):
    slots = N_Z * N_X * N_X * CAP
    tokens = N_X * TOKENS

    def kernel(place_ref, *refs):
        z = place_ref[0]
        s = lax.broadcasted_iota(jnp.int32, (slots, tokens), 0)
        t = lax.broadcasted_iota(jnp.int32, (slots, tokens), 1)
        dz, expert_x, owner, cap = s // 32, (s // 8) % 4, (s // 2) % 4, s % 2
        expert = ((z + dz) % N_Z) * N_X + expert_x
        wanted = jnp.where(owner == t // TOKENS, expert + 1, -1).astype(F32)
        ids = sum(
            r[r.shape[0] - RIDER + TOKENS : r.shape[0] - RIDER + TOKENS + TOPK, 0:tokens].astype(F32)
            for r in refs[:4]
        )
        present = jnp.zeros((slots, tokens), F32)
        for k in range(TOPK):
            present = present + (ids[k : k + 1, :] == wanted).astype(F32)
        earlier = (
            lax.broadcasted_iota(jnp.int32, (tokens, tokens), 0)
            < lax.broadcasted_iota(jnp.int32, (tokens, tokens), 1)
        ).astype(F32)
        rank = jnp.dot(present, earlier, preferred_element_type=F32)
        fits = jnp.abs(rank - cap.astype(F32)) < 0.5
        refs[4][...] = jnp.where(fits, present, 0.0).astype(BF16)

    return pl.pallas_call(
        kernel,
        in_specs=[pl.BlockSpec(memory_space=SMEM)] + [whole()] * 4,
        out_specs=whole(),
        out_shape=jax.ShapeDtypeStruct((slots, tokens), BF16),
        compiler_params=params(),
        name="route",
    )(place, *hidden)


def route_weights(place, ids, gates, live):
    slots = N_X * N_Z * CAP

    def kernel(place_ref, live_ref, id_ref, gate_ref, weight_ref):
        z = place_ref[0]
        s = lax.broadcasted_iota(jnp.int32, (slots, TOKENS), 0)
        t = lax.broadcasted_iota(jnp.int32, (slots, TOKENS), 1)
        expert_x, dz, cap = s // (N_Z * CAP), (s // CAP) % N_Z, s % CAP
        expert = ((z + dz) % N_Z) * N_X + expert_x
        present = jnp.zeros((slots, TOKENS), F32)
        weight = jnp.zeros((slots, TOKENS), F32)
        for k in range(TOPK):
            hit = ((id_ref[k : k + 1, :] == expert) & (t < live_ref[0])).astype(F32)
            present = present + hit
            weight = weight + hit * gate_ref[k : k + 1, :].astype(F32)
        earlier = (
            lax.broadcasted_iota(jnp.int32, (TOKENS, TOKENS), 0)
            < lax.broadcasted_iota(jnp.int32, (TOKENS, TOKENS), 1)
        ).astype(F32)
        rank = jnp.dot(present, earlier, preferred_element_type=F32)
        weight_ref[...] = jnp.where(jnp.abs(rank - cap.astype(F32)) < 0.5, weight, 0.0) / 4096.0

    return pl.pallas_call(
        kernel,
        in_specs=[pl.BlockSpec(memory_space=SMEM)] * 2 + [whole()] * 2,
        out_specs=whole(),
        out_shape=jax.ShapeDtypeStruct((slots, TOKENS), F32),
        compiler_params=params(),
        name="route_weights",
    )(place, live, ids, gates)


def finish_rows(place, hidden, sums, pick):
    cols = sums[0].shape[1]

    def kernel(place_ref, h0, h1, h2, h3, s0, s1, s2, pick_ref, *refs):
        mixed_ref, send_refs = refs[0], refs[1:5]
        for d, h in enumerate((h0, h1, h2, h3)):
            row = lax.rem(place_ref[1] + N_X - d, N_X) * TOKENS
            at = pl.ds(pl.multiple_of(row, TOKENS), TOKENS)
            top = h.shape[0] - RIDER
            rows = jnp.concatenate(
                [h[top : top + TOKENS, :], h[top + TOKENS + TOPK : top + 2 * TOKENS + TOPK, :]], axis=1
            )
            mixed_ref[at, :] = (
                rows.astype(F32)
                + (s0[at, :].astype(F32) + s1[at, :].astype(F32) + s2[at, :].astype(F32))
            ).astype(BF16)
        send = jnp.dot(pick_ref[...], mixed_ref[...], preferred_element_type=F32).astype(BF16)
        for dz in range(N_Z):
            send_refs[dz][...] = send[dz * 32 : dz * 32 + 32, :]

    return pl.pallas_call(
        kernel,
        in_specs=[pl.BlockSpec(memory_space=SMEM)] + [whole()] * 8,
        out_specs=[whole()] * 5,
        out_shape=[jax.ShapeDtypeStruct((N_X * TOKENS, cols), BF16)]
        + [jax.ShapeDtypeStruct((32, cols), BF16)] * 4,
        compiler_params=params(),
        name="finish_rows",
    )(place, *hidden, *sums, pick)


def by_columns(groups, mixed):
    cols = mixed.shape[1]

    def kernel(*refs):
        held = [r[...] for r in refs[:4]]
        for x in range(N_X):
            refs[5][x, 0:32, :] = jnp.concatenate([h[x * 8 : x * 8 + 8, :] for h in held], axis=0)
            refs[5][x, 32:64, :] = refs[4][x * TOKENS : (x + 1) * TOKENS, :]

    return pl.pallas_call(
        kernel,
        in_specs=[whole()] * 5,
        out_specs=whole(),
        out_shape=jax.ShapeDtypeStruct((N_X, 64, cols), BF16),
        compiler_params=params(),
        name="by_columns",
    )(*groups, mixed)


def join_columns(pieces, gain):
    cols = pieces.shape[2]

    def kernel(piece_ref, gain_ref, block_ref, mixed_ref):
        values = [piece_ref[x, 0:32, :].astype(F32) for x in range(N_X)]
        square = sum(jnp.sum(v * v, axis=1, keepdims=True) for v in values)
        scale = lax.rsqrt(square / D + 1e-06)
        for x, value in enumerate(values):
            column = slice(x * cols, (x + 1) * cols)
            block_ref[:, column] = (value * scale * gain_ref[:, column]).astype(BF16)
            mixed_ref[:, column] = piece_ref[x, 32:64, :]

    return pl.pallas_call(
        kernel,
        in_specs=[whole()] * 2,
        out_specs=[whole()] * 2,
        out_shape=[jax.ShapeDtypeStruct((32, D), BF16)] * 2,
        compiler_params=params(),
        name="join_columns",
    )(pieces, gain)


def regroup(groups):
    rows = 4 * 4 * CAP

    def kernel(*refs):
        held = jnp.concatenate([r[...] for r in refs[:4]], axis=0)
        to = lax.broadcasted_iota(jnp.int32, (rows, rows), 0)
        come = lax.broadcasted_iota(jnp.int32, (rows, rows), 1)
        b, a, cap = to // 8, (to // CAP) % 4, to % CAP
        order = (come == a * 8 + b * CAP + cap).astype(BF16)
        moved = jnp.dot(order, held, preferred_element_type=F32).astype(BF16)
        for i in range(4):
            refs[4][i] = moved[i * 8 : i * 8 + 8, :]

    return pl.pallas_call(
        kernel,
        in_specs=[whole()] * 4,
        out_specs=whole(),
        out_shape=jax.ShapeDtypeStruct((4, 8, D), BF16),
        compiler_params=params(),
        name="regroup",
    )(*groups)


def run_expert(blocks, gate, up, down):
    n = len(blocks)

    def kernel(*refs):
        in_refs, (gate_ref, up_ref, down_ref), out_refs = refs[:n], refs[n : n + 3], refs[n + 3 :]
        rows = jnp.concatenate([r[...] for r in in_refs], axis=0)
        last = (((1,), (1,)), ((), ()))
        gate_part = lax.dot_general(rows, gate_ref[...], last, preferred_element_type=F32)
        up_part = lax.dot_general(rows, up_ref[...], last, preferred_element_type=F32)
        hidden = (gate_part / (1.0 + jnp.exp(-gate_part)) * up_part).astype(BF16)
        result = jnp.dot(hidden, down_ref[...], preferred_element_type=F32).astype(BF16)
        at = 0
        for r in out_refs:
            r[...] = result[at : at + r.shape[0], :]
            at += r.shape[0]

    return pl.pallas_call(
        kernel,
        in_specs=[whole()] * (n + 3),
        out_specs=[whole()] * n,
        out_shape=[jax.ShapeDtypeStruct(b.shape, BF16) for b in blocks],
        compiler_params=params(24),
        name="run_expert",
    )(*blocks, gate, up, down)


def combine(weight, groups):
    def kernel(weight_ref, *refs):
        held = jnp.concatenate([refs[0][i] for i in range(4)], axis=0).astype(F32)
        refs[1][...] = lax.dot_general(
            weight_ref[...],
            held,
            (((0,), (0,)), ((), ())),
            precision=lax.Precision.HIGHEST,
            preferred_element_type=F32,
        ).astype(BF16)

    return pl.pallas_call(
        kernel,
        in_specs=[whole()] * 2,
        out_specs=whole(),
        out_shape=jax.ShapeDtypeStruct((TOKENS, D), BF16),
        compiler_params=params(),
        name="combine",
    )(weight, groups)


def stack(arrays):
    rows = sum(a.shape[0] for a in arrays)

    def kernel(*refs):
        at = 0
        for r in refs[:-1]:
            refs[-1][at : at + r.shape[0], :] = r[...]
            at += r.shape[0]

    return pl.pallas_call(
        kernel,
        in_specs=[whole()] * len(arrays),
        out_specs=whole(),
        out_shape=jax.ShapeDtypeStruct((rows, arrays[0].shape[1]), BF16),
        compiler_params=params(4),
        name="stack",
    )(*arrays)


def tie(values, *others):
    n = len(values)
    return lax.optimization_barrier((*values, *others))[:n]


def add(*arrays):
    return sum(a.astype(F32) for a in arrays).astype(BF16)


def exchange_x(a):
    groups = [[z * N_X + x for x in range(N_X)] for z in range(N_Z)]
    return lax.all_to_all(a, "exp", 0, 0, tiled=True, axis_index_groups=groups)


def scatter_ctx(parts):
    own, swapped, below, above, below_swapped, below_two, above_swapped, far = parts
    got_far = swap_l(far)
    got_below_swapped = swap_l(below_swapped)
    got_above_swapped = turn_y(above_swapped, 1)
    got_two = turn_y(add(below_two, got_far), -1)
    got_above = turn_y(above, 1)
    got_swapped = swap_l(add(swapped, got_above_swapped))
    got_below = turn_y(add(below, got_two, got_below_swapped), -1)
    return add(own, got_above, got_below, got_swapped)


def on_device(
    hidden_in,
    queries,
    keys,
    values,
    out_proj,
    norm_gain,
    expert_ids,
    gate_fixed,
    live_counts,
    gate_proj,
    up_proj,
    down_proj,
):
    exp_index = lax.axis_index("exp")
    ctx_index = lax.axis_index("ctx")
    rep_index = lax.axis_index("rep")
    z, x = exp_index // N_X, exp_index % N_X
    y, side = ctx_index // 2, ctx_index % 2
    place = jnp.stack([z, x, rep_index]).astype(jnp.int32)
    seq_rows = queries.shape[0]
    local_heads = queries.shape[1] // HEAD_DIM
    kv_index = exp_index * local_heads // (HEADS // KV_HEADS)

    spot = jnp.stack([y, side, ctx_index]).astype(jnp.int32)

    keys, values, out_proj = [
        pltpu.with_memory_space_constraint(a, pltpu.HBM) for a in (keys, values, out_proj)
    ]
    own = pick_head(kv_index.astype(jnp.int32)[None], keys, values)
    swapped = swap_l(own)
    away = pick_weights(jnp.stack([rep_index, x]).astype(jnp.int32), out_proj)
    fetched = [shift_x(away[d - 1], d) for d in range(1, N_X)]
    (swapped,) = tie((swapped,), *away)
    pair = stack([own, swapped])
    below = shift_y(pair, 1)
    above = shift_y(pair, -1)
    state = attend(queries, [pair], spot, [(0, 0), (0, 1)], None)
    riders = pick_hidden(place, live_counts, hidden_in, expert_ids.T)
    below, above = tie((below, above), *state, *riders)
    block = own.shape[0]
    far_a = shift_y(below[:block], 1)
    far_b = shift_y(above[block:], -1)
    state = attend(
        queries, [below, above], spot, [(-1, 0), (-1, 1), (1, 0), (1, 1)], state
    )
    far_a, far_b, *fetched = tie((far_a, far_b, *fetched), *state)
    messages = attend(
        queries, [far_a, far_b], spot, [(-2, 0), (-2, 1)], state, [[riders[2], riders[1]], [riders[3]]]
    )

    from_left = shift_x(messages[0], 1)
    from_right = shift_x(messages[1], 3)
    half = seq_rows // 2
    far_a = shift_x(forward(from_left, 0, half, RIDER), 1)
    far_b = shift_x(forward(from_right, half, half, 0), 3)
    weight = route_weights(
        tie((place,), from_left)[0], live=live_counts, ids=expert_ids.T, gates=gate_fixed.T
    )
    other = swap_core(stack(fetched))
    near = project_near(
        place, messages[0], out_proj, [from_left, from_right], [fetched[0], fetched[2]], other
    )
    far_a, far_b, near = tie((far_a, far_b, near))
    hidden = [riders[0], from_left, far_a, from_right]
    mine, up_chunk, down_chunk, low, high = project_far(
        place, near, [far_a, far_b], fetched[1], other
    )

    middle = low.shape[1]
    got_low = shift_z(low, 1)
    got_high = shift_z(high, -1)
    pick = route(place, hidden)
    got_low, got_high = tie((got_low, got_high), pick)
    up_chunk = jnp.concatenate([add(up_chunk[:, :middle], got_low), up_chunk[:, middle:]], axis=1)
    down_chunk = jnp.concatenate(
        [down_chunk[:, :middle], add(down_chunk[:, middle:], got_high)], axis=1
    )
    got_up = shift_z(up_chunk, 1)
    got_down = shift_z(down_chunk, -1)
    mixed, *send = finish_rows(place, hidden, [mine, got_up, got_down], pick)

    by_z = [send[0]] + [shift_z(send[d], d) for d in range(1, N_Z)]
    block, mixed = join_columns(exchange_x(by_columns(by_z, mixed)), norm_gain.reshape(1, D))
    swapped = swap_l(block)
    below = turn_y(block, 1)
    above = turn_y(block, -1)
    below_two = turn_y(below, 1)
    below_swapped = swap_l(below)
    above_swapped = turn_y(swapped, -1)
    far = swap_l(below_two)
    parts = run_expert(
        [block, swapped, below, above, below_swapped, below_two, above_swapped, far],
        gate_proj[0].T,
        up_proj[0].T,
        down_proj[0],
    )

    result = scatter_ctx(parts)
    back_z = [result[:8]] + [shift_z(result[8 * d : 8 * d + 8], -d) for d in range(1, N_Z)]
    return (mixed, combine(weight, exchange_x(regroup(back_z))))


def solution(mesh):
    in_specs = (
        P(("rep", "ctx", "exp"), None),
        P(("rep", "ctx"), "exp"),
        P(("rep", "ctx"), None),
        P(("rep", "ctx"), None),
        P("exp", None),
        P(),
        P(("rep", "ctx", "exp"), None),
        P(("rep", "ctx", "exp"), None),
        P(("rep", "ctx", "exp")),
        P("exp", None, "ctx"),
        P("exp", None, "ctx"),
        P("exp", "ctx", None),
    )
    out_specs = (P(("rep", "ctx", "exp"), None), P(("rep", "ctx", "exp"), None))
    return jax.shard_map(
        on_device, mesh=mesh, in_specs=in_specs, out_specs=out_specs, check_vma=False
    )
```

```python
import functools
import math

import jax
import jax.numpy as jnp
from jax import lax
from jax.experimental import pallas as pl
from jax.experimental.pallas import tpu as pltpu
from jax.sharding import PartitionSpec as P

D = 4096
HEADS = 64
KV_HEADS = 4
HEAD_DIM = 128
TOPK = 8
CAP = 2
N_X = 4
N_Z = 4
N_Y = 4
TOKENS = 32
RIDER = 2 * (TOKENS + TOPK)
BF16 = jnp.bfloat16
F32 = jnp.float32
LOWEST = -1e30
EXP2_SCALE = HEAD_DIM ** (-0.5) * math.log2(math.e)
VMEM = pltpu.VMEM
SMEM = pltpu.SMEM


def params(limit_mib=8):
    return pltpu.CompilerParams(vmem_limit_bytes=limit_mib << 20)


def whole():
    return pl.BlockSpec(memory_space=VMEM)


def shift_x(a, d):
    pairs = [(z * N_X + x, z * N_X + (x + d) % N_X) for z in range(N_Z) for x in range(N_X)]
    return lax.ppermute(a, "exp", pairs)


def shift_z(a, d):
    pairs = [(z * N_X + x, (z + d) % N_Z * N_X + x) for z in range(N_Z) for x in range(N_X)]
    return lax.ppermute(a, "exp", pairs)


def shift_y(a, d):
    pairs = [(y * 2 + k, (y + d) % N_Y * 2 + k) for y in range(N_Y) for k in range(2)]
    return lax.ppermute(a, "ctx", pairs)


def turn_y(a, d):
    pairs = []
    for core in range(2):
        for y in range(N_Y):
            to = (y + (d if core == 0 else -d)) % N_Y
            pairs += [((y * 2 + k) * 2 + core, (to * 2 + k) * 2 + core) for k in range(2)]
    return lax.ppermute(a, ("ctx", "rep"), pairs)


def swap_l(a):
    return lax.ppermute(a, "ctx", [(i, i ^ 1) for i in range(2 * N_Y)])


def swap_core(a):
    return lax.ppermute(a, "rep", [(0, 1), (1, 0)])


def pick_head(where_am, keys, values):
    rows = keys.shape[0]

    def kernel(where_ref, key_ref, value_ref, out_ref):
        out_ref[0:rows, :] = key_ref[...]
        out_ref[rows:, :] = value_ref[...]

    column = pl.BlockSpec((rows, HEAD_DIM), lambda i, w: (0, w[0]))
    return pl.pallas_call(
        kernel,
        grid_spec=pltpu.PrefetchScalarGridSpec(
            num_scalar_prefetch=1,
            grid=(1,),
            in_specs=[column, column],
            out_specs=pl.BlockSpec((2 * rows, HEAD_DIM), lambda i, w: (0, 0)),
        ),
        out_shape=jax.ShapeDtypeStruct((2 * rows, HEAD_DIM), BF16),
        compiler_params=params(),
        name="pick_head",
    )(where_am, keys, values)


def pick_weights(place, out_proj):
    rows, cols = out_proj.shape[0] // 2, out_proj.shape[1] // N_X

    def kernel(place_ref, *refs):
        for source, target in zip(refs[:3], refs[3:]):
            target[...] = source[...]

    def block(d):
        return pl.BlockSpec((rows, cols), lambda i, w: (w[0], lax.rem(w[1] + d, N_X)))

    return pl.pallas_call(
        kernel,
        grid_spec=pltpu.PrefetchScalarGridSpec(
            num_scalar_prefetch=1,
            grid=(1,),
            in_specs=[block(d) for d in range(1, N_X)],
            out_specs=[pl.BlockSpec((rows, cols), lambda i, w: (0, 0))] * 3,
        ),
        out_shape=[jax.ShapeDtypeStruct((rows, cols), BF16)] * 3,
        compiler_params=params(),
        name="pick_weights",
    )(place, out_proj, out_proj, out_proj)


def attend(queries, blocks, spot, steps, state, riders=None):
    rows, heads = queries.shape[0], queries.shape[1] // HEAD_DIM
    calls = len(blocks)
    n = sum(b.shape[0] for b in blocks) // (2 * rows)
    first = state is None
    last = riders is not None
    passengers = [r for group in riders for r in group] if last else []
    tile = 128

    def kernel(*refs):
        spot_ref, q_ref = refs[0], refs[1]
        bias = []
        for dy, flip in steps:
            side = 1 - spot_ref[1] if flip else spot_ref[1]
            owner = lax.rem(spot_ref[0] + N_Y + dy, N_Y) * 2 + side
            bias.append(jnp.where(owner <= spot_ref[2], 0.0, LOWEST).astype(F32))
        kv_refs = [
            r.at[first_row : first_row + 2 * rows]
            for r in refs[2 : 2 + calls]
            for first_row in range(0, r.shape[0], 2 * rows)
        ]
        rest, (key_ref, value_ref) = refs[2 + calls : -2], refs[-2:]
        if not first:
            acc_in, top_in = rest[0], rest[1]
            rest = rest[2:]
        if last:
            rider_refs, rest = list(rest[: len(passengers)]), rest[len(passengers) :]
            for group, target in zip(riders, rest):
                for at in range(rows, rows + RIDER * len(group), RIDER):
                    target[at : at + RIDER, :] = rider_refs.pop(0)[...]
        for b, r in enumerate(kv_refs):
            at = slice(b * rows, (b + 1) * rows)
            key_ref[at, :] = r[0:rows, :]
            value_ref[at, 0:HEAD_DIM] = r[rows:, :]
        value_ref[:, HEAD_DIM:] = jnp.ones((n * rows, HEAD_DIM), BF16)

        def head(h, carry):
            lanes = pl.ds(pl.multiple_of(h * HEAD_DIM, HEAD_DIM), HEAD_DIM)

            def score(part):
                return lax.dot_general(
                    q_ref[pl.ds(part * tile, tile), lanes],
                    key_ref[...],
                    (((1,), (1,)), ((), ())),
                    preferred_element_type=F32,
                )

            upcoming = score(0)
            for part in range(rows // tile):
                at = pl.ds(part * tile, tile)
                scores = upcoming
                if (part + 1) * tile < rows:
                    upcoming = score(part + 1)
                if first:
                    i = lax.broadcasted_iota(jnp.int32, (tile, rows), 0) + part * tile
                    j = lax.broadcasted_iota(jnp.int32, (tile, rows), 1)
                    diagonal = jnp.where(j <= i, scores[:, :rows], LOWEST)
                    scores = jnp.concatenate([diagonal, scores[:, rows:]], axis=1)
                    newest = jnp.full((tile, HEAD_DIM), LOWEST, F32)
                else:
                    before = top_in[h, at, :]
                    newest = before
                for b in range(n):
                    highest = jnp.max(scores[:, b * rows : (b + 1) * rows], axis=1, keepdims=True)
                    newest = jnp.maximum(newest, highest + bias[b])
                offsets = [(newest - bias[b]) * EXP2_SCALE for b in range(n)]
                pieces = []
                for lane in range(0, n * rows, HEAD_DIM):
                    pieces.append(
                        jnp.exp2(
                            scores[:, lane : lane + HEAD_DIM] * EXP2_SCALE - offsets[lane // rows]
                        ).astype(BF16)
                    )
                total = jnp.dot(
                    jnp.concatenate(pieces, axis=1), value_ref[...], preferred_element_type=F32
                )
                if not first:
                    factor = jnp.exp2((before - newest) * EXP2_SCALE)
                    total = acc_in[h, at, :] * jnp.concatenate([factor, factor], axis=1) + total
                if last:
                    done = (total[:, :HEAD_DIM] / total[:, HEAD_DIM:]).astype(BF16)
                    for target in rest:
                        target[at, lanes] = done
                else:
                    rest[0][h, at, :] = total
                    rest[1][h, at, :] = newest
            return carry

        lax.fori_loop(0, heads, head, 0)

    state_shapes = [
        jax.ShapeDtypeStruct((heads, rows, 2 * HEAD_DIM), F32),
        jax.ShapeDtypeStruct((heads, rows, HEAD_DIM), F32),
    ]
    return pl.pallas_call(
        kernel,
        in_specs=[pl.BlockSpec(memory_space=SMEM)]
        + [whole()] * (1 + calls + (0 if first else 2) + len(passengers)),
        out_specs=[whole()] * 2,
        out_shape=[
            jax.ShapeDtypeStruct((rows + RIDER * len(group), queries.shape[1]), BF16)
            for group in riders
        ]
        if last
        else state_shapes,
        scratch_shapes=[VMEM((n * rows, HEAD_DIM), BF16), VMEM((n * rows, 2 * HEAD_DIM), BF16)],
        compiler_params=params(16),
        cost_estimate=pl.CostEstimate(
            flops=heads * n * rows * rows * HEAD_DIM * 4,
            transcendentals=heads * n * rows * rows,
            bytes_accessed=4 << 20,
        ),
        name="attend",
    )(spot, queries, *blocks, *(() if first else state), *passengers)


def rows_of(place_ref, left_ref, dz, columns):
    row = lax.rem(place_ref[0] + dz, N_Z) * (N_X * TOKENS)
    return left_ref[pl.ds(pl.multiple_of(row, N_X * TOKENS), N_X * TOKENS), columns]


def project_near(place, own, out_proj, lefts, fetched, other):
    n = len(lefts)
    cols = out_proj.shape[1] // N_X

    def kernel(place_ref, own_ref, weight_ref, *refs):
        left_refs, fetched_refs, other_ref, out_ref = refs[:n], refs[n : 2 * n], refs[2 * n], refs[-1]

        def chunk(dz, carry):
            total = jnp.dot(
                rows_of(place_ref, own_ref, dz, slice(None)),
                weight_ref[...],
                preferred_element_type=F32,
            )
            for k in range(n):
                total = total + fetched_part(
                    place_ref, left_refs[k], fetched_refs[k], other_ref, (0, 2)[k], dz
                )
            out_ref[dz] = total
            return carry

        lax.fori_loop(0, N_Z, chunk, 0)

    fixed = lambda i, w: (0, 0)
    square = pl.BlockSpec(own.shape, fixed)
    return pl.pallas_call(
        kernel,
        grid_spec=pltpu.PrefetchScalarGridSpec(
            num_scalar_prefetch=1,
            grid=(1,),
            in_specs=[square, pl.BlockSpec((out_proj.shape[0], cols), lambda i, w: (0, w[1]))]
            + [pl.BlockSpec(left.shape, fixed) for left in lefts]
            + [pl.BlockSpec(fetched[0].shape, fixed)] * n
            + [pl.BlockSpec(other.shape, fixed)],
            out_specs=pl.BlockSpec((N_Z, N_X * TOKENS, cols), lambda i, w: (0, 0, 0)),
        ),
        out_shape=jax.ShapeDtypeStruct((N_Z, N_X * TOKENS, cols), F32),
        compiler_params=params(28),
        cost_estimate=pl.CostEstimate(flops=1, transcendentals=0, bytes_accessed=1),
        name="project_near",
    )(place, own, out_proj, *lefts, *fetched, other)


def fetched_part(place_ref, left_ref, fetched_ref, other_ref, at, dz):
    half = fetched_ref.shape[0]
    core = place_ref[2]
    mine = pl.ds(pl.multiple_of(core * half, half), half)
    theirs = pl.ds(pl.multiple_of((1 - core) * half, half), half)
    return jnp.dot(
        rows_of(place_ref, left_ref, dz, mine), fetched_ref[...], preferred_element_type=F32
    ) + jnp.dot(
        rows_of(place_ref, left_ref, dz, theirs),
        other_ref[at * half : (at + 1) * half, :],
        preferred_element_type=F32,
    )


def forward(message, first, rows, riders):
    attended = message.shape[0] // 512 * 512

    def kernel(message_ref, out_ref):
        out_ref[0:rows, :] = message_ref[first : first + rows, :]
        if riders:
            out_ref[rows:, :] = message_ref[attended : attended + riders, :]

    return pl.pallas_call(
        kernel,
        in_specs=[whole()],
        out_specs=whole(),
        out_shape=jax.ShapeDtypeStruct((rows + riders, message.shape[1]), BF16),
        compiler_params=params(4),
        name="forward",
    )(message)


def project_far(place, near, lefts, fetched, other):
    shape = near.shape[1:]
    middle = shape[1] // 2

    def kernel(place_ref, upper_ref, lower_ref, fetched_ref, other_ref, *refs):
        near_ref, out_refs, left_ref = refs[0], refs[1:-1], refs[-1]
        half = left_ref.shape[0] // 2
        left_ref[:half, :] = upper_ref[:half, :]
        left_ref[half:, :] = lower_ref[...]
        for dz in (2, 1, 3, 0):
            total = near_ref[dz] + fetched_part(
                place_ref, left_ref, fetched_ref, other_ref, 1, dz
            )
            total = total.astype(BF16)
            if dz == 2:
                out_refs[3][...] = total[:, :middle]
                out_refs[4][...] = total[:, middle:]
            else:
                out_refs[{0: 0, 1: 1, 3: 2}[dz]][...] = total

    return pl.pallas_call(
        kernel,
        in_specs=[pl.BlockSpec(memory_space=SMEM)] + [whole()] * 5,
        out_specs=[whole()] * 5,
        scratch_shapes=[VMEM((2 * lefts[1].shape[0], lefts[1].shape[1]), BF16)],
        out_shape=[jax.ShapeDtypeStruct(shape, BF16)] * 3
        + [jax.ShapeDtypeStruct((shape[0], middle), BF16)] * 2,
        compiler_params=params(),
        name="project_far",
    )(place, *lefts, fetched, other, near)


def pick_hidden(place, live, hidden_in, ids):
    cols = D // N_X // 2

    def kernel(place_ref, live_ref, hidden_ref, id_ref, *out_refs):
        x = place_ref[1]
        t = lax.broadcasted_iota(jnp.int32, (TOPK, TOKENS), 1)
        alive = jnp.where(t < live_ref[0], id_ref[...] + 1, 0).astype(F32)
        lanes = (
            lax.broadcasted_iota(jnp.int32, (TOKENS, cols), 1)
            == lax.broadcasted_iota(jnp.int32, (TOKENS, cols), 0) + x * TOKENS
        ).astype(F32)
        alive = jnp.dot(alive, lanes, preferred_element_type=F32)
        for d in range(N_X):
            for side in range(2):
                column = pl.multiple_of(lax.rem(x + d, N_X) * (2 * cols) + side * cols, cols)
                top = side * (TOKENS + TOPK)
                out_refs[d][top : top + TOKENS, :] = hidden_ref[:, pl.ds(column, cols)]
                out_refs[d][top + TOKENS : top + TOKENS + TOPK, :] = (
                    alive if side == 0 else jnp.zeros_like(alive)
                ).astype(BF16)

    return pl.pallas_call(
        kernel,
        in_specs=[pl.BlockSpec(memory_space=SMEM)] * 2 + [whole()] * 2,
        out_specs=[whole()] * N_X,
        out_shape=[jax.ShapeDtypeStruct((RIDER, cols), BF16)] * N_X,
        compiler_params=params(),
        name="pick_hidden",
    )(place, live, hidden_in, ids)


def route(place, hidden):
    slots = N_Z * N_X * N_X * CAP
    tokens = N_X * TOKENS

    def kernel(place_ref, *refs):
        z = place_ref[0]
        s = lax.broadcasted_iota(jnp.int32, (slots, tokens), 0)
        t = lax.broadcasted_iota(jnp.int32, (slots, tokens), 1)
        dz, expert_x, owner, cap = s // 32, (s // 8) % 4, (s // 2) % 4, s % 2
        expert = ((z + dz) % N_Z) * N_X + expert_x
        wanted = jnp.where(owner == t // TOKENS, expert + 1, -1).astype(F32)
        ids = sum(
            r[r.shape[0] - RIDER + TOKENS : r.shape[0] - RIDER + TOKENS + TOPK, 0:tokens].astype(F32)
            for r in refs[:4]
        )
        present = jnp.zeros((slots, tokens), F32)
        for k in range(TOPK):
            present = present + (ids[k : k + 1, :] == wanted).astype(F32)
        earlier = (
            lax.broadcasted_iota(jnp.int32, (tokens, tokens), 0)
            < lax.broadcasted_iota(jnp.int32, (tokens, tokens), 1)
        ).astype(F32)
        rank = jnp.dot(present, earlier, preferred_element_type=F32)
        fits = jnp.abs(rank - cap.astype(F32)) < 0.5
        refs[4][...] = jnp.where(fits, present, 0.0).astype(BF16)

    return pl.pallas_call(
        kernel,
        in_specs=[pl.BlockSpec(memory_space=SMEM)] + [whole()] * 4,
        out_specs=whole(),
        out_shape=jax.ShapeDtypeStruct((slots, tokens), BF16),
        compiler_params=params(),
        name="route",
    )(place, *hidden)


def route_weights(place, ids, gates, live):
    slots = N_X * N_Z * CAP

    def kernel(place_ref, live_ref, id_ref, gate_ref, weight_ref):
        z = place_ref[0]
        s = lax.broadcasted_iota(jnp.int32, (slots, TOKENS), 0)
        t = lax.broadcasted_iota(jnp.int32, (slots, TOKENS), 1)
        expert_x, dz, cap = s // (N_Z * CAP), (s // CAP) % N_Z, s % CAP
        expert = ((z + dz) % N_Z) * N_X + expert_x
        present = jnp.zeros((slots, TOKENS), F32)
        weight = jnp.zeros((slots, TOKENS), F32)
        for k in range(TOPK):
            hit = ((id_ref[k : k + 1, :] == expert) & (t < live_ref[0])).astype(F32)
            present = present + hit
            weight = weight + hit * gate_ref[k : k + 1, :].astype(F32)
        earlier = (
            lax.broadcasted_iota(jnp.int32, (TOKENS, TOKENS), 0)
            < lax.broadcasted_iota(jnp.int32, (TOKENS, TOKENS), 1)
        ).astype(F32)
        rank = jnp.dot(present, earlier, preferred_element_type=F32)
        weight_ref[...] = jnp.where(jnp.abs(rank - cap.astype(F32)) < 0.5, weight, 0.0) / 4096.0

    return pl.pallas_call(
        kernel,
        in_specs=[pl.BlockSpec(memory_space=SMEM)] * 2 + [whole()] * 2,
        out_specs=whole(),
        out_shape=jax.ShapeDtypeStruct((slots, TOKENS), F32),
        compiler_params=params(),
        name="route_weights",
    )(place, live, ids, gates)


def finish_rows(place, hidden, sums, pick):
    cols = sums[0].shape[1]

    def kernel(place_ref, h0, h1, h2, h3, s0, s1, s2, pick_ref, *refs):
        mixed_ref, send_refs = refs[0], refs[1:5]
        for d, h in enumerate((h0, h1, h2, h3)):
            row = lax.rem(place_ref[1] + N_X - d, N_X) * TOKENS
            at = pl.ds(pl.multiple_of(row, TOKENS), TOKENS)
            top = h.shape[0] - RIDER
            rows = jnp.concatenate(
                [h[top : top + TOKENS, :], h[top + TOKENS + TOPK : top + 2 * TOKENS + TOPK, :]], axis=1
            )
            mixed_ref[at, :] = (
                rows.astype(F32)
                + (s0[at, :].astype(F32) + s1[at, :].astype(F32) + s2[at, :].astype(F32))
            ).astype(BF16)
        send = jnp.dot(pick_ref[...], mixed_ref[...], preferred_element_type=F32).astype(BF16)
        for dz in range(N_Z):
            send_refs[dz][...] = send[dz * 32 : dz * 32 + 32, :]

    return pl.pallas_call(
        kernel,
        in_specs=[pl.BlockSpec(memory_space=SMEM)] + [whole()] * 8,
        out_specs=[whole()] * 5,
        out_shape=[jax.ShapeDtypeStruct((N_X * TOKENS, cols), BF16)]
        + [jax.ShapeDtypeStruct((32, cols), BF16)] * 4,
        compiler_params=params(),
        name="finish_rows",
    )(place, *hidden, *sums, pick)


def by_columns(groups, mixed):
    cols = mixed.shape[1]

    def kernel(*refs):
        held = [r[...] for r in refs[:4]]
        for x in range(N_X):
            refs[5][x, 0:32, :] = jnp.concatenate([h[x * 8 : x * 8 + 8, :] for h in held], axis=0)
            refs[5][x, 32:64, :] = refs[4][x * TOKENS : (x + 1) * TOKENS, :]

    return pl.pallas_call(
        kernel,
        in_specs=[whole()] * 5,
        out_specs=whole(),
        out_shape=jax.ShapeDtypeStruct((N_X, 64, cols), BF16),
        compiler_params=params(),
        name="by_columns",
    )(*groups, mixed)


def join_columns(pieces, gain):
    cols = pieces.shape[2]

    def kernel(piece_ref, gain_ref, block_ref, mixed_ref):
        values = [piece_ref[x, 0:32, :].astype(F32) for x in range(N_X)]
        square = sum(jnp.sum(v * v, axis=1, keepdims=True) for v in values)
        scale = lax.rsqrt(square / D + 1e-06)
        for x, value in enumerate(values):
            column = slice(x * cols, (x + 1) * cols)
            block_ref[:, column] = (value * scale * gain_ref[:, column]).astype(BF16)
            mixed_ref[:, column] = piece_ref[x, 32:64, :]

    return pl.pallas_call(
        kernel,
        in_specs=[whole()] * 2,
        out_specs=[whole()] * 2,
        out_shape=[jax.ShapeDtypeStruct((32, D), BF16)] * 2,
        compiler_params=params(),
        name="join_columns",
    )(pieces, gain)


def regroup(groups):
    rows = 4 * 4 * CAP

    def kernel(*refs):
        held = jnp.concatenate([r[...] for r in refs[:4]], axis=0)
        to = lax.broadcasted_iota(jnp.int32, (rows, rows), 0)
        come = lax.broadcasted_iota(jnp.int32, (rows, rows), 1)
        b, a, cap = to // 8, (to // CAP) % 4, to % CAP
        order = (come == a * 8 + b * CAP + cap).astype(BF16)
        moved = jnp.dot(order, held, preferred_element_type=F32).astype(BF16)
        for i in range(4):
            refs[4][i] = moved[i * 8 : i * 8 + 8, :]

    return pl.pallas_call(
        kernel,
        in_specs=[whole()] * 4,
        out_specs=whole(),
        out_shape=jax.ShapeDtypeStruct((4, 8, D), BF16),
        compiler_params=params(),
        name="regroup",
    )(*groups)


def run_expert(blocks, gate, up, down):
    n = len(blocks)

    def kernel(*refs):
        in_refs, (gate_ref, up_ref, down_ref), out_refs = refs[:n], refs[n : n + 3], refs[n + 3 :]
        rows = jnp.concatenate([r[...] for r in in_refs], axis=0)
        last = (((1,), (1,)), ((), ()))
        gate_part = lax.dot_general(rows, gate_ref[...], last, preferred_element_type=F32)
        up_part = lax.dot_general(rows, up_ref[...], last, preferred_element_type=F32)
        hidden = (gate_part / (1.0 + jnp.exp(-gate_part)) * up_part).astype(BF16)
        result = jnp.dot(hidden, down_ref[...], preferred_element_type=F32).astype(BF16)
        at = 0
        for r in out_refs:
            r[...] = result[at : at + r.shape[0], :]
            at += r.shape[0]

    return pl.pallas_call(
        kernel,
        in_specs=[whole()] * (n + 3),
        out_specs=[whole()] * n,
        out_shape=[jax.ShapeDtypeStruct(b.shape, BF16) for b in blocks],
        compiler_params=params(24),
        name="run_expert",
    )(*blocks, gate, up, down)


def combine(weight, groups):
    def kernel(weight_ref, *refs):
        held = jnp.concatenate([refs[0][i] for i in range(4)], axis=0).astype(F32)
        refs[1][...] = lax.dot_general(
            weight_ref[...],
            held,
            (((0,), (0,)), ((), ())),
            precision=lax.Precision.HIGHEST,
            preferred_element_type=F32,
        ).astype(BF16)

    return pl.pallas_call(
        kernel,
        in_specs=[whole()] * 2,
        out_specs=whole(),
        out_shape=jax.ShapeDtypeStruct((TOKENS, D), BF16),
        compiler_params=params(),
        name="combine",
    )(weight, groups)


def stack(arrays):
    rows = sum(a.shape[0] for a in arrays)

    def kernel(*refs):
        at = 0
        for r in refs[:-1]:
            refs[-1][at : at + r.shape[0], :] = r[...]
            at += r.shape[0]

    return pl.pallas_call(
        kernel,
        in_specs=[whole()] * len(arrays),
        out_specs=whole(),
        out_shape=jax.ShapeDtypeStruct((rows, arrays[0].shape[1]), BF16),
        compiler_params=params(4),
        name="stack",
    )(*arrays)


def tie(values, *others):
    n = len(values)
    return lax.optimization_barrier((*values, *others))[:n]


def add(*arrays):
    return sum(a.astype(F32) for a in arrays).astype(BF16)


def exchange_x(a):
    groups = [[z * N_X + x for x in range(N_X)] for z in range(N_Z)]
    return lax.all_to_all(a, "exp", 0, 0, tiled=True, axis_index_groups=groups)


def scatter_ctx(parts):
    own, swapped, below, above, below_swapped, below_two, above_swapped, far = parts
    got_far = swap_l(far)
    got_below_swapped = turn_y(below_swapped, -1)
    got_above_swapped = turn_y(above_swapped, 1)
    got_two = turn_y(add(below_two, got_far), -1)
    got_above = turn_y(above, 1)
    got_swapped = swap_l(add(swapped, got_above_swapped, got_below_swapped))
    got_below = turn_y(add(below, got_two), -1)
    return add(own, got_above, got_below, got_swapped)


def on_device(
    hidden_in,
    queries,
    keys,
    values,
    out_proj,
    norm_gain,
    expert_ids,
    gate_fixed,
    live_counts,
    gate_proj,
    up_proj,
    down_proj,
):
    exp_index = lax.axis_index("exp")
    ctx_index = lax.axis_index("ctx")
    rep_index = lax.axis_index("rep")
    z, x = exp_index // N_X, exp_index % N_X
    y, side = ctx_index // 2, ctx_index % 2
    place = jnp.stack([z, x, rep_index]).astype(jnp.int32)
    seq_rows = queries.shape[0]
    local_heads = queries.shape[1] // HEAD_DIM
    kv_index = exp_index * local_heads // (HEADS // KV_HEADS)

    spot = jnp.stack([y, side, ctx_index]).astype(jnp.int32)

    keys, values, out_proj = [
        pltpu.with_memory_space_constraint(a, pltpu.HBM) for a in (keys, values, out_proj)
    ]
    own = pick_head(kv_index.astype(jnp.int32)[None], keys, values)
    swapped = swap_l(own)
    away = pick_weights(jnp.stack([rep_index, x]).astype(jnp.int32), out_proj)
    fetched = [shift_x(away[d - 1], d) for d in range(1, N_X)]
    (swapped,) = tie((swapped,), *away)
    pair = stack([own, swapped])
    below = shift_y(pair, 1)
    above = shift_y(pair, -1)
    state = attend(queries, [pair], spot, [(0, 0), (0, 1)], None)
    riders = pick_hidden(place, live_counts, hidden_in, expert_ids.T)
    below, above = tie((below, above), *state, *riders)
    block = own.shape[0]
    far_a = shift_y(below[:block], 1)
    far_b = shift_y(above[block:], -1)
    state = attend(
        queries, [below, above], spot, [(-1, 0), (-1, 1), (1, 0), (1, 1)], state
    )
    far_a, far_b, *fetched = tie((far_a, far_b, *fetched), *state)
    messages = attend(
        queries, [far_a, far_b], spot, [(-2, 0), (-2, 1)], state, [[riders[2], riders[1]], [riders[3]]]
    )

    from_left = shift_x(messages[0], 1)
    from_right = shift_x(messages[1], 3)
    half = seq_rows // 2
    far_a = shift_x(forward(from_left, 0, half, RIDER), 1)
    far_b = shift_x(forward(from_right, half, half, 0), 3)
    weight = route_weights(
        tie((place,), from_left)[0], live=live_counts, ids=expert_ids.T, gates=gate_fixed.T
    )
    other = swap_core(stack(fetched))
    near = project_near(
        place, messages[0], out_proj, [from_left, from_right], [fetched[0], fetched[2]], other
    )
    far_a, far_b, near = tie((far_a, far_b, near))
    hidden = [riders[0], from_left, far_a, from_right]
    mine, up_chunk, down_chunk, low, high = project_far(
        place, near, [far_a, far_b], fetched[1], other
    )

    middle = low.shape[1]
    got_low = shift_z(low, 1)
    got_high = shift_z(high, -1)
    pick = route(place, hidden)
    got_low, got_high = tie((got_low, got_high), pick)
    up_chunk = jnp.concatenate([add(up_chunk[:, :middle], got_low), up_chunk[:, middle:]], axis=1)
    down_chunk = jnp.concatenate(
        [down_chunk[:, :middle], add(down_chunk[:, middle:], got_high)], axis=1
    )
    got_up = shift_z(up_chunk, 1)
    got_down = shift_z(down_chunk, -1)
    mixed, *send = finish_rows(place, hidden, [mine, got_up, got_down], pick)

    by_z = [send[0]] + [shift_z(send[d], d) for d in range(1, N_Z)]
    block, mixed = join_columns(exchange_x(by_columns(by_z, mixed)), norm_gain.reshape(1, D))
    swapped = swap_l(block)
    below = turn_y(block, 1)
    above = turn_y(block, -1)
    below_two = turn_y(below, 1)
    below_swapped = turn_y(swapped, 1)
    above_swapped = turn_y(swapped, -1)
    far = swap_l(below_two)
    parts = run_expert(
        [block, swapped, below, above, below_swapped, below_two, above_swapped, far],
        gate_proj[0].T,
        up_proj[0].T,
        down_proj[0],
    )

    result = scatter_ctx(parts)
    back_z = [result[:8]] + [shift_z(result[8 * d : 8 * d + 8], -d) for d in range(1, N_Z)]
    return (mixed, combine(weight, exchange_x(regroup(back_z))))


def solution(mesh):
    in_specs = (
        P(("rep", "ctx", "exp"), None),
        P(("rep", "ctx"), "exp"),
        P(("rep", "ctx"), None),
        P(("rep", "ctx"), None),
        P("exp", None),
        P(),
        P(("rep", "ctx", "exp"), None),
        P(("rep", "ctx", "exp"), None),
        P(("rep", "ctx", "exp")),
        P("exp", None, "ctx"),
        P("exp", None, "ctx"),
        P("exp", "ctx", None),
    )
    out_specs = (P(("rep", "ctx", "exp"), None), P(("rep", "ctx", "exp"), None))
    return jax.shard_map(
        on_device, mesh=mesh, in_specs=in_specs, out_specs=out_specs, check_vma=False
    )
```
